256 devices in a mesh: dp: 8 (over z), space: 8 (over x, core), tensor: 4 (over y).
Axes of the slice: x: 4, y: 4, z: 8, core: 2. Of those that a mesh axis runs over, the one named last changes fastest.
Arguments:
- feat_policy: bfloat16 [8, 2, 320, 32, 128], P('dp', None, 'tensor', 'space'), may hold values from -6 to 6
- feat_ref: bfloat16 [8, 2, 320, 32, 128], P('dp', None, 'tensor', 'space'), may hold values from -6 to 6
- noise: float32 [8, 2, 4, 32, 128], P('dp', None, None, 'space'), may hold values from -6 to 6
- w1_policy: bfloat16 [9, 320, 320], P(None, 'tensor'), may hold values from -0.109375 to 0.109375
- w1_ref: bfloat16 [9, 320, 320], P(None, 'tensor'), may hold values from -0.109375 to 0.109375
- b1_policy: float32 [320], P('tensor'), may hold values from -3 to 3
- b1_ref: float32 [320], P('tensor'), may hold values from -3 to 3
- gn_gain_policy: float32 [320], P('tensor'), may hold values from 0.25 to 1.75
- gn_bias_policy: float32 [320], P('tensor'), may hold values from -3 to 3
- gn_gain_ref: float32 [320], P('tensor'), may hold values from 0.25 to 1.75
- gn_bias_ref: float32 [320], P('tensor'), may hold values from -3 to 3
- w2_policy: bfloat16 [9, 4, 320], P(None, None, 'tensor'), may hold values from -0.109375 to 0.109375
- w2_ref: bfloat16 [9, 4, 320], P(None, None, 'tensor'), may hold values from -0.109375 to 0.109375
- time_table: float32 [1000, 320], P(None, 'tensor'), may hold values from -3 to 3
- timestep: int32 [8], P('dp'), may hold values from 0 to 999
- winner: int32 [8], P('dp'), may hold values from 0 to 1
Outputs:
- logits: float32 [8], P('dp')
- grad_w1: float32 [9, 320, 320], P(None, 'tensor', ('dp', 'space'))
- grad_w2: float32 [9, 4, 320], P(None, None, 'tensor')
The draws below stay inside these ranges and needn't reach their ends.
All inputs are finite; a program needn't handle non-finite values.
Results may differ from the reference program's by a relative error of at most 0.0068.
Values may be sent and summed in bfloat16 or wider, within the bound.
No kernel may reach another device: no remote copies, remote signals or barrier semaphores. Data moves between devices by JAX's collectives and lax.ppermute only.
A program may use at most 64 MiB of HBM per device.

```python
import jax
import jax.numpy as jnp
from jax import lax

C = 320
OUT_CH = 4
STEPS = 1000
GROUPS = 32
W = 128
H = 32
PAIRS = 8


def place_ends(values, stream_key, smallest, largest):
    longest = values.shape.index(max(values.shape))
    spots = []
    for shift in (0, 1):
        where = [jax.random.randint(jax.random.fold_in(stream_key, axis), (), 0, length) for axis, length in enumerate(values.shape)]
        where[longest] = (where[longest] + shift) % values.shape[longest]
        spots.append(tuple(where))
    return values.at[spots[0]].set(smallest).at[spots[1]].set(largest)


def level_of(key, shape, pieces, smallest, largest):
    def one(dim, blocks):
        heights = jax.random.uniform(jax.random.fold_in(jax.random.fold_in(key, 6), dim), (blocks,), jnp.float32, smallest / len(pieces), largest / len(pieces))
        return jnp.repeat(jnp.exp(heights), shape[dim] // blocks).reshape((-1,) + (1,) * (len(shape) - dim - 1))

    loudness = one(*pieces[0])
    for cut in pieces[1:]:
        loudness = loudness * one(*cut)
    return loudness


def bell_draw(key, shape, scale, limit, shards=(), dtype=jnp.bfloat16):
    factor_of = level_of(key, shape, shards, -0.22, 0.18) if shards else 1.0
    values = jax.random.normal(key, shape, jnp.float32) * scale * factor_of
    return jnp.minimum(jnp.maximum(values, -limit), limit).astype(dtype)


def setup_inputs(seed: int = 0) -> dict:
    streams_of = jax.random.split(jax.random.key(seed), 17)
    feat_policy = bell_draw(streams_of[0], (PAIRS, 2, C, H, W), 1.0, 6.0, ((0, 8), (2, 4), (3, 8)))
    feat_ref = bell_draw(streams_of[1], (PAIRS, 2, C, H, W), 1.0, 6.0, ((0, 8), (2, 4), (3, 8)))
    noise = bell_draw(streams_of[2], (PAIRS, 2, OUT_CH, H, W), 1.0, 6.0, ((0, 8), (3, 8)), jnp.float32)
    w1_policy = bell_draw(streams_of[3], (9, C, C), (9 * C) ** -0.5, 0.109375, ((1, 4),))
    w1_ref = bell_draw(streams_of[4], (9, C, C), (9 * C) ** -0.5, 0.109375, ((1, 4),))
    b1_policy = bell_draw(streams_of[5], (C,), 0.5, 3.0, ((0, 4),), jnp.float32)
    b1_ref = bell_draw(streams_of[6], (C,), 0.5, 3.0, ((0, 4),), jnp.float32)
    gn_gain_policy = jnp.clip(1.0 + 0.15 * jax.random.normal(streams_of[7], (C,), jnp.float32), 0.25, 1.75)
    gn_bias_policy = bell_draw(streams_of[8], (C,), 0.5, 3.0, ((0, 4),), jnp.float32)
    gn_gain_ref = jnp.clip(1.0 + 0.15 * jax.random.normal(streams_of[9], (C,), jnp.float32), 0.25, 1.75)
    gn_bias_ref = bell_draw(streams_of[10], (C,), 0.5, 3.0, ((0, 4),), jnp.float32)
    w2_policy = bell_draw(streams_of[11], (9, OUT_CH, C), (9 * C) ** -0.5, 0.109375, ((2, 4),))
    w2_ref = bell_draw(streams_of[12], (9, OUT_CH, C), (9 * C) ** -0.5, 0.109375, ((2, 4),))
    time_table = bell_draw(streams_of[13], (STEPS, C), 0.5, 3.0, ((1, 4),), jnp.float32)
    timestep = place_ends(jax.random.randint(streams_of[14], (PAIRS,), 0, STEPS), jax.random.fold_in(streams_of[14], 1), 0, STEPS - 1).astype(jnp.int32)
    winner = place_ends(jax.random.randint(streams_of[15], (PAIRS,), 0, 2), jax.random.fold_in(streams_of[15], 1), 0, 1).astype(jnp.int32)
    return dict(feat_policy=feat_policy, feat_ref=feat_ref, noise=noise, w1_policy=w1_policy, w1_ref=w1_ref, b1_policy=b1_policy, b1_ref=b1_ref, gn_gain_policy=gn_gain_policy, gn_bias_policy=gn_bias_policy, gn_gain_ref=gn_gain_ref, gn_bias_ref=gn_bias_ref, w2_policy=w2_policy, w2_ref=w2_ref, time_table=time_table, timestep=timestep, winner=winner)


dpo_beta = 500.0
norm_eps = 1e-05

def to_kernel(weights):
    return weights.reshape(3, 3, weights.shape[1], weights.shape[2]).transpose(2, 3, 0, 1).astype(jnp.float32)

def flip_kernel(weights):
    shaped = weights.reshape(3, 3, weights.shape[1], weights.shape[2])[::-1, ::-1]
    return shaped.transpose(3, 2, 0, 1).astype(jnp.float32)

def conv_same(inputs, kernel):
    return lax.conv_general_dilated(inputs, kernel, (1, 1), ((1, 1), (1, 1)), dimension_numbers=('NCHW', 'OIHW', 'NCHW'), precision=lax.Precision.HIGHEST)

def kernel_grad(inputs, deltas):
    result = lax.conv_general_dilated(inputs, deltas, (1, 1), ((1, 1), (1, 1)), dimension_numbers=('CNHW', 'IOHW', 'NCHW'), precision=lax.Precision.HIGHEST)
    return result.transpose(2, 3, 1, 0).reshape(9, result.shape[1], result.shape[0])

def group_view(values):
    return values.reshape(values.shape[0], GROUPS, C // GROUPS, values.shape[2], values.shape[3])

def group_norm(pre_values, gain_vec, bias_vec):
    shaped = group_view(pre_values)
    group_mean = lax.optimization_barrier(jnp.mean(shaped, axis=(2, 3, 4), keepdims=True))
    group_square = lax.optimization_barrier(jnp.mean(shaped * shaped, axis=(2, 3, 4), keepdims=True))
    inv_std = lax.rsqrt(group_square - group_mean * group_mean + norm_eps)
    centered = ((shaped - group_mean) * inv_std).reshape(pre_values.shape)
    normed = centered * gain_vec[None, :, None, None] + bias_vec[None, :, None, None]
    return (normed, centered, inv_std)

def reference(feat_policy, feat_ref, noise, w1_policy, w1_ref, b1_policy, b1_ref, gn_gain_policy, gn_bias_policy, gn_gain_ref, gn_bias_ref, w2_policy, w2_ref, time_table, timestep, winner):
    kernel_one_policy = to_kernel(w1_policy)
    kernel_one_frozen = to_kernel(w1_ref)
    kernel_two_policy = to_kernel(w2_policy)
    kernel_two_frozen = to_kernel(w2_ref)
    kernel_back = flip_kernel(w2_policy)
    cell_total = OUT_CH * H * W

    def pair_step(carry, inputs):
        grad_one, grad_two = carry
        pair_policy, pair_frozen, pair_noise, step_index, pair_winner = inputs
        shift = time_table[step_index]
        pre_policy = conv_same(pair_policy.astype(jnp.float32), kernel_one_policy) + (b1_policy + shift)[None, :, None, None]
        pre_frozen = conv_same(pair_frozen.astype(jnp.float32), kernel_one_frozen) + (b1_ref + shift)[None, :, None, None]
        normed_policy, centered_policy, inv_policy = group_norm(pre_policy, gn_gain_policy, gn_bias_policy)
        normed_frozen, centered_frozen, inv_frozen = group_norm(pre_frozen, gn_gain_ref, gn_bias_ref)
        hidden_policy = jax.nn.silu(normed_policy).astype(jnp.bfloat16)
        hidden_frozen = jax.nn.silu(normed_frozen).astype(jnp.bfloat16)
        pred_policy = conv_same(hidden_policy.astype(jnp.float32), kernel_two_policy)
        pred_frozen = conv_same(hidden_frozen.astype(jnp.float32), kernel_two_frozen)
        err_policy = lax.optimization_barrier(jnp.mean((pred_policy - pair_noise) ** 2, axis=(1, 2, 3)))
        err_frozen = lax.optimization_barrier(jnp.mean((pred_frozen - pair_noise) ** 2, axis=(1, 2, 3)))
        pair_sign = 1.0 - 2.0 * pair_winner.astype(jnp.float32)
        logit = -0.5 * dpo_beta * pair_sign * (err_policy[0] - err_policy[1] - (err_frozen[0] - err_frozen[1]))
        weight = jax.nn.sigmoid(-logit)
        scaled = dpo_beta * weight * pair_sign / cell_total * jnp.array([1.0, -1.0], jnp.float32)
        dpred = (scaled[:, None, None, None] * (pred_policy - pair_noise)).astype(jnp.bfloat16)
        grad_two = grad_two + kernel_grad(hidden_policy.astype(jnp.float32), dpred.astype(jnp.float32))
        dhidden = conv_same(dpred.astype(jnp.float32), kernel_back)
        gate_value = jax.nn.sigmoid(normed_policy)
        gnorm = dhidden * gate_value * (1.0 + normed_policy * (1.0 - gate_value)) * gn_gain_policy[None, :, None, None]
        grouped_grad = group_view(gnorm)
        grouped_centered = group_view(centered_policy)
        first_mean = lax.optimization_barrier(jnp.mean(grouped_grad, axis=(2, 3, 4), keepdims=True))
        second_mean = lax.optimization_barrier(jnp.mean(grouped_grad * grouped_centered, axis=(2, 3, 4), keepdims=True))
        delta = (inv_policy * (grouped_grad - first_mean - grouped_centered * second_mean)).reshape(pre_policy.shape).astype(jnp.bfloat16)
        grad_one = grad_one + kernel_grad(pair_policy.astype(jnp.float32), delta.astype(jnp.float32))
        return ((grad_one, grad_two), logit)
    start_one = jnp.zeros((9, C, C), jnp.float32)
    start_two = jnp.zeros((9, OUT_CH, C), jnp.float32)
    (grad_one, grad_two), logits = lax.scan(pair_step, (start_one, start_two), (feat_policy, feat_ref, noise, timestep, winner))
    return (logits, grad_one, grad_two)
```

```python
import functools

import jax
import jax.numpy as jnp
from jax import lax
from jax.experimental import pallas as pl
from jax.experimental.pallas import tpu as pltpu
from jax.sharding import PartitionSpec as P

C = 320
GROUPS = 32
BETA = 500.0
EPS = 1e-05
CH = 80
ROWS = 4
COLS = 128
PIX = ROWS * COLS
GSIZE = C // GROUPS
LOCAL_GROUPS = CH // GSIZE
COUNT = float(GSIZE * 32 * 128)
CELLS = float(4 * 32 * 128)
F32 = jnp.float32
BF16 = jnp.bfloat16
HIGHEST = lax.Precision.HIGHEST

VM = pl.BlockSpec(memory_space=pltpu.VMEM)
SM = pl.BlockSpec(memory_space=pltpu.SMEM)


def call(kernel, ins, outs, name, flops, smem=0, scratch=()):
    in_bytes = sum(a.size * a.dtype.itemsize for a in ins)
    out_bytes = sum(s.size * s.dtype.itemsize for s in outs)
    return pl.pallas_call(
        kernel,
        out_shape=outs,
        in_specs=[SM] * smem + [VM] * (len(ins) - smem),
        out_specs=[VM] * len(outs),
        scratch_shapes=list(scratch),
        name=name,
        cost_estimate=pl.CostEstimate(
            flops=flops, bytes_accessed=in_bytes + out_bytes, transcendentals=0
        ),
        compiler_params=pltpu.CompilerParams(vmem_limit_bytes=40 * 1024 * 1024),
    )(*ins)


def arr(shape, dtype):
    return jax.ShapeDtypeStruct(shape, dtype)


def dot(a, b):
    return lax.dot_general(a, b, (((1,), (0,)), ((), ())), preferred_element_type=F32)


def dot_nt(a, b):
    return lax.dot_general(a, b, (((1,), (1,)), ((), ())), preferred_element_type=F32)


def exact_dot(a, b):
    return lax.dot_general(
        a, b, (((1,), (0,)), ((), ())), preferred_element_type=F32, precision=HIGHEST
    )


def from_left(tile):
    lane = lax.broadcasted_iota(jnp.int32, tile.shape, tile.ndim - 1)
    return jnp.where(lane == 0, 0.0, pltpu.roll(tile, 1, tile.ndim - 1))


def from_right(tile):
    lane = lax.broadcasted_iota(jnp.int32, tile.shape, tile.ndim - 1)
    return jnp.where(lane == COLS - 1, 0.0, pltpu.roll(tile, COLS - 1, tile.ndim - 1))


def row_of(tile, r):
    return tile[:, r * COLS : (r + 1) * COLS]


def members():
    group = lax.broadcasted_iota(jnp.int32, (2 * LOCAL_GROUPS, 2 * CH), 0)
    chan = lax.broadcasted_iota(jnp.int32, (2 * LOCAL_GROUPS, 2 * CH), 1)
    low = group * GSIZE
    return jnp.where((chan >= low) & (chan < low + GSIZE), 1.0, 0.0).astype(F32)


def spread(stat):
    chan = lax.broadcasted_iota(jnp.int32, (2 * CH, 2 * LOCAL_GROUPS), 0)
    group = lax.broadcasted_iota(jnp.int32, (2 * CH, 2 * LOCAL_GROUPS), 1)
    low = group * GSIZE
    pick = jnp.where((chan >= low) & (chan < low + GSIZE), 1.0, 0.0).astype(F32)
    return exact_dot(pick, stat)


def in_lanes(columns):
    rows = columns[0].shape[0]
    lane = lax.broadcasted_iota(jnp.int32, (rows, COLS), 1)
    out = jnp.zeros((rows, COLS), F32)
    for index, column in enumerate(columns):
        out = jnp.where(lane == index, column, out)
    return out


def conv_kernel(halo, t_ref, f0, f1, f2, f3, w_ref, bias_ref, pre_ref, up_ref, dn_ref, fs_ref, *ends):
    t = t_ref[0]
    for k, f in enumerate((f0, f1, f2, f3)):
        owner = lax.rem(t - k + 4, 4)
        base = pl.multiple_of(owner * CH, 16)
        for im in range(2):
            for r in range(ROWS):
                lo = im * PIX + r * COLS
                fs_ref[pl.ds(base, CH), lo : lo + COLS] = f[im, r]
    for im in range(2):
        feats = fs_ref[:, im * PIX : (im + 1) * PIX]
        taps = [dot(w_ref[ky * 3 * CH : (ky + 1) * 3 * CH, :], feats) for ky in range(3)]
        for r in range(-1, ROWS + 1):
            total = None
            for ky in range(3):
                src = r + ky - 1
                if 0 <= src < ROWS:
                    term = row_of(taps[ky], src)
                    total = term if total is None else total + term
            out = (
                total[CH : 2 * CH]
                + from_left(total[0:CH])
                + from_right(total[2 * CH : 3 * CH])
            )
            if r == -1:
                up_ref[im * CH : (im + 1) * CH, :] = out
            elif r == ROWS:
                dn_ref[im * CH : (im + 1) * CH, :] = out
            else:
                pre_ref[im * CH : (im + 1) * CH, r * COLS : (r + 1) * COLS] = (
                    out + bias_ref[im * CH : (im + 1) * CH, :]
                )
    if halo:
        for im in range(2):
            lanes = slice(im * COLS, (im + 1) * COLS)
            ends[0][:, lanes] = fs_ref[:, im * PIX : im * PIX + COLS]
            ends[1][:, lanes] = fs_ref[:, im * PIX + (ROWS - 1) * COLS : (im + 1) * PIX]


def stat_kernel(pre_p, left_p, right_p, pre_r, left_r, right_r, full_p, full_r, out_ref):
    columns = []
    for pre, left, right, full in (
        (pre_p, left_p, right_p, full_p),
        (pre_r, left_r, right_r, full_r),
    ):
        rows = [pre[:, r * COLS : (r + 1) * COLS] for r in range(ROWS)]
        rows[0] = rows[0] + left[...]
        rows[ROWS - 1] = rows[ROWS - 1] + right[...]
        total = rows[0] + rows[1] + rows[2] + rows[3]
        square = (
            rows[0] * rows[0] + rows[1] * rows[1] + rows[2] * rows[2] + rows[3] * rows[3]
        )
        for r in range(ROWS):
            full[:, r * COLS : (r + 1) * COLS] = rows[r]
        columns.append(jnp.sum(total, axis=1, keepdims=True))
        columns.append(jnp.sum(square, axis=1, keepdims=True))
    sums = exact_dot(members(), in_lanes(columns))
    for peer in range(out_ref.shape[0]):
        out_ref[peer] = sums


def moments(total):
    wide = spread(total / COUNT)
    result = []
    for m in range(2):
        mean = wide[:, 2 * m : 2 * m + 1]
        square = wide[:, 2 * m + 1 : 2 * m + 2]
        result.append((mean, lax.rsqrt(square - mean * mean + EPS)))
    return result


def hidden_kernel(full_p, full_r, sums_ref, col_ref, lift_ref, part_ref, hid_ref, stat_ref):
    stats = moments(jnp.sum(sums_ref[...], axis=0))
    stat_ref[...] = in_lanes([stats[0][0], stats[0][1]])
    for m, full in enumerate((full_p, full_r)):
        mean, inv = stats[m]
        gain = col_ref[:, 2 * m : 2 * m + 1]
        shift = col_ref[:, 2 * m + 1 : 2 * m + 2]
        normed = ((full[...] - mean) * inv) * gain + shift
        hidden = (normed * jax.nn.sigmoid(normed)).astype(BF16)
        if m == 0:
            hid_ref[...] = hidden
        taps = dot(lift_ref[m], hidden)
        for r in range(-1, ROWS + 1):
            totals = [None, None, None]
            for kx in range(3):
                for ky in range(3):
                    src = r + ky - 1
                    if 0 <= src < ROWS:
                        tap = 3 * ky + kx
                        term = taps[8 * tap : 8 * tap + 8, src * COLS : (src + 1) * COLS]
                        totals[kx] = term if totals[kx] is None else totals[kx] + term
            part_ref[m, r + 1] = totals[1] + from_left(totals[0]) + from_right(totals[2])


def pred_kernel(p0, p1, p2, p3, noise_ref, own_ref, left_ref, right_ref):
    for m in range(2):
        rows = []
        for r in range(ROWS + 2):
            total = p0[m, r] + p1[m, r] + p2[m, r] + p3[m, r]
            if 1 <= r <= ROWS:
                total = total - noise_ref[r - 1]
            own_ref[m, r] = total
            rows.append(total)
        left_ref[m, 0] = rows[0]
        left_ref[m, 1] = rows[1]
        right_ref[m, 0] = rows[ROWS]
        right_ref[m, 1] = rows[ROWS + 1]


def back_kernel(
    edge_ref, own, left, right, full_p, stat_ref, col_ref, hid_ref, drop_ref, gnorm_ref, out_ref
):
    top = edge_ref[0]
    bottom = edge_ref[1]
    residual = []
    errors = []
    for m in range(2):
        rows = [own[m, r] for r in range(ROWS + 2)]
        rows[0] = rows[0] + left[m, 0]
        rows[1] = rows[1] + left[m, 1]
        rows[ROWS] = rows[ROWS] + right[m, 0]
        rows[ROWS + 1] = rows[ROWS + 1] + right[m, 1]
        square = rows[1] * rows[1]
        for r in range(2, ROWS + 1):
            square = square + rows[r] * rows[r]
        errors.append(jnp.sum(square, axis=1, keepdims=True))
        if m == 0:
            rows[0] = jnp.where(top > 0, 0.0, rows[0])
            rows[ROWS + 1] = jnp.where(bottom > 0, 0.0, rows[ROWS + 1])
            residual = rows
    image = lax.broadcasted_iota(jnp.int32, (8, COLS), 0)
    residual = [jnp.where(image < 4, row, -row) for row in residual]
    moved = [
        [from_right(row) for row in residual],
        residual,
        [from_left(row) for row in residual],
    ]
    blocks = []
    for ky in range(3):
        for kx in range(3):
            blocks.append(
                jnp.concatenate([moved[kx][r + 2 - ky] for r in range(ROWS)], axis=1)
            )
    cot = jnp.concatenate(blocks, axis=0).astype(BF16)
    dhidden = dot(drop_ref[...], cot)
    mean = stat_ref[:, 0:1]
    inv = stat_ref[:, 1:2]
    gain = col_ref[:, 0:1]
    shift = col_ref[:, 1:2]
    centered = (full_p[...] - mean) * inv
    normed = centered * gain + shift
    gate = jax.nn.sigmoid(normed)
    gnorm = dhidden * gate * (1.0 + normed * (1.0 - gate)) * gain
    gnorm_ref[...] = gnorm
    first = jnp.sum(gnorm, axis=1, keepdims=True)
    second = jnp.sum(gnorm * centered, axis=1, keepdims=True)
    sums = exact_dot(members(), in_lanes([first, second]))
    grads = [dot_nt(cot, hid_ref[im * CH : (im + 1) * CH, :]) for im in range(2)]
    error = in_lanes(errors)
    pad = jnp.zeros((4, COLS - CH), F32)
    heads = []
    for tap in range(9):
        head = grads[0][8 * tap : 8 * tap + 4] + grads[1][8 * tap + 4 : 8 * tap + 8]
        heads.append(jnp.concatenate([head, pad], axis=1))
    for peer in range(out_ref.shape[0]):
        out_ref[peer, 0:16, :] = sums
        out_ref[peer, 16:24, :] = error
        out_ref[peer, 24:28, :] = heads[peer]
        out_ref[peer, 28:32, :] = heads[8]


def weight_kernel(
    win_ref, gnorm_ref, full_p, stat_ref, red_ref, fs_ref, above_ref, below_ref,
    out_ref, logit_ref, grad_ref, pack_ref
):
    total = jnp.sum(red_ref[...], axis=0)
    row = lax.broadcasted_iota(jnp.int32, (8, COLS), 0)
    signed = jnp.where(row < 4, total[16:24], -total[16:24])
    gaps = jnp.sum(signed, axis=0, keepdims=True)
    gap = (gaps[:, 0:1] - gaps[:, 1:2]) * (1.0 / CELLS)
    sign = 1.0 - 2.0 * win_ref[0].astype(F32)
    logit = (-0.5 * BETA) * sign * gap
    logit_ref[...] = logit
    scale = (BETA / CELLS) * sign * jax.nn.sigmoid(-logit)
    wide = spread(total[0:16] / COUNT)
    mean = stat_ref[:, 0:1]
    inv = stat_ref[:, 1:2]
    centered = (full_p[...] - mean) * inv
    delta = inv * (gnorm_ref[...] - wide[:, 0:1] - centered * wide[:, 1:2])
    shifted = [[], [], []]
    for im in range(2):
        for r in range(ROWS):
            part = delta[im * CH : (im + 1) * CH, r * COLS : (r + 1) * COLS]
            shifted[0].append(from_right(part))
            shifted[1].append(part)
            shifted[2].append(from_left(part))
    stack = jnp.concatenate(
        [jnp.concatenate(parts, axis=1).astype(BF16) for parts in shifted]
        + [jnp.zeros((16, 2 * PIX), BF16)],
        axis=0,
    )
    for ky in range(3):
        pieces = []
        for im in range(2):
            lanes = slice(im * COLS, (im + 1) * COLS)
            if ky == 0:
                pieces.append(above_ref[:, lanes])
                pieces.append(fs_ref[:, im * PIX : im * PIX + 3 * COLS])
            elif ky == 1:
                pieces.append(fs_ref[:, im * PIX : (im + 1) * PIX])
            else:
                pieces.append(fs_ref[:, im * PIX + COLS : (im + 1) * PIX])
                pieces.append(below_ref[:, lanes])
        feats = jnp.concatenate(pieces, axis=1)
        grad = dot_nt(feats, stack) * scale
        grad_ref[2 * ky] = grad[:, 0:COLS]
        grad_ref[2 * ky + 1] = grad[:, COLS : 2 * COLS]
    peers = out_ref.shape[0]
    chunk = C // peers
    rows = out_ref.shape[1]
    for ii in range(chunk):
        for half in range(6):
            pack_ref[pl.ds(half * chunk + ii, peers, stride=rows), :] = grad_ref[
                half, pl.ds(ii, peers, stride=chunk), :
            ]
    head = total[24:32] * scale
    for peer in range(peers):
        tile = pack_ref[peer * rows : peer * rows + 32, :]
        keep = lax.broadcasted_iota(jnp.int32, (32, COLS), 0) < 6 * chunk
        out_ref[peer, 0:32, :] = jnp.where(keep, tile, 0.0).astype(BF16)
        out_ref[peer, 32:40, :] = head.astype(BF16)


def sum_kernel(space, got_ref, one_ref, two_ref):
    peers = got_ref.shape[0]
    chunk = C // peers
    per_space = []
    for s in range(space):
        total = got_ref[s].astype(F32)
        for d in range(1, peers // space):
            total = total + got_ref[d * space + s].astype(F32)
        per_space.append(total)
        two_ref[s] = total[32:36, 0:CH]
        if s == 0:
            two_ref[8] = total[36:40, 0:CH]
    total = per_space[0]
    for s in range(1, space):
        total = total + per_space[s]
    for ky in range(3):
        lo = 2 * ky * chunk
        wide = jnp.concatenate(
            [total[lo : lo + chunk], total[lo + chunk : lo + 2 * chunk]], axis=1
        )
        for kx in range(3):
            one_ref[3 * ky + kx] = wide[:, kx * CH : (kx + 1) * CH]


def ring(axis, step):
    count = lax.axis_size(axis)
    return [(i, (i + step) % count) for i in range(count)]


def line(axis, step):
    count = lax.axis_size(axis)
    return [(i, i + step) for i in range(count) if 0 <= i + step < count]


def body(
    feat_policy,
    feat_ref,
    noise,
    w1_policy,
    w1_ref,
    b1_policy,
    b1_ref,
    gn_gain_policy,
    gn_bias_policy,
    gn_gain_ref,
    gn_bias_ref,
    w2_policy,
    w2_ref,
    time_table,
    timestep,
    winner,
):
    space = lax.axis_size("space")
    peers = lax.axis_size("dp") * space
    t_index = lax.axis_index("tensor").astype(jnp.int32).reshape(1)
    s_index = lax.axis_index("space")
    edges = jnp.stack([s_index == 0, s_index == space - 1]).astype(jnp.int32)

    def gather(feat):
        own = feat[0].transpose(0, 2, 1, 3)
        return [own] + [lax.ppermute(own, "tensor", ring("tensor", k)) for k in (1, 2, 3)]

    parts_p = gather(feat_policy)
    parts_r = gather(feat_ref)

    shift = lax.dynamic_slice_in_dim(time_table, timestep[0], 1, 0)[0]

    def twice(vec):
        return jnp.concatenate([vec, vec])

    bias_p = twice(b1_policy + shift)[:, None]
    bias_r = twice(b1_ref + shift)[:, None]
    columns = jnp.stack(
        [twice(gn_gain_policy), twice(gn_bias_policy), twice(gn_gain_ref), twice(gn_bias_ref)],
        axis=1,
    )

    def lifted(w2):
        zero = jnp.zeros((9, 4, CH), w2.dtype)
        first = jnp.concatenate([w2, zero], axis=1).reshape(72, CH)
        second = jnp.concatenate([zero, w2], axis=1).reshape(72, CH)
        return jnp.concatenate([first, second], axis=1)

    lift = jnp.stack([lifted(w2_policy), lifted(w2_ref)])
    drop = lift[0].T
    noise_rows = noise[0].transpose(2, 0, 1, 3).reshape(ROWS, 8, COLS)

    conv_flops = 2 * 9 * C * CH * 2 * PIX

    def conv(parts, w1, bias, halo, name):
        outs = [
            arr((2 * CH, PIX), F32),
            arr((2 * CH, COLS), F32),
            arr((2 * CH, COLS), F32),
            arr((C, 2 * PIX), BF16),
        ]
        if halo:
            outs += [arr((C, 2 * COLS), BF16)] * 2
        return call(
            functools.partial(conv_kernel, halo),
            [t_index, *parts, w1.reshape(9 * CH, C), bias],
            outs,
            name,
            conv_flops,
            smem=1,
        )

    pre_p, up_p, dn_p, feats, first_row, last_row = conv(parts_p, w1_policy, bias_p, True, "conv_p")
    right_p = lax.ppermute(up_p, "space", line("space", -1))
    left_p = lax.ppermute(dn_p, "space", line("space", 1))
    pre_r, up_r, dn_r, _ = conv(parts_r, w1_ref, bias_r, False, "conv_r")
    right_r = lax.ppermute(up_r, "space", line("space", -1))
    left_r = lax.ppermute(dn_r, "space", line("space", 1))
    below = lax.ppermute(first_row, "space", line("space", -1))
    above = lax.ppermute(last_row, "space", line("space", 1))

    full_p, full_r, sums = call(
        stat_kernel,
        [pre_p, left_p, right_p, pre_r, left_r, right_r],
        [arr((2 * CH, PIX), F32), arr((2 * CH, PIX), F32), arr((space, 16, COLS), F32)],
        "stats",
        10**6,
    )
    sums = lax.all_to_all(sums, "space", 0, 0, tiled=True)
    part, hidden, stat = call(
        hidden_kernel,
        [full_p, full_r, sums, columns, lift],
        [arr((2, ROWS + 2, 8, COLS), F32), arr((2 * CH, PIX), BF16), arr((2 * CH, COLS), F32)],
        "hidden",
        10**7,
    )
    others = [lax.ppermute(part, "tensor", ring("tensor", k)) for k in (1, 2, 3)]
    own, to_left, to_right = call(
        pred_kernel,
        [part, *others, noise_rows],
        [arr((2, ROWS + 2, 8, COLS), F32), arr((2, 2, 8, COLS), F32), arr((2, 2, 8, COLS), F32)],
        "pred",
        10**5,
    )
    from_l = lax.ppermute(to_right, "space", line("space", 1))
    from_r = lax.ppermute(to_left, "space", line("space", -1))
    gnorm, partial = call(
        back_kernel,
        [edges, own, from_l, from_r, full_p, stat, columns, hidden, drop],
        [arr((2 * CH, PIX), F32), arr((space, 32, COLS), F32)],
        "back",
        10**7,
        smem=1,
    )
    partial = lax.all_to_all(partial, "space", 0, 0, tiled=True)
    packed, logits = call(
        weight_kernel,
        [winner, gnorm, full_p, stat, partial, feats, above, below],
        [arr((peers, 40, COLS), BF16), arr((1, 1), F32)],
        "weight",
        conv_flops,
        smem=1,
        scratch=[pltpu.VMEM((6, C, COLS), F32), pltpu.VMEM((peers * 40, COLS), F32)],
    )
    got = lax.all_to_all(packed, ("dp", "space"), 0, 0, tiled=True)
    grad_one, grad_two = call(
        functools.partial(sum_kernel, space),
        [got],
        [arr((9, C // peers, CH), F32), arr((9, 4, CH), F32)],
        "total",
        10**6,
    )
    return (logits.reshape(1), grad_one.transpose(0, 2, 1), grad_two)


def solution(mesh):
    in_specs = (
        P("dp", None, "tensor", "space", None),
        P("dp", None, "tensor", "space", None),
        P("dp", None, None, "space", None),
        P(None, "tensor", None),
        P(None, "tensor", None),
        P("tensor"),
        P("tensor"),
        P("tensor"),
        P("tensor"),
        P("tensor"),
        P("tensor"),
        P(None, None, "tensor"),
        P(None, None, "tensor"),
        P(None, "tensor"),
        P("dp"),
        P("dp"),
    )
    out_specs = (P("dp"), P(None, "tensor", ("dp", "space")), P(None, None, "tensor"))
    return jax.shard_map(body, mesh=mesh, in_specs=in_specs, out_specs=out_specs, check_vma=False)
```

```python
import functools

import jax
import jax.numpy as jnp
from jax import lax
from jax.experimental import pallas as pl
from jax.experimental.pallas import tpu as pltpu
from jax.sharding import PartitionSpec as P

C = 320
GROUPS = 32
BETA = 500.0
EPS = 1e-05
CH = 80
ROWS = 4
COLS = 128
PIX = ROWS * COLS
GSIZE = C // GROUPS
LOCAL_GROUPS = CH // GSIZE
COUNT = float(GSIZE * 32 * 128)
CELLS = float(4 * 32 * 128)
F32 = jnp.float32
BF16 = jnp.bfloat16
HIGHEST = lax.Precision.HIGHEST

VM = pl.BlockSpec(memory_space=pltpu.VMEM)
SM = pl.BlockSpec(memory_space=pltpu.SMEM)


def call(kernel, ins, outs, name, flops, smem=0, scratch=()):
    in_bytes = sum(a.size * a.dtype.itemsize for a in ins)
    out_bytes = sum(s.size * s.dtype.itemsize for s in outs)
    return pl.pallas_call(
        kernel,
        out_shape=outs,
        in_specs=[SM] * smem + [VM] * (len(ins) - smem),
        out_specs=[VM] * len(outs),
        scratch_shapes=list(scratch),
        name=name,
        cost_estimate=pl.CostEstimate(
            flops=flops, bytes_accessed=in_bytes + out_bytes, transcendentals=0
        ),
        compiler_params=pltpu.CompilerParams(vmem_limit_bytes=12 * 1024 * 1024),
    )(*ins)


def arr(shape, dtype):
    return jax.ShapeDtypeStruct(shape, dtype)


def dot(a, b):
    return lax.dot_general(a, b, (((1,), (0,)), ((), ())), preferred_element_type=F32)


def dot_nt(a, b):
    return lax.dot_general(a, b, (((1,), (1,)), ((), ())), preferred_element_type=F32)


def exact_dot(a, b):
    return lax.dot_general(
        a, b, (((1,), (0,)), ((), ())), preferred_element_type=F32, precision=HIGHEST
    )


def from_left(tile):
    lane = lax.broadcasted_iota(jnp.int32, tile.shape, tile.ndim - 1)
    return jnp.where(lane == 0, 0.0, pltpu.roll(tile, 1, tile.ndim - 1))


def from_right(tile):
    lane = lax.broadcasted_iota(jnp.int32, tile.shape, tile.ndim - 1)
    return jnp.where(lane == COLS - 1, 0.0, pltpu.roll(tile, COLS - 1, tile.ndim - 1))


def row_of(tile, r):
    return tile[:, r * COLS : (r + 1) * COLS]


def members():
    group = lax.broadcasted_iota(jnp.int32, (2 * LOCAL_GROUPS, 2 * CH), 0)
    chan = lax.broadcasted_iota(jnp.int32, (2 * LOCAL_GROUPS, 2 * CH), 1)
    low = group * GSIZE
    return jnp.where((chan >= low) & (chan < low + GSIZE), 1.0, 0.0).astype(F32)


def spread(stat):
    chan = lax.broadcasted_iota(jnp.int32, (2 * CH, 2 * LOCAL_GROUPS), 0)
    group = lax.broadcasted_iota(jnp.int32, (2 * CH, 2 * LOCAL_GROUPS), 1)
    low = group * GSIZE
    pick = jnp.where((chan >= low) & (chan < low + GSIZE), 1.0, 0.0).astype(F32)
    return exact_dot(pick, stat)


def in_lanes(columns):
    rows = columns[0].shape[0]
    lane = lax.broadcasted_iota(jnp.int32, (rows, COLS), 1)
    out = jnp.zeros((rows, COLS), F32)
    for index, column in enumerate(columns):
        out = jnp.where(lane == index, column, out)
    return out


def prep_kernel(
    place_ref, b_p, b_r, gain_p, off_p, gain_r, off_r, w2_p, w2_r, table_ref, noise_ref,
    col_ref, lift_ref, drop_ref, rows_ref
):
    lane = lax.broadcasted_iota(jnp.int32, table_ref.shape, 1)
    shift = jnp.sum(
        jnp.where(lane == place_ref[6], table_ref[...], 0.0), axis=1, keepdims=True
    )
    eye = lax.broadcasted_iota(jnp.int32, (CH, CH), 0) == lax.broadcasted_iota(
        jnp.int32, (CH, CH), 1
    )

    def upright(ref):
        return jnp.sum(jnp.where(eye, ref[...], 0.0), axis=1, keepdims=True)

    block = in_lanes(
        [
            upright(gain_p),
            upright(off_p),
            upright(gain_r),
            upright(off_r),
            upright(b_p) + shift,
            upright(b_r) + shift,
        ]
    )
    col_ref[0:CH, :] = block
    col_ref[CH : 2 * CH, :] = block
    one = jnp.where(eye, 1.0, 0.0).astype(BF16)
    zero = jnp.zeros((4, CH), F32)
    for m, ref in enumerate((w2_p, w2_r)):
        for im in range(2):
            pieces = []
            for tap in range(9):
                rows = ref[tap].astype(F32)
                pieces += [rows, zero] if im == 0 else [zero, rows]
            padded = jnp.concatenate(pieces, axis=0).astype(BF16)
            lift_ref[m, im] = padded
            if m == 0:
                drop_ref[im * CH : (im + 1) * CH, :] = dot_nt(one, padded).astype(BF16)
    for im in range(2):
        for o in range(4):
            slot = im * 4 + o
            for r in range(ROWS):
                rows_ref[r, slot : slot + 1, :] = noise_ref[im, o, r : r + 1, :]


def conv_kernel(last, t_ref, f0, f1, f2a, f2b, f3, w_ref, col_ref, *refs):
    if last:
        side_l, side_r, noise_ref, pre_ref, up_ref, dn_ref, send_l, send_r, fs_ref = refs
    else:
        pre_ref, up_ref, dn_ref, send_l, send_r, fs_ref = refs
    t = t_ref[5]
    bias = 5 if last else 4
    for k in range(4):
        base = pl.multiple_of(lax.rem(t - k + 4, 4) * CH, 16)
        for im in range(2):
            for r in range(ROWS):
                lo = im * PIX + r * COLS
                if k == 2:
                    piece = f2a[r] if im == 0 else f2b[r]
                else:
                    piece = (f0, f1, None, f3)[k][im, r]
                fs_ref[pl.ds(base, CH), lo : lo + COLS] = piece
    if last:
        send_l[0:960, :] = side_l[...]
        send_r[0:960, :] = side_r[...]
        for ref, rows in ((send_l, (0, 1)), (send_r, (2, 3))):
            for index, r in enumerate(rows):
                value = noise_ref[r]
                high = value.astype(BF16).astype(F32)
                both = jnp.concatenate([high, value - high], axis=0).astype(BF16)
                ref[1600 + 16 * index : 1616 + 16 * index, :] = both
        start, keep_l, keep_r = 960, (-1, 0), (ROWS - 1, ROWS)
    else:
        start, keep_l, keep_r = 0, (-1, 0, 1, 2), (1, 2, 3, 4)
    for im in range(2):
        feats = fs_ref[:, im * PIX : (im + 1) * PIX]
        taps = [dot(w_ref[ky * 3 * CH : (ky + 1) * 3 * CH, :], feats) for ky in range(3)]
        chans = slice(im * CH, (im + 1) * CH)
        for r in range(-1, ROWS + 1):
            total = None
            for ky in range(3):
                src = r + ky - 1
                if 0 <= src < ROWS:
                    term = row_of(taps[ky], src)
                    total = term if total is None else total + term
            out = (
                total[CH : 2 * CH]
                + from_left(total[0:CH])
                + from_right(total[2 * CH : 3 * CH])
            )
            if r == -1:
                up_ref[chans, :] = out
            elif r == ROWS:
                dn_ref[chans, :] = out
            else:
                out = out + col_ref[chans, bias : bias + 1]
                pre_ref[chans, r * COLS : (r + 1) * COLS] = out
            for keep, ref in ((keep_l, send_l), (keep_r, send_r)):
                if r in keep:
                    lo = start + keep.index(r) * 2 * CH + im * CH
                    high = out.astype(BF16)
                    ref[lo : lo + CH, :] = high
                    if r in (-1, 0, ROWS - 1, ROWS):
                        near = 0 if r < 1 else 2 - len(keep)
                        slot = keep.index(r) + near + len(keep)
                        lo = start + slot * 2 * CH + im * CH
                        ref[lo : lo + CH, :] = (out - high.astype(F32)).astype(BF16)


def stat_kernel(
    pre_p, up_p, dn_p, pre_r, up_r, dn_r, left, right, noise_ref, ext_p, ext_r, noise_ext, out_ref
):
    def got(ref, index):
        return ref[index * 2 * CH : (index + 1) * 2 * CH, :].astype(F32)

    def near(ref, index, low):
        return got(ref, index) + got(ref, low)

    columns = []
    for pre, up, dn, ext, first, halo in (
        (pre_p, up_p, dn_p, ext_p, 0, 3),
        (pre_r, up_r, dn_r, ext_r, 6, 1),
    ):
        low = first + halo + 1
        rows = [pre[:, r * COLS : (r + 1) * COLS] for r in range(ROWS)]
        rows[0] = rows[0] + near(left, first + halo, low + 1)
        rows[ROWS - 1] = rows[ROWS - 1] + near(right, first, low)
        total = rows[0] + rows[1] + rows[2] + rows[3]
        square = (
            rows[0] * rows[0] + rows[1] * rows[1] + rows[2] * rows[2] + rows[3] * rows[3]
        )
        before = [got(left, first + index) for index in range(halo)]
        before[-1] = near(left, first + halo - 1, low) + up[...]
        after = [got(right, first + 1 + index) for index in range(halo)]
        after[0] = near(right, first + 1, low + 1) + dn[...]
        for index, row in enumerate(before + rows + after):
            ext[:, index * COLS : (index + 1) * COLS] = row
        columns.append(jnp.sum(total, axis=1, keepdims=True))
        columns.append(jnp.sum(square, axis=1, keepdims=True))
    for index in range(2):
        lo = 1600 + 16 * index
        pair = left[lo : lo + 16, :].astype(F32)
        noise_ext[index] = pair[0:8] + pair[8:16]
        pair = right[lo : lo + 16, :].astype(F32)
        noise_ext[ROWS + 2 + index] = pair[0:8] + pair[8:16]
    for r in range(ROWS):
        noise_ext[2 + r] = noise_ref[r]
    sums = exact_dot(members(), in_lanes(columns))
    for peer in range(out_ref.shape[0]):
        out_ref[peer] = sums


def moments(total):
    wide = spread(total / COUNT)
    result = []
    for m in range(2):
        mean = wide[:, 2 * m : 2 * m + 1]
        square = wide[:, 2 * m + 1 : 2 * m + 2]
        result.append((mean, lax.rsqrt(square - mean * mean + EPS)))
    return result


def hidden_kernel(
    edge_ref, ext_p, ext_r, sums_ref, col_ref, lift_ref, part_ref, hid_ref, stat_ref
):
    stats = moments(jnp.sum(sums_ref[...], axis=0))
    stat_ref[...] = in_lanes([stats[0][0], stats[0][1]])
    for m, (ext, halo, start) in enumerate(((ext_p, 3, 0), (ext_r, 1, 8))):
        mean, inv = stats[m]
        gain = col_ref[:, 2 * m : 2 * m + 1]
        shift = col_ref[:, 2 * m + 1 : 2 * m + 2]
        pieces = []
        for index in range(ROWS + 2 * halo):
            value = ext[:, index * COLS : (index + 1) * COLS]
            normed = ((value - mean) * inv) * gain + shift
            hidden = normed * jax.nn.sigmoid(normed)
            if index < halo:
                hidden = jnp.where(edge_ref[1] > 0, 0.0, hidden)
            if index >= ROWS + halo:
                hidden = jnp.where(edge_ref[2] > 0, 0.0, hidden)
            hidden = hidden.astype(BF16)
            if m == 0 and halo <= index < halo + ROWS:
                hid_ref[:, (index - halo) * COLS : (index - halo + 1) * COLS] = hidden
            pieces.append(hidden)
        joined = jnp.concatenate(pieces, axis=1)
        taps = dot(lift_ref[m, 0], joined[0:CH]) + dot(lift_ref[m, 1], joined[CH : 2 * CH])
        for index in range(ROWS + 2 * halo - 2):
            totals = [None, None, None]
            for kx in range(3):
                for ky in range(3):
                    tap = 3 * ky + kx
                    lo = (index + ky) * COLS
                    term = taps[8 * tap : 8 * tap + 8, lo : lo + COLS]
                    totals[kx] = term if totals[kx] is None else totals[kx] + term
            part_ref[start + index] = (
                totals[1] + from_left(totals[0]) + from_right(totals[2])
            )


def back_kernel(
    edge_ref, p0, p1, p2, p3, noise_ext, ext_p, stat_ref, col_ref, hid_ref, drop_ref,
    gnorm_ref, head_ref, out_ref
):
    def pred(index):
        return (p0[index] + p1[index]) + (p2[index] + p3[index])

    residual = [pred(index) - noise_ext[index] for index in range(ROWS + 4)]
    frozen = [pred(8 + r) - noise_ext[2 + r] for r in range(ROWS)]
    errors = []
    for rows in (residual[2 : 2 + ROWS], frozen):
        square = rows[0] * rows[0]
        for row in rows[1:]:
            square = square + row * row
        errors.append(jnp.sum(square, axis=1, keepdims=True))
    image = lax.broadcasted_iota(jnp.int32, (8, COLS), 0)
    residual = [jnp.where(image < 4, row, -row) for row in residual]
    for index in range(2):
        residual[index] = jnp.where(edge_ref[1] > 0, 0.0, residual[index])
        residual[ROWS + 2 + index] = jnp.where(edge_ref[2] > 0, 0.0, residual[ROWS + 2 + index])
    moved = [
        [from_right(row) for row in residual],
        residual,
        [from_left(row) for row in residual],
    ]
    blocks = []
    for ky in range(3):
        for kx in range(3):
            blocks.append(
                jnp.concatenate([moved[kx][r + 2 - ky] for r in range(ROWS + 2)], axis=1)
            )
    cot = jnp.concatenate(blocks, axis=0).astype(BF16)
    dhidden = dot(drop_ref[...], cot)
    mean = stat_ref[:, 0:1]
    inv = stat_ref[:, 1:2]
    gain = col_ref[:, 0:1]
    shift = col_ref[:, 1:2]
    first = None
    second = None
    for index in range(ROWS + 2):
        lanes = slice(index * COLS, (index + 1) * COLS)
        centered = (ext_p[:, (index + 2) * COLS : (index + 3) * COLS] - mean) * inv
        normed = centered * gain + shift
        gate = jax.nn.sigmoid(normed)
        gnorm = dhidden[:, lanes] * gate * (1.0 + normed * (1.0 - gate)) * gain
        gnorm_ref[:, lanes] = gnorm
        if 1 <= index <= ROWS:
            first = gnorm if first is None else first + gnorm
            extra = gnorm * centered
            second = extra if second is None else second + extra
    first = jnp.sum(first, axis=1, keepdims=True)
    second = jnp.sum(second, axis=1, keepdims=True)
    sums = exact_dot(members(), in_lanes([first, second]))
    mine = cot[:, COLS : (ROWS + 1) * COLS]
    grads = [dot_nt(mine, hid_ref[im * CH : (im + 1) * CH, :]) for im in range(2)]
    error = in_lanes(errors)
    head_ref[...] = jnp.zeros(head_ref.shape, F32)
    for tap in range(9):
        head = grads[0][8 * tap : 8 * tap + 4] + grads[1][8 * tap + 4 : 8 * tap + 8]
        head_ref[4 * tap : 4 * tap + 4, 0:CH] = head
    for peer in range(out_ref.shape[0]):
        out_ref[peer, 0:16, :] = sums
        out_ref[peer, 16:24, :] = error


def weight_kernel(
    place_ref, gnorm_ref, ext_p, stat_ref, red_ref, fs_ref, head_ref,
    keep_ref, send_ref, both_ref, logit_ref, grad_ref, pack_ref
):
    total = jnp.sum(red_ref[...], axis=0)
    row = lax.broadcasted_iota(jnp.int32, (8, COLS), 0)
    signed = jnp.where(row < 4, total[16:24], -total[16:24])
    gaps = jnp.sum(signed, axis=0, keepdims=True)
    gap = (gaps[:, 0:1] - gaps[:, 1:2]) * (1.0 / CELLS)
    sign = 1.0 - 2.0 * place_ref[0].astype(F32)
    logit = (-0.5 * BETA) * sign * gap
    logit_ref[...] = logit
    scale = (BETA / CELLS) * sign * jax.nn.sigmoid(-logit)
    wide = spread(total[0:16] / COUNT)
    mean = stat_ref[:, 0:1]
    inv = stat_ref[:, 1:2]
    parts = []
    for index in range(ROWS + 2):
        centered = (ext_p[:, (index + 2) * COLS : (index + 3) * COLS] - mean) * inv
        gnorm = gnorm_ref[:, index * COLS : (index + 1) * COLS]
        delta = inv * (gnorm - wide[:, 0:1] - centered * wide[:, 1:2])
        if index == 0:
            delta = jnp.where(place_ref[1] > 0, 0.0, delta)
        if index == ROWS + 1:
            delta = jnp.where(place_ref[2] > 0, 0.0, delta)
        parts.append(
            [from_right(delta).astype(BF16), delta.astype(BF16), from_left(delta).astype(BF16)]
        )
    blank = jnp.zeros((16, 2 * PIX), BF16)
    for ky in range(3):
        rows = []
        for kx in range(3):
            tiles = []
            for im in range(2):
                for r in range(ROWS):
                    tiles.append(parts[r + 2 - ky][kx][im * CH : (im + 1) * CH])
            rows.append(jnp.concatenate(tiles, axis=1))
        stack = jnp.concatenate(rows + [blank], axis=0)
        grad = dot_nt(fs_ref[...], stack) * scale
        grad_ref[2 * ky] = grad[:, 0:COLS]
        grad_ref[2 * ky + 1] = grad[:, COLS : 2 * COLS]
    chunk = 5
    peers = C // chunk
    for ii in range(chunk):
        for half in range(6):
            pack_ref[pl.ds(half * chunk + ii, peers, stride=32), :] = grad_ref[
                half, pl.ds(ii, peers, stride=chunk), :
            ]
    core = place_ref[3]
    used = lax.broadcasted_iota(jnp.int32, (32, COLS), 0) < 6 * chunk
    for x in range(4):
        for d in range(8):
            lo = (x * 8 + d) * 32
            mine = pl.multiple_of((d * 8 + 2 * x + core) * 32, 32)
            keep_ref[lo : lo + 32, :] = jnp.where(used, pack_ref[pl.ds(mine, 32), :], 0.0)
            his = pl.multiple_of((d * 8 + 2 * x + 1 - core) * 32, 32)
            tile = jnp.where(used, pack_ref[pl.ds(his, 32), :], 0.0)
            send_ref[lo : lo + 32, :] = tile.astype(BF16)
    head = head_ref[...] * scale
    both_ref[...] = head
    send_ref[1024:1072, :] = head.astype(BF16)


def core_kernel(x_ref, keep_ref, both_ref, got_ref, own_ref, s1, s2, s3):
    x = x_ref[4]
    head = both_ref[...] + got_ref[1024:1072, :].astype(F32)
    for k, ref in enumerate((own_ref, s1, s2, s3)):
        lo = pl.multiple_of(lax.rem(x + k, 4) * 256, 256)
        block = keep_ref[pl.ds(lo, 256), :] + got_ref[pl.ds(lo, 256), :].astype(F32)
        ref[0:256, :] = block.astype(ref.dtype)
        ref[256:304, :] = head.astype(ref.dtype)


def cross_kernel(own_ref, r1, r2, r3, out_ref):
    def total(lo, hi):
        return (own_ref[lo:hi, :] + r1[lo:hi, :].astype(F32)) + (
            r2[lo:hi, :].astype(F32) + r3[lo:hi, :].astype(F32)
        )

    head = total(256, 304).astype(BF16)
    for d in range(8):
        out_ref[d, 0:32, :] = total(32 * d, 32 * d + 32).astype(BF16)
        out_ref[d, 32:80, :] = head


def sum_kernel(got_ref, one_ref, two_ref):
    total = got_ref[0].astype(F32)
    for d in range(1, got_ref.shape[0]):
        total = total + got_ref[d].astype(F32)
    chunk = 5
    for tap in range(9):
        two_ref[tap] = total[32 + 4 * tap : 36 + 4 * tap, 0:CH]
    for ky in range(3):
        lo = 2 * ky * chunk
        wide = jnp.concatenate(
            [total[lo : lo + chunk], total[lo + chunk : lo + 2 * chunk]], axis=1
        )
        for kx in range(3):
            one_ref[3 * ky + kx] = wide[:, kx * CH : (kx + 1) * CH]


def ring(axis, step):
    count = lax.axis_size(axis)
    return [(i, (i + step) % count) for i in range(count)]


def line(axis, step):
    count = lax.axis_size(axis)
    return [(i, i + step) for i in range(count) if 0 <= i + step < count]


def body(
    feat_policy,
    feat_ref,
    noise,
    w1_policy,
    w1_ref,
    b1_policy,
    b1_ref,
    gn_gain_policy,
    gn_bias_policy,
    gn_gain_ref,
    gn_bias_ref,
    w2_policy,
    w2_ref,
    time_table,
    timestep,
    winner,
):
    space = lax.axis_size("space")
    s_index = lax.axis_index("space").astype(jnp.int32)
    is_top = (s_index == 0).astype(jnp.int32)
    is_bottom = (s_index == space - 1).astype(jnp.int32)
    place = jnp.stack(
        [
            winner[0].astype(jnp.int32),
            is_top,
            is_bottom,
            s_index & 1,
            s_index >> 1,
            lax.axis_index("tensor").astype(jnp.int32),
            timestep[0].astype(jnp.int32),
        ]
    )

    def gather(own):
        left = lax.ppermute(own, "tensor", ring("tensor", 1))
        right = lax.ppermute(own, "tensor", ring("tensor", -1))
        return own, left, right

    def relay(own, left, right):
        far_a = lax.ppermute(left[0], "tensor", ring("tensor", 1))
        far_b = lax.ppermute(right[1], "tensor", ring("tensor", -1))
        return own, left, far_a, far_b, right

    own_p = feat_policy[0].transpose(0, 2, 1, 3)
    feat_ref, own_p = lax.optimization_barrier((feat_ref, own_p))
    own_r = feat_ref[0].transpose(0, 2, 1, 3)
    parts_p = relay(*gather(own_p))
    parts_r = relay(*gather(own_r))

    vectors = [b1_policy, b1_ref, gn_gain_policy, gn_bias_policy, gn_gain_ref, gn_bias_ref]
    columns, lift, drop, noise_rows = call(
        prep_kernel,
        [place, *[v[None, :] for v in vectors], w2_policy, w2_ref, time_table.T, noise[0]],
        [
            arr((2 * CH, COLS), F32),
            arr((2, 2, 72, CH), BF16),
            arr((2 * CH, 72), BF16),
            arr((ROWS, 8, COLS), F32),
        ],
        "prep",
        10**6,
        smem=1,
    )

    conv_flops = 2 * 9 * C * CH * 2 * PIX
    wide = arr((2 * CH, PIX), F32)
    thin = arr((2 * CH, COLS), F32)

    pre_p, up_p, dn_p, side_l, side_r, feats = call(
        functools.partial(conv_kernel, False),
        [place, *parts_p, w1_policy.reshape(9 * CH, C), columns],
        [wide, thin, thin, arr((960, COLS), BF16), arr((960, COLS), BF16), arr((C, 2 * PIX), BF16)],
        "conv_p",
        conv_flops,
        smem=1,
    )
    pre_r, up_r, dn_r, to_left, to_right = call(
        functools.partial(conv_kernel, True),
        [place, *parts_r, w1_ref.reshape(9 * CH, C), columns, side_l, side_r, noise_rows],
        [wide, thin, thin, arr((1632, COLS), BF16), arr((1632, COLS), BF16)],
        "conv_r",
        conv_flops,
        smem=1,
        scratch=[pltpu.VMEM((C, 2 * PIX), BF16)],
    )
    left = lax.ppermute(to_right, "space", line("space", 1))
    right = lax.ppermute(to_left, "space", line("space", -1))

    ext_p, ext_r, noise_ext, sums = call(
        stat_kernel,
        [pre_p, up_p, dn_p, pre_r, up_r, dn_r, left, right, noise_rows],
        [
            arr((2 * CH, 10 * COLS), F32),
            arr((2 * CH, 6 * COLS), F32),
            arr((8, 8, COLS), F32),
            arr((space, 16, COLS), F32),
        ],
        "stats",
        10**6,
    )
    sums = lax.all_to_all(sums, "space", 0, 0, tiled=True)
    part, hidden, stat = call(
        hidden_kernel,
        [place, ext_p, ext_r, sums, columns, lift],
        [arr((12, 8, COLS), F32), arr((2 * CH, PIX), BF16), thin],
        "hidden",
        10**7,
        smem=1,
    )
    others = [lax.ppermute(part, "tensor", ring("tensor", k)) for k in (1, 2, 3)]
    gnorm, head, partial = call(
        back_kernel,
        [place, part, *others, noise_ext, ext_p, stat, columns, hidden, drop],
        [arr((2 * CH, 6 * COLS), F32), arr((48, COLS), F32), arr((space, 24, COLS), F32)],
        "back",
        10**7,
        smem=1,
    )
    partial = lax.all_to_all(partial, "space", 0, 0, tiled=True)
    keep, send, both, logits = call(
        weight_kernel,
        [place, gnorm, ext_p, stat, partial, feats, head],
        [arr((1024, COLS), F32), arr((1072, COLS), BF16), arr((48, COLS), F32), arr((1, 1), F32)],
        "weight",
        conv_flops,
        smem=1,
        scratch=[pltpu.VMEM((6, C, COLS), F32), pltpu.VMEM((64 * 32, COLS), F32)],
    )
    got = lax.ppermute(send, "space", [(i, i ^ 1) for i in range(space)])
    own, s1, s2, s3 = call(
        core_kernel,
        [place, keep, both, got],
        [arr((304, COLS), F32)] + [arr((304, COLS), BF16)] * 3,
        "core",
        10**6,
        smem=1,
    )
    back = [
        lax.ppermute(sent, "space", ring("space", 2 * k)) for k, sent in ((1, s1), (2, s2), (3, s3))
    ]
    (packed,) = call(cross_kernel, [own, *back], [arr((8, 80, COLS), BF16)], "cross", 10**6)
    packed = lax.all_to_all(packed, "dp", 0, 0, tiled=True)
    grad_one, grad_two = call(
        sum_kernel, [packed], [arr((9, 5, CH), F32), arr((9, 4, CH), F32)], "total", 10**6
    )
    return (logits.reshape(1), grad_one.transpose(0, 2, 1), grad_two)


def solution(mesh):
    in_specs = (
        P("dp", None, "tensor", "space", None),
        P("dp", None, "tensor", "space", None),
        P("dp", None, None, "space", None),
        P(None, "tensor", None),
        P(None, "tensor", None),
        P("tensor"),
        P("tensor"),
        P("tensor"),
        P("tensor"),
        P("tensor"),
        P("tensor"),
        P(None, None, "tensor"),
        P(None, None, "tensor"),
        P(None, "tensor"),
        P("dp"),
        P("dp"),
    )
    out_specs = (P("dp"), P(None, "tensor", ("dp", "space")), P(None, None, "tensor"))
    return jax.shard_map(body, mesh=mesh, in_specs=in_specs, out_specs=out_specs, check_vma=False)
```

```python
import functools

import jax
import jax.numpy as jnp
from jax import lax
from jax.experimental import pallas as pl
from jax.experimental.pallas import tpu as pltpu
from jax.sharding import PartitionSpec as P

C = 320
GROUPS = 32
BETA = 500.0
EPS = 1e-05
CH = 80
ROWS = 4
COLS = 128
PIX = ROWS * COLS
GSIZE = C // GROUPS
LOCAL_GROUPS = CH // GSIZE
COUNT = float(GSIZE * 32 * 128)
CELLS = float(4 * 32 * 128)
F32 = jnp.float32
BF16 = jnp.bfloat16
HIGHEST = lax.Precision.HIGHEST

VM = pl.BlockSpec(memory_space=pltpu.VMEM)
SM = pl.BlockSpec(memory_space=pltpu.SMEM)


def call(kernel, ins, outs, name, flops, smem=0, scratch=()):
    in_bytes = sum(a.size * a.dtype.itemsize for a in ins)
    out_bytes = sum(s.size * s.dtype.itemsize for s in outs)
    return pl.pallas_call(
        kernel,
        out_shape=outs,
        in_specs=[SM] * smem + [VM] * (len(ins) - smem),
        out_specs=[VM] * len(outs),
        scratch_shapes=list(scratch),
        name=name,
        cost_estimate=pl.CostEstimate(
            flops=flops, bytes_accessed=in_bytes + out_bytes, transcendentals=0
        ),
        compiler_params=pltpu.CompilerParams(vmem_limit_bytes=12 * 1024 * 1024),
    )(*ins)


def arr(shape, dtype):
    return jax.ShapeDtypeStruct(shape, dtype)


def dot(a, b):
    return lax.dot_general(a, b, (((1,), (0,)), ((), ())), preferred_element_type=F32)


def dot_nt(a, b):
    return lax.dot_general(a, b, (((1,), (1,)), ((), ())), preferred_element_type=F32)


def exact_dot(a, b):
    return lax.dot_general(
        a, b, (((1,), (0,)), ((), ())), preferred_element_type=F32, precision=HIGHEST
    )


def from_left(tile):
    lane = lax.broadcasted_iota(jnp.int32, tile.shape, tile.ndim - 1)
    return jnp.where(lane == 0, 0.0, pltpu.roll(tile, 1, tile.ndim - 1))


def from_right(tile):
    lane = lax.broadcasted_iota(jnp.int32, tile.shape, tile.ndim - 1)
    return jnp.where(lane == COLS - 1, 0.0, pltpu.roll(tile, COLS - 1, tile.ndim - 1))


def row_of(tile, r):
    return tile[:, r * COLS : (r + 1) * COLS]


def members():
    group = lax.broadcasted_iota(jnp.int32, (2 * LOCAL_GROUPS, 2 * CH), 0)
    chan = lax.broadcasted_iota(jnp.int32, (2 * LOCAL_GROUPS, 2 * CH), 1)
    low = group * GSIZE
    return jnp.where((chan >= low) & (chan < low + GSIZE), 1.0, 0.0).astype(F32)


def spread(stat):
    chan = lax.broadcasted_iota(jnp.int32, (2 * CH, 2 * LOCAL_GROUPS), 0)
    group = lax.broadcasted_iota(jnp.int32, (2 * CH, 2 * LOCAL_GROUPS), 1)
    low = group * GSIZE
    pick = jnp.where((chan >= low) & (chan < low + GSIZE), 1.0, 0.0).astype(F32)
    return exact_dot(pick, stat)


def in_lanes(columns):
    rows = columns[0].shape[0]
    lane = lax.broadcasted_iota(jnp.int32, (rows, COLS), 1)
    out = jnp.zeros((rows, COLS), F32)
    for index, column in enumerate(columns):
        out = jnp.where(lane == index, column, out)
    return out


def prep_kernel(
    place_ref, b_p, b_r, gain_p, off_p, gain_r, off_r, w2_p, w2_r, table_ref, noise_ref,
    col_ref, lift_ref, drop_ref, rows_ref
):
    lane = lax.broadcasted_iota(jnp.int32, table_ref.shape, 1)
    shift = jnp.sum(
        jnp.where(lane == place_ref[6], table_ref[...], 0.0), axis=1, keepdims=True
    )
    eye = lax.broadcasted_iota(jnp.int32, (CH, CH), 0) == lax.broadcasted_iota(
        jnp.int32, (CH, CH), 1
    )

    def upright(ref):
        return jnp.sum(jnp.where(eye, ref[...], 0.0), axis=1, keepdims=True)

    block = in_lanes(
        [
            upright(gain_p),
            upright(off_p),
            upright(gain_r),
            upright(off_r),
            upright(b_p) + shift,
            upright(b_r) + shift,
        ]
    )
    col_ref[0:CH, :] = block
    col_ref[CH : 2 * CH, :] = block
    one = jnp.where(eye, 1.0, 0.0).astype(BF16)
    zero = jnp.zeros((4, CH), F32)
    for m, ref in enumerate((w2_p, w2_r)):
        for im in range(2):
            pieces = []
            for tap in range(9):
                rows = ref[tap].astype(F32)
                pieces += [rows, zero] if im == 0 else [zero, rows]
            padded = jnp.concatenate(pieces, axis=0).astype(BF16)
            lift_ref[m, im] = padded
            if m == 0:
                drop_ref[im * CH : (im + 1) * CH, :] = dot_nt(one, padded).astype(BF16)
    for im in range(2):
        for o in range(4):
            slot = im * 4 + o
            for r in range(ROWS):
                rows_ref[r, slot : slot + 1, :] = noise_ref[im, o, r : r + 1, :]


def conv_kernel(last, t_ref, f0, f1, f2, f3, w_ref, col_ref, *refs):
    if last:
        side_a, side_b, noise_ref, pre_ref, up_ref, dn_ref, send_a, send_b, fs_ref = refs
    else:
        pre_ref, up_ref, dn_ref, send_a, send_b, fs_ref = refs
    t = t_ref[5]
    bias = 5 if last else 4
    for k in range(4):
        base = pl.multiple_of(lax.rem(t - k + 4, 4) * CH, 16)
        for im in range(2):
            for r in range(ROWS):
                lo = im * PIX + r * COLS
                fs_ref[pl.ds(base, CH), lo : lo + COLS] = (f0, f1, f2, f3)[k][im, r]
    odd = t_ref[3] > 0
    if last:
        send_a[0:960, :] = side_a[...]
        send_b[0:960, :] = side_b[...]
        for index in range(2):
            first, second = noise_ref[index], noise_ref[2 + index]
            for ref, value in (
                (send_a, jnp.where(odd, first, second)),
                (send_b, jnp.where(odd, second, first)),
            ):
                high = value.astype(BF16).astype(F32)
                both = jnp.concatenate([high, value - high], axis=0).astype(BF16)
                ref[1600 + 16 * index : 1616 + 16 * index, :] = both
        start, count = 960, 2
    else:
        start, count = 0, 4
    for im in range(2):
        feats = fs_ref[:, im * PIX : (im + 1) * PIX]
        taps = [dot(w_ref[ky * 3 * CH : (ky + 1) * 3 * CH, :], feats) for ky in range(3)]
        chans = slice(im * CH, (im + 1) * CH)
        outs = []
        for r in range(-1, ROWS + 1):
            total = None
            for ky in range(3):
                src = r + ky - 1
                if 0 <= src < ROWS:
                    term = row_of(taps[ky], src)
                    total = term if total is None else total + term
            out = (
                total[CH : 2 * CH]
                + from_left(total[0:CH])
                + from_right(total[2 * CH : 3 * CH])
            )
            if r == -1:
                up_ref[chans, :] = out
            elif r == ROWS:
                dn_ref[chans, :] = out
            else:
                out = out + col_ref[chans, bias : bias + 1]
                pre_ref[chans, r * COLS : (r + 1) * COLS] = out
            outs.append(out)
        for index in range(count):
            upper, lower = outs[index], outs[ROWS + 2 - count + index]
            for ref, value in (
                (send_a, jnp.where(odd, upper, lower)),
                (send_b, jnp.where(odd, lower, upper)),
            ):
                high = value.astype(BF16)
                lo = start + index * 2 * CH + im * CH
                ref[lo : lo + CH, :] = high
                ref_low = start + (count + index) * 2 * CH + im * CH
                if count == 2:
                    ref[ref_low : ref_low + CH, :] = (value - high.astype(F32)).astype(BF16)
        if count == 4:
            for index in range(2):
                upper, lower = outs[index], outs[ROWS + index]
                for ref, value in (
                    (send_a, jnp.where(odd, upper, lower)),
                    (send_b, jnp.where(odd, lower, upper)),
                ):
                    rest = value - value.astype(BF16).astype(F32)
                    lo = start + (count + index) * 2 * CH + im * CH
                    ref[lo : lo + CH, :] = rest.astype(BF16)


def stat_kernel(
    place_ref, pre_p, up_p, dn_p, pre_r, up_r, dn_r, got_a, got_b, noise_ref,
    ext_p, ext_r, noise_ext, out_ref
):
    odd = place_ref[3] > 0
    top = place_ref[1] > 0
    bottom = place_ref[2] > 0
    left, right = (got_a, got_b), (got_b, got_a)

    def rows_at(side, lo, hi):
        return jnp.where(odd, side[0][lo:hi, :].astype(F32), side[1][lo:hi, :].astype(F32))

    def got(side, index):
        return rows_at(side, index * 2 * CH, (index + 1) * 2 * CH)

    def near(ref, index, low):
        return got(ref, index) + got(ref, low)

    columns = []
    for pre, up, dn, ext, first, halo in (
        (pre_p, up_p, dn_p, ext_p, 0, 3),
        (pre_r, up_r, dn_r, ext_r, 6, 1),
    ):
        low = first + halo + 1
        rows = [pre[:, r * COLS : (r + 1) * COLS] for r in range(ROWS)]
        rows[0] = rows[0] + jnp.where(top, 0.0, near(left, first + halo, low + 1))
        rows[ROWS - 1] = rows[ROWS - 1] + jnp.where(bottom, 0.0, near(right, first, low))
        total = rows[0] + rows[1] + rows[2] + rows[3]
        square = (
            rows[0] * rows[0] + rows[1] * rows[1] + rows[2] * rows[2] + rows[3] * rows[3]
        )
        before = [got(left, first + index) for index in range(halo)]
        before[-1] = near(left, first + halo - 1, low) + up[...]
        after = [got(right, first + 1 + index) for index in range(halo)]
        after[0] = near(right, first + 1, low + 1) + dn[...]
        for index, row in enumerate(before + rows + after):
            ext[:, index * COLS : (index + 1) * COLS] = row
        columns.append(jnp.sum(total, axis=1, keepdims=True))
        columns.append(jnp.sum(square, axis=1, keepdims=True))
    for index in range(2):
        lo = 1600 + 16 * index
        pair = rows_at(left, lo, lo + 16)
        noise_ext[index] = pair[0:8] + pair[8:16]
        pair = rows_at(right, lo, lo + 16)
        noise_ext[ROWS + 2 + index] = pair[0:8] + pair[8:16]
    for r in range(ROWS):
        noise_ext[2 + r] = noise_ref[r]
    sums = exact_dot(members(), in_lanes(columns))
    for peer in range(out_ref.shape[0]):
        out_ref[peer] = sums


def moments(total):
    wide = spread(total / COUNT)
    result = []
    for m in range(2):
        mean = wide[:, 2 * m : 2 * m + 1]
        square = wide[:, 2 * m + 1 : 2 * m + 2]
        result.append((mean, lax.rsqrt(square - mean * mean + EPS)))
    return result


def hidden_kernel(
    edge_ref, ext_p, ext_r, sums_ref, col_ref, lift_ref, part_ref, hid_ref, stat_ref
):
    stats = moments(jnp.sum(sums_ref[...], axis=0))
    stat_ref[...] = in_lanes([stats[0][0], stats[0][1]])
    for m, (ext, halo, start) in enumerate(((ext_p, 3, 0), (ext_r, 1, 8))):
        mean, inv = stats[m]
        gain = col_ref[:, 2 * m : 2 * m + 1]
        shift = col_ref[:, 2 * m + 1 : 2 * m + 2]
        pieces = []
        for index in range(ROWS + 2 * halo):
            value = ext[:, index * COLS : (index + 1) * COLS]
            normed = ((value - mean) * inv) * gain + shift
            hidden = normed * jax.nn.sigmoid(normed)
            if index < halo:
                hidden = jnp.where(edge_ref[1] > 0, 0.0, hidden)
            if index >= ROWS + halo:
                hidden = jnp.where(edge_ref[2] > 0, 0.0, hidden)
            hidden = hidden.astype(BF16)
            if m == 0 and halo <= index < halo + ROWS:
                hid_ref[:, (index - halo) * COLS : (index - halo + 1) * COLS] = hidden
            pieces.append(hidden)
        joined = jnp.concatenate(pieces, axis=1)
        taps = dot(lift_ref[m, 0], joined[0:CH]) + dot(lift_ref[m, 1], joined[CH : 2 * CH])
        for index in range(ROWS + 2 * halo - 2):
            totals = [None, None, None]
            for kx in range(3):
                for ky in range(3):
                    tap = 3 * ky + kx
                    lo = (index + ky) * COLS
                    term = taps[8 * tap : 8 * tap + 8, lo : lo + COLS]
                    totals[kx] = term if totals[kx] is None else totals[kx] + term
            part_ref[start + index] = (
                totals[1] + from_left(totals[0]) + from_right(totals[2])
            )


def back_kernel(
    edge_ref, p0, p1, p2, p3, noise_ext, ext_p, stat_ref, col_ref, hid_ref, drop_ref,
    gnorm_ref, head_ref, out_ref
):
    def pred(index):
        return (p0[index] + p1[index]) + (p2[index] + p3[index])

    residual = [pred(index) - noise_ext[index] for index in range(ROWS + 4)]
    frozen = [pred(8 + r) - noise_ext[2 + r] for r in range(ROWS)]
    errors = []
    for rows in (residual[2 : 2 + ROWS], frozen):
        square = rows[0] * rows[0]
        for row in rows[1:]:
            square = square + row * row
        errors.append(jnp.sum(square, axis=1, keepdims=True))
    image = lax.broadcasted_iota(jnp.int32, (8, COLS), 0)
    residual = [jnp.where(image < 4, row, -row) for row in residual]
    for index in range(2):
        residual[index] = jnp.where(edge_ref[1] > 0, 0.0, residual[index])
        residual[ROWS + 2 + index] = jnp.where(edge_ref[2] > 0, 0.0, residual[ROWS + 2 + index])
    moved = [
        [from_right(row) for row in residual],
        residual,
        [from_left(row) for row in residual],
    ]
    blocks = []
    for ky in range(3):
        for kx in range(3):
            blocks.append(
                jnp.concatenate([moved[kx][r + 2 - ky] for r in range(ROWS + 2)], axis=1)
            )
    cot = jnp.concatenate(blocks, axis=0).astype(BF16)
    dhidden = dot(drop_ref[...], cot)
    mean = stat_ref[:, 0:1]
    inv = stat_ref[:, 1:2]
    gain = col_ref[:, 0:1]
    shift = col_ref[:, 1:2]
    first = None
    second = None
    for index in range(ROWS + 2):
        lanes = slice(index * COLS, (index + 1) * COLS)
        centered = (ext_p[:, (index + 2) * COLS : (index + 3) * COLS] - mean) * inv
        normed = centered * gain + shift
        gate = jax.nn.sigmoid(normed)
        gnorm = dhidden[:, lanes] * gate * (1.0 + normed * (1.0 - gate)) * gain
        gnorm_ref[:, lanes] = gnorm
        if 1 <= index <= ROWS:
            first = gnorm if first is None else first + gnorm
            extra = gnorm * centered
            second = extra if second is None else second + extra
    first = jnp.sum(first, axis=1, keepdims=True)
    second = jnp.sum(second, axis=1, keepdims=True)
    sums = exact_dot(members(), in_lanes([first, second]))
    mine = cot[:, COLS : (ROWS + 1) * COLS]
    grads = [dot_nt(mine, hid_ref[im * CH : (im + 1) * CH, :]) for im in range(2)]
    error = in_lanes(errors)
    head_ref[...] = jnp.zeros(head_ref.shape, F32)
    for tap in range(9):
        head = grads[0][8 * tap : 8 * tap + 4] + grads[1][8 * tap + 4 : 8 * tap + 8]
        if tap < 6:
            head_ref[4 * tap : 4 * tap + 4, 0:CH] = head
        else:
            lo = 4 * tap - 24
            head_ref[lo : lo + 4, CH:COLS] = head[:, 0 : COLS - CH]
            head_ref[lo + 12 : lo + 16, CH : 3 * CH - COLS] = head[:, COLS - CH : CH]
    for peer in range(out_ref.shape[0]):
        out_ref[peer, 0:16, :] = sums
        out_ref[peer, 16:24, :] = error


def weight_kernel(
    place_ref, gnorm_ref, ext_p, stat_ref, red_ref, fs_ref, head_ref,
    keep_ref, send_ref, both_ref, logit_ref, grad_ref, pack_ref
):
    total = jnp.sum(red_ref[...], axis=0)
    row = lax.broadcasted_iota(jnp.int32, (8, COLS), 0)
    signed = jnp.where(row < 4, total[16:24], -total[16:24])
    gaps = jnp.sum(signed, axis=0, keepdims=True)
    gap = (gaps[:, 0:1] - gaps[:, 1:2]) * (1.0 / CELLS)
    sign = 1.0 - 2.0 * place_ref[0].astype(F32)
    logit = (-0.5 * BETA) * sign * gap
    logit_ref[...] = logit
    scale = (BETA / CELLS) * sign * jax.nn.sigmoid(-logit)
    wide = spread(total[0:16] / COUNT)
    mean = stat_ref[:, 0:1]
    inv = stat_ref[:, 1:2]
    parts = []
    for index in range(ROWS + 2):
        centered = (ext_p[:, (index + 2) * COLS : (index + 3) * COLS] - mean) * inv
        gnorm = gnorm_ref[:, index * COLS : (index + 1) * COLS]
        delta = inv * (gnorm - wide[:, 0:1] - centered * wide[:, 1:2])
        if index == 0:
            delta = jnp.where(place_ref[1] > 0, 0.0, delta)
        if index == ROWS + 1:
            delta = jnp.where(place_ref[2] > 0, 0.0, delta)
        parts.append(
            [from_right(delta).astype(BF16), delta.astype(BF16), from_left(delta).astype(BF16)]
        )
    blank = jnp.zeros((16, 2 * PIX), BF16)
    for ky in range(3):
        rows = []
        for kx in range(3):
            tiles = []
            for im in range(2):
                for r in range(ROWS):
                    tiles.append(parts[r + 2 - ky][kx][im * CH : (im + 1) * CH])
            rows.append(jnp.concatenate(tiles, axis=1))
        stack = jnp.concatenate(rows + [blank], axis=0)
        grad = dot_nt(fs_ref[...], stack) * scale
        grad_ref[2 * ky] = grad[:, 0:COLS]
        grad_ref[2 * ky + 1] = grad[:, COLS : 2 * COLS]
    chunk = 5
    core = place_ref[3]
    for ref, who in ((keep_ref, core), (pack_ref, 1 - core)):
        for x in range(4):
            for ii in range(chunk):
                for half in range(6):
                    ref[pl.ds(x * 256 + half * chunk + ii, 8, stride=32), :] = grad_ref[
                        half, pl.ds(who * chunk + 2 * chunk * x + ii, 8, stride=8 * chunk), :
                    ]
            for spare in (30, 31):
                ref[pl.ds(x * 256 + spare, 8, stride=32), :] = jnp.zeros((8, COLS), F32)
    send_ref[0:1024, :] = pack_ref[...].astype(BF16)
    head = head_ref[...] * scale
    both_ref[...] = head
    send_ref[1024:1056, :] = head.astype(BF16)


def core_kernel(x_ref, keep_ref, both_ref, got_ref, own_ref, s1, s2, s3):
    x = x_ref[4]
    head = both_ref[...] + got_ref[1024:1056, :].astype(F32)
    for k, ref in enumerate((own_ref, s1, s2, s3)):
        lo = pl.multiple_of(lax.rem(x + k, 4) * 256, 256)
        block = keep_ref[pl.ds(lo, 256), :] + got_ref[pl.ds(lo, 256), :].astype(F32)
        ref[0:256, :] = block.astype(ref.dtype)
        ref[256:288, :] = head.astype(ref.dtype)


def cross_kernel(own_ref, r1, r2, r3, out_ref):
    def total(lo, hi):
        return (own_ref[lo:hi, :] + r1[lo:hi, :].astype(F32)) + (
            r2[lo:hi, :].astype(F32) + r3[lo:hi, :].astype(F32)
        )

    head = total(256, 288).astype(BF16)
    for d in range(8):
        out_ref[d, 0:32, :] = total(32 * d, 32 * d + 32).astype(BF16)
        out_ref[d, 32:56, :] = head[0:24]


def sum_kernel(got_ref, one_ref, two_ref):
    total = got_ref[0].astype(F32)
    for d in range(1, got_ref.shape[0]):
        total = total + got_ref[d].astype(F32)
    chunk = 5
    for tap in range(6):
        two_ref[tap] = total[32 + 4 * tap : 36 + 4 * tap, 0:CH]
    for tap in range(6, 9):
        lo = 8 + 4 * tap
        two_ref[tap] = jnp.concatenate(
            [total[lo : lo + 4, CH:COLS], total[lo + 12 : lo + 16, CH : 3 * CH - COLS]], axis=1
        )
    for ky in range(3):
        lo = 2 * ky * chunk
        wide = jnp.concatenate(
            [total[lo : lo + chunk], total[lo + chunk : lo + 2 * chunk]], axis=1
        )
        for kx in range(3):
            one_ref[3 * ky + kx] = wide[:, kx * CH : (kx + 1) * CH]


def ring(axis, step):
    count = lax.axis_size(axis)
    return [(i, (i + step) % count) for i in range(count)]


def body(
    feat_policy,
    feat_ref,
    noise,
    w1_policy,
    w1_ref,
    b1_policy,
    b1_ref,
    gn_gain_policy,
    gn_bias_policy,
    gn_gain_ref,
    gn_bias_ref,
    w2_policy,
    w2_ref,
    time_table,
    timestep,
    winner,
):
    space = lax.axis_size("space")
    s_index = lax.axis_index("space").astype(jnp.int32)
    is_top = (s_index == 0).astype(jnp.int32)
    is_bottom = (s_index == space - 1).astype(jnp.int32)
    place = jnp.stack(
        [
            winner[0].astype(jnp.int32),
            is_top,
            is_bottom,
            s_index & 1,
            s_index >> 1,
            lax.axis_index("tensor").astype(jnp.int32),
            timestep[0].astype(jnp.int32),
        ]
    )

    def gather(own):
        return [own] + [lax.ppermute(own, "tensor", ring("tensor", k)) for k in (1, 2, 3)]

    own_p = feat_policy[0].transpose(0, 2, 1, 3)
    feat_ref, own_p = lax.optimization_barrier((feat_ref, own_p))
    own_r = feat_ref[0].transpose(0, 2, 1, 3)
    parts_p = gather(own_p)
    parts_r = gather(own_r)

    vectors = [b1_policy, b1_ref, gn_gain_policy, gn_bias_policy, gn_gain_ref, gn_bias_ref]
    columns, lift, drop, noise_rows = call(
        prep_kernel,
        [place, *[v[None, :] for v in vectors], w2_policy, w2_ref, time_table.T, noise[0]],
        [
            arr((2 * CH, COLS), F32),
            arr((2, 2, 72, CH), BF16),
            arr((2 * CH, 72), BF16),
            arr((ROWS, 8, COLS), F32),
        ],
        "prep",
        10**6,
        smem=1,
    )

    conv_flops = 2 * 9 * C * CH * 2 * PIX
    wide = arr((2 * CH, PIX), F32)
    thin = arr((2 * CH, COLS), F32)

    pre_p, up_p, dn_p, side_a, side_b, feats = call(
        functools.partial(conv_kernel, False),
        [place, *parts_p, w1_policy.reshape(9 * CH, C), columns],
        [wide, thin, thin, arr((960, COLS), BF16), arr((960, COLS), BF16), arr((C, 2 * PIX), BF16)],
        "conv_p",
        conv_flops,
        smem=1,
    )
    pre_r, up_r, dn_r, to_a, to_b = call(
        functools.partial(conv_kernel, True),
        [place, *parts_r, w1_ref.reshape(9 * CH, C), columns, side_a, side_b, noise_rows],
        [wide, thin, thin, arr((1632, COLS), BF16), arr((1632, COLS), BF16)],
        "conv_r",
        conv_flops,
        smem=1,
        scratch=[pltpu.VMEM((C, 2 * PIX), BF16)],
    )
    partner = [(i, i ^ 1) for i in range(space)]
    across = [(i, (i + 1 if i % 2 else i - 1) % space) for i in range(space)]
    got_b = lax.ppermute(to_b, "space", across)
    got_a = lax.ppermute(to_a, "space", partner)

    ext_p, ext_r, noise_ext, sums = call(
        stat_kernel,
        [place, pre_p, up_p, dn_p, pre_r, up_r, dn_r, got_a, got_b, noise_rows],
        [
            arr((2 * CH, 10 * COLS), F32),
            arr((2 * CH, 6 * COLS), F32),
            arr((8, 8, COLS), F32),
            arr((space, 16, COLS), F32),
        ],
        "stats",
        10**6,
        smem=1,
    )
    sums = lax.all_to_all(sums, "space", 0, 0, tiled=True)
    part, hidden, stat = call(
        hidden_kernel,
        [place, ext_p, ext_r, sums, columns, lift],
        [arr((12, 8, COLS), F32), arr((2 * CH, PIX), BF16), thin],
        "hidden",
        10**7,
        smem=1,
    )
    others = [lax.ppermute(part, "tensor", ring("tensor", k)) for k in (1, 2, 3)]
    gnorm, head, partial = call(
        back_kernel,
        [place, part, *others, noise_ext, ext_p, stat, columns, hidden, drop],
        [arr((2 * CH, 6 * COLS), F32), arr((32, COLS), F32), arr((space, 24, COLS), F32)],
        "back",
        10**7,
        smem=1,
    )
    partial = lax.all_to_all(partial, "space", 0, 0, tiled=True)
    keep, send, both, logits = call(
        weight_kernel,
        [place, gnorm, ext_p, stat, partial, feats, head],
        [arr((1024, COLS), F32), arr((1056, COLS), BF16), arr((32, COLS), F32), arr((1, 1), F32)],
        "weight",
        conv_flops,
        smem=1,
        scratch=[pltpu.VMEM((6, C, COLS), F32), pltpu.VMEM((1024, COLS), F32)],
    )
    got = lax.ppermute(send, "space", partner)
    own, s1, s2, s3 = call(
        core_kernel,
        [place, keep, both, got],
        [arr((288, COLS), F32)] + [arr((288, COLS), BF16)] * 3,
        "core",
        10**6,
        smem=1,
    )
    back = [
        lax.ppermute(sent, "space", ring("space", 2 * k)) for k, sent in ((1, s1), (2, s2), (3, s3))
    ]
    (packed,) = call(cross_kernel, [own, *back], [arr((8, 56, COLS), BF16)], "cross", 10**6)
    packed = lax.all_to_all(packed, "dp", 0, 0, tiled=True)
    grad_one, grad_two = call(
        sum_kernel, [packed], [arr((9, 5, CH), F32), arr((9, 4, CH), F32)], "total", 10**6
    )
    return (logits.reshape(1), grad_one.transpose(0, 2, 1), grad_two)


def solution(mesh):
    in_specs = (
        P("dp", None, "tensor", "space", None),
        P("dp", None, "tensor", "space", None),
        P("dp", None, None, "space", None),
        P(None, "tensor", None),
        P(None, "tensor", None),
        P("tensor"),
        P("tensor"),
        P("tensor"),
        P("tensor"),
        P("tensor"),
        P("tensor"),
        P(None, None, "tensor"),
        P(None, None, "tensor"),
        P(None, "tensor"),
        P("dp"),
        P("dp"),
    )
    out_specs = (P("dp"), P(None, "tensor", ("dp", "space")), P(None, None, "tensor"))
    return jax.shard_map(body, mesh=mesh, in_specs=in_specs, out_specs=out_specs, check_vma=False)
```

```python
import functools

import jax
import jax.numpy as jnp
from jax import lax
from jax.experimental import pallas as pl
from jax.experimental.pallas import tpu as pltpu
from jax.sharding import PartitionSpec as P

C = 320
GROUPS = 32
BETA = 500.0
EPS = 1e-05
CH = 80
ROWS = 4
COLS = 128
PIX = ROWS * COLS
GSIZE = C // GROUPS
LOCAL_GROUPS = CH // GSIZE
COUNT = float(GSIZE * 32 * 128)
CELLS = float(4 * 32 * 128)
F32 = jnp.float32
BF16 = jnp.bfloat16
HIGHEST = lax.Precision.HIGHEST

VM = pl.BlockSpec(memory_space=pltpu.VMEM)
SM = pl.BlockSpec(memory_space=pltpu.SMEM)


def call(kernel, ins, outs, flops, smem=0, scratch=()):
    in_bytes = sum(a.size * a.dtype.itemsize for a in ins)
    out_bytes = sum(s.size * s.dtype.itemsize for s in outs)
    return pl.pallas_call(
        kernel,
        out_shape=outs,
        in_specs=[SM] * smem + [VM] * (len(ins) - smem),
        out_specs=[VM] * len(outs),
        scratch_shapes=list(scratch),
        cost_estimate=pl.CostEstimate(
            flops=flops, bytes_accessed=in_bytes + out_bytes, transcendentals=0
        ),
        compiler_params=pltpu.CompilerParams(vmem_limit_bytes=12 * 1024 * 1024),
    )(*ins)


def arr(shape, dtype):
    return jax.ShapeDtypeStruct(shape, dtype)


def dot(a, b):
    return lax.dot_general(a, b, (((1,), (0,)), ((), ())), preferred_element_type=F32)


def dot_nt(a, b):
    return lax.dot_general(a, b, (((1,), (1,)), ((), ())), preferred_element_type=F32)


def exact_dot(a, b):
    return lax.dot_general(
        a, b, (((1,), (0,)), ((), ())), preferred_element_type=F32, precision=HIGHEST
    )


def from_left(tile):
    lane = lax.broadcasted_iota(jnp.int32, tile.shape, tile.ndim - 1)
    return jnp.where(lane == 0, 0.0, pltpu.roll(tile, 1, tile.ndim - 1))


def from_right(tile):
    lane = lax.broadcasted_iota(jnp.int32, tile.shape, tile.ndim - 1)
    return jnp.where(lane == COLS - 1, 0.0, pltpu.roll(tile, COLS - 1, tile.ndim - 1))


def row_of(tile, r):
    return tile[:, r * COLS : (r + 1) * COLS]


def sigmoid(value):
    return 0.5 + 0.5 * jnp.tanh(0.5 * value)


def members():
    group = lax.broadcasted_iota(jnp.int32, (2 * LOCAL_GROUPS, 2 * CH), 0)
    chan = lax.broadcasted_iota(jnp.int32, (2 * LOCAL_GROUPS, 2 * CH), 1)
    low = group * GSIZE
    return jnp.where((chan >= low) & (chan < low + GSIZE), 1.0, 0.0).astype(F32)


def spread(stat):
    chan = lax.broadcasted_iota(jnp.int32, (2 * CH, 2 * LOCAL_GROUPS), 0)
    group = lax.broadcasted_iota(jnp.int32, (2 * CH, 2 * LOCAL_GROUPS), 1)
    low = group * GSIZE
    pick = jnp.where((chan >= low) & (chan < low + GSIZE), 1.0, 0.0).astype(F32)
    return exact_dot(pick, stat)


def in_lanes(columns):
    rows = columns[0].shape[0]
    lane = lax.broadcasted_iota(jnp.int32, (rows, COLS), 1)
    out = jnp.zeros((rows, COLS), F32)
    for index, column in enumerate(columns):
        out = jnp.where(lane == index, column, out)
    return out


def prep_kernel(
    place_ref, b_p, b_r, gain_p, off_p, gain_r, off_r, w2_p, w2_r, table_ref, noise_ref, w1_p, w1_r,
    col_ref, lift_ref, drop_ref, rows_ref, w1_p_out, w1_r_out
):
    w1_p_out[...] = w1_p[...]
    w1_r_out[...] = w1_r[...]
    lane = lax.broadcasted_iota(jnp.int32, table_ref.shape, 1)
    shift = jnp.sum(
        jnp.where(lane == place_ref[6], table_ref[...], 0.0), axis=1, keepdims=True
    )
    eye = lax.broadcasted_iota(jnp.int32, (CH, CH), 0) == lax.broadcasted_iota(
        jnp.int32, (CH, CH), 1
    )

    def upright(ref):
        return jnp.sum(jnp.where(eye, ref[...], 0.0), axis=1, keepdims=True)

    block = in_lanes(
        [
            upright(gain_p),
            upright(off_p),
            upright(gain_r),
            upright(off_r),
            upright(b_p) + shift,
            upright(b_r) + shift,
        ]
    )
    col_ref[0:CH, :] = block
    col_ref[CH : 2 * CH, :] = block
    one = jnp.where(eye, 1.0, 0.0).astype(BF16)
    zero = jnp.zeros((4, CH), F32)
    for m, ref in enumerate((w2_p, w2_r)):
        for im in range(2):
            pieces = []
            for tap in range(9):
                rows = ref[tap].astype(F32)
                pieces += [rows, zero] if im == 0 else [zero, rows]
            padded = jnp.concatenate(pieces, axis=0).astype(BF16)
            lift_ref[m, im] = padded
            if m == 0:
                drop_ref[im * CH : (im + 1) * CH, :] = dot_nt(one, padded).astype(BF16)
    for im in range(2):
        for o in range(4):
            slot = im * 4 + o
            for r in range(ROWS):
                rows_ref[r, slot : slot + 1, :] = noise_ref[im, o, r : r + 1, :]


def conv_kernel(last, t_ref, f0, f1, f2, f3, w_ref, col_ref, *refs):
    if last:
        pre_ref, up_ref, dn_ref, send_a, send_b, fs_ref = refs
    else:
        noise_ref, pre_ref, up_ref, dn_ref, send_a, send_b, perm_ref, fs_ref = refs
    t = t_ref[5]
    bias = 5 if last else 4
    for k in range(4):
        base = pl.multiple_of(lax.rem(t - k + 4, 4) * CH, 16)
        for im in range(2):
            for r in range(ROWS):
                lo = im * PIX + r * COLS
                fs_ref[pl.ds(base, CH), lo : lo + COLS] = (f0, f1, f2, f3)[k][im, r]
    odd = t_ref[3] > 0
    count = 2 if last else 4
    if not last:
        for index in range(2):
            first, second = noise_ref[index], noise_ref[2 + index]
            for ref, value in (
                (send_a, jnp.where(odd, first, second)),
                (send_b, jnp.where(odd, second, first)),
            ):
                high = value.astype(BF16).astype(F32)
                both = jnp.concatenate([high, value - high], axis=0).astype(BF16)
                ref[960 + 16 * index : 976 + 16 * index, :] = both
        row = lax.broadcasted_iota(jnp.int32, (C, C), 0)
        chan = lax.broadcasted_iota(jnp.int32, (C, C), 1)
        core, rest = row // 160, row % 160
        want = 40 * (rest % 8) + 10 * (rest // 40) + 5 * core + (rest % 40) // 8
        pick = jnp.where(chan == want, 1.0, 0.0).astype(BF16)
        perm_ref[...] = dot(pick, fs_ref[...]).astype(BF16)
    for im in range(2):
        feats = fs_ref[:, im * PIX : (im + 1) * PIX]
        taps = [dot(w_ref[ky * 3 * CH : (ky + 1) * 3 * CH, :], feats) for ky in range(3)]
        chans = slice(im * CH, (im + 1) * CH)
        outs = []
        for r in range(-1, ROWS + 1):
            total = None
            for ky in range(3):
                src = r + ky - 1
                if 0 <= src < ROWS:
                    term = row_of(taps[ky], src)
                    total = term if total is None else total + term
            out = (
                total[CH : 2 * CH]
                + from_left(total[0:CH])
                + from_right(total[2 * CH : 3 * CH])
            )
            if r == -1:
                up_ref[chans, :] = out
            elif r == ROWS:
                dn_ref[chans, :] = out
            else:
                out = out + col_ref[chans, bias : bias + 1]
                pre_ref[chans, r * COLS : (r + 1) * COLS] = out
            outs.append(out)
        for index in range(count):
            upper, lower = outs[index], outs[ROWS + 2 - count + index]
            for ref, value in (
                (send_a, jnp.where(odd, upper, lower)),
                (send_b, jnp.where(odd, lower, upper)),
            ):
                high = value.astype(BF16)
                lo = index * 2 * CH + im * CH
                ref[lo : lo + CH, :] = high
                ref_low = (count + index) * 2 * CH + im * CH
                if count == 2:
                    ref[ref_low : ref_low + CH, :] = (value - high.astype(F32)).astype(BF16)
        if count == 4:
            for index in range(2):
                upper, lower = outs[index], outs[ROWS + index]
                for ref, value in (
                    (send_a, jnp.where(odd, upper, lower)),
                    (send_b, jnp.where(odd, lower, upper)),
                ):
                    rest = value - value.astype(BF16).astype(F32)
                    lo = (count + index) * 2 * CH + im * CH
                    ref[lo : lo + CH, :] = rest.astype(BF16)


def stat_kernel(
    place_ref, pre_p, up_p, dn_p, pre_r, up_r, dn_r, got_ap, got_bp, got_ar, got_br, noise_ref,
    ext_p, ext_r, noise_ext, out_ref
):
    odd = place_ref[3] > 0
    top = place_ref[1] > 0
    bottom = place_ref[2] > 0

    def rows_at(side, lo, hi):
        return jnp.where(odd, side[0][lo:hi, :].astype(F32), side[1][lo:hi, :].astype(F32))

    def got(side, index):
        return rows_at(side, index * 2 * CH, (index + 1) * 2 * CH)

    def near(ref, index, low):
        return got(ref, index) + got(ref, low)

    columns = []
    first = 0
    for pre, up, dn, ext, got_a, got_b, halo in (
        (pre_p, up_p, dn_p, ext_p, got_ap, got_bp, 3),
        (pre_r, up_r, dn_r, ext_r, got_ar, got_br, 1),
    ):
        left, right = (got_a, got_b), (got_b, got_a)
        low = first + halo + 1
        rows = [pre[:, r * COLS : (r + 1) * COLS] for r in range(ROWS)]
        rows[0] = rows[0] + jnp.where(top, 0.0, near(left, first + halo, low + 1))
        rows[ROWS - 1] = rows[ROWS - 1] + jnp.where(bottom, 0.0, near(right, first, low))
        total = rows[0] + rows[1] + rows[2] + rows[3]
        square = (
            rows[0] * rows[0] + rows[1] * rows[1] + rows[2] * rows[2] + rows[3] * rows[3]
        )
        before = [got(left, first + index) for index in range(halo)]
        before[-1] = near(left, first + halo - 1, low) + up[...]
        after = [got(right, first + 1 + index) for index in range(halo)]
        after[0] = near(right, first + 1, low + 1) + dn[...]
        for index, row in enumerate(before + rows + after):
            ext[:, index * COLS : (index + 1) * COLS] = row
        columns.append(jnp.sum(total, axis=1, keepdims=True))
        columns.append(jnp.sum(square, axis=1, keepdims=True))
    for index in range(2):
        lo = 960 + 16 * index
        left, right = (got_ap, got_bp), (got_bp, got_ap)
        pair = rows_at(left, lo, lo + 16)
        noise_ext[index] = pair[0:8] + pair[8:16]
        pair = rows_at(right, lo, lo + 16)
        noise_ext[ROWS + 2 + index] = pair[0:8] + pair[8:16]
    for r in range(ROWS):
        noise_ext[2 + r] = noise_ref[r]
    sums = exact_dot(members(), in_lanes(columns))
    for peer in range(out_ref.shape[0]):
        out_ref[peer] = sums


def moments(total):
    wide = spread(total / COUNT)
    result = []
    for m in range(2):
        mean = wide[:, 2 * m : 2 * m + 1]
        square = wide[:, 2 * m + 1 : 2 * m + 2]
        result.append((mean, lax.rsqrt(square - mean * mean + EPS)))
    return result


def hidden_kernel(
    edge_ref, ext_p, ext_r, sums_ref, col_ref, lift_ref, part_ref, hid_ref, stat_ref
):
    stats = moments(jnp.sum(sums_ref[...], axis=0))
    stat_ref[...] = in_lanes([stats[0][0], stats[0][1]])
    for m, (ext, halo, start) in enumerate(((ext_p, 3, 0), (ext_r, 1, 8))):
        mean, inv = stats[m]
        gain = col_ref[:, 2 * m : 2 * m + 1]
        shift = col_ref[:, 2 * m + 1 : 2 * m + 2]
        pieces = []
        for index in range(ROWS + 2 * halo):
            value = ext[:, index * COLS : (index + 1) * COLS]
            normed = ((value - mean) * inv) * gain + shift
            hidden = normed * sigmoid(normed)
            if index < halo:
                hidden = jnp.where(edge_ref[1] > 0, 0.0, hidden)
            if index >= ROWS + halo:
                hidden = jnp.where(edge_ref[2] > 0, 0.0, hidden)
            hidden = hidden.astype(BF16)
            if m == 0 and halo <= index < halo + ROWS:
                hid_ref[:, (index - halo) * COLS : (index - halo + 1) * COLS] = hidden
            pieces.append(hidden)
        joined = jnp.concatenate(pieces, axis=1)
        taps = dot(lift_ref[m, 0], joined[0:CH]) + dot(lift_ref[m, 1], joined[CH : 2 * CH])
        for index in range(ROWS + 2 * halo - 2):
            totals = [None, None, None]
            for kx in range(3):
                for ky in range(3):
                    tap = 3 * ky + kx
                    lo = (index + ky) * COLS
                    term = taps[8 * tap : 8 * tap + 8, lo : lo + COLS]
                    totals[kx] = term if totals[kx] is None else totals[kx] + term
            part_ref[start + index] = (
                totals[1] + from_left(totals[0]) + from_right(totals[2])
            )


def back_kernel(
    edge_ref, p0, p1, p2, p3, noise_ext, ext_p, stat_ref, col_ref, hid_ref, drop_ref,
    gnorm_ref, head_ref, out_ref
):
    def pred(index):
        return (p0[index] + p1[index]) + (p2[index] + p3[index])

    residual = [pred(index) - noise_ext[index] for index in range(ROWS + 4)]
    frozen = [pred(8 + r) - noise_ext[2 + r] for r in range(ROWS)]
    errors = []
    for rows in (residual[2 : 2 + ROWS], frozen):
        square = rows[0] * rows[0]
        for row in rows[1:]:
            square = square + row * row
        errors.append(jnp.sum(square, axis=1, keepdims=True))
    image = lax.broadcasted_iota(jnp.int32, (8, COLS), 0)
    residual = [jnp.where(image < 4, row, -row) for row in residual]
    for index in range(2):
        residual[index] = jnp.where(edge_ref[1] > 0, 0.0, residual[index])
        residual[ROWS + 2 + index] = jnp.where(edge_ref[2] > 0, 0.0, residual[ROWS + 2 + index])
    moved = [
        [from_right(row) for row in residual],
        residual,
        [from_left(row) for row in residual],
    ]
    blocks = []
    for ky in range(3):
        for kx in range(3):
            blocks.append(
                jnp.concatenate([moved[kx][r + 2 - ky] for r in range(ROWS + 2)], axis=1)
            )
    cot = jnp.concatenate(blocks, axis=0).astype(BF16)
    dhidden = dot(drop_ref[...], cot)
    mean = stat_ref[:, 0:1]
    inv = stat_ref[:, 1:2]
    gain = col_ref[:, 0:1]
    shift = col_ref[:, 1:2]
    first = None
    second = None
    for index in range(ROWS + 2):
        lanes = slice(index * COLS, (index + 1) * COLS)
        centered = (ext_p[:, (index + 2) * COLS : (index + 3) * COLS] - mean) * inv
        normed = centered * gain + shift
        gate = sigmoid(normed)
        gnorm = dhidden[:, lanes] * gate * (1.0 + normed * (1.0 - gate)) * gain
        gnorm_ref[:, lanes] = gnorm
        if 1 <= index <= ROWS:
            first = gnorm if first is None else first + gnorm
            extra = gnorm * centered
            second = extra if second is None else second + extra
    first = jnp.sum(first, axis=1, keepdims=True)
    second = jnp.sum(second, axis=1, keepdims=True)
    sums = exact_dot(members(), in_lanes([first, second]))
    mine = cot[:, COLS : (ROWS + 1) * COLS]
    grads = [dot_nt(mine, hid_ref[im * CH : (im + 1) * CH, :]) for im in range(2)]
    error = in_lanes(errors)
    head_ref[...] = jnp.zeros(head_ref.shape, F32)
    for tap in range(9):
        head = grads[0][8 * tap : 8 * tap + 4] + grads[1][8 * tap + 4 : 8 * tap + 8]
        if tap < 6:
            head_ref[4 * tap : 4 * tap + 4, 0:CH] = head
        else:
            lo = 4 * tap - 24
            head_ref[lo : lo + 4, CH:COLS] = head[:, 0 : COLS - CH]
            head_ref[lo + 12 : lo + 16, CH : 3 * CH - COLS] = head[:, COLS - CH : CH]
    for peer in range(out_ref.shape[0]):
        out_ref[peer, 0:16, :] = sums
        out_ref[peer, 16:24, :] = error


def weight_kernel(
    place_ref, gnorm_ref, ext_p, stat_ref, red_ref, fs_ref, head_ref,
    keep_ref, send_ref, both_ref, logit_ref, grad_ref
):
    total = jnp.sum(red_ref[...], axis=0)
    row = lax.broadcasted_iota(jnp.int32, (8, COLS), 0)
    signed = jnp.where(row < 4, total[16:24], -total[16:24])
    gaps = jnp.sum(signed, axis=0, keepdims=True)
    gap = (gaps[:, 0:1] - gaps[:, 1:2]) * (1.0 / CELLS)
    sign = 1.0 - 2.0 * place_ref[0].astype(F32)
    logit = (-0.5 * BETA) * sign * gap
    logit_ref[...] = logit
    scale = (BETA / CELLS) * sign * jax.nn.sigmoid(-logit)
    wide = spread(total[0:16] / COUNT)
    mean = stat_ref[:, 0:1]
    inv = stat_ref[:, 1:2]
    parts = []
    for index in range(ROWS + 2):
        centered = (ext_p[:, (index + 2) * COLS : (index + 3) * COLS] - mean) * inv
        gnorm = gnorm_ref[:, index * COLS : (index + 1) * COLS]
        delta = inv * (gnorm - wide[:, 0:1] - centered * wide[:, 1:2])
        if index == 0:
            delta = jnp.where(place_ref[1] > 0, 0.0, delta)
        if index == ROWS + 1:
            delta = jnp.where(place_ref[2] > 0, 0.0, delta)
        parts.append(
            [from_right(delta).astype(BF16), delta.astype(BF16), from_left(delta).astype(BF16)]
        )
    blank = jnp.zeros((16, 2 * PIX), BF16)
    for ky in range(3):
        rows = []
        for kx in range(3):
            tiles = []
            for im in range(2):
                for r in range(ROWS):
                    tiles.append(parts[r + 2 - ky][kx][im * CH : (im + 1) * CH])
            rows.append(jnp.concatenate(tiles, axis=1))
        stack = jnp.concatenate(rows + [blank], axis=0)
        grad = dot_nt(fs_ref[...], stack) * scale
        grad_ref[:, 256 * ky : 256 * ky + 256] = grad
    core = place_ref[3]
    head = head_ref[...] * scale
    both_ref[...] = head
    for x in range(4):
        mine = pl.multiple_of(core * 160 + 40 * x, 8)
        his = pl.multiple_of((1 - core) * 160 + 40 * x, 8)
        keep_ref[x] = grad_ref[pl.ds(mine, 40), :]
        tail = [head[8 * j : 8 * j + 8] for j in range(3)] + [jnp.zeros((8, 3 * COLS), F32)]
        block = jnp.concatenate(
            [grad_ref[pl.ds(his, 40), :], jnp.concatenate(tail, axis=1)], axis=0
        )
        send_ref[x] = block.astype(BF16)


def core_kernel(x_ref, keep_ref, both_ref, got_ref, own_ref, s1, s2, s3):
    x = x_ref[4]
    tail = [both_ref[8 * j : 8 * j + 8, :] for j in range(3)] + [jnp.zeros((8, 3 * COLS), F32)]
    tail = jnp.concatenate(tail, axis=1)
    for k, ref in enumerate((own_ref, s1, s2, s3)):
        where = lax.rem(x + k, 4)
        got = got_ref[where].astype(F32)
        block = jnp.concatenate([keep_ref[where] + got[0:40], tail + got[40:48]], axis=0)
        ref[...] = block.astype(ref.dtype)


def cross_kernel(own_ref, r1, r2, r3, out_ref, pack_ref):
    total = (own_ref[...] + r1[...].astype(F32)) + (r2[...].astype(F32) + r3[...].astype(F32))
    for half in range(6):
        lanes = slice(half * COLS, (half + 1) * COLS)
        for ii in range(5):
            pack_ref[pl.ds(half * 5 + ii, 8, stride=56), :] = total[8 * ii : 8 * ii + 8, lanes]
    for spare in (30, 31):
        pack_ref[pl.ds(spare, 8, stride=56), :] = jnp.zeros((8, COLS), F32)
    for d in range(8):
        for j in range(3):
            pack_ref[56 * d + 32 + 8 * j : 56 * d + 40 + 8 * j, :] = total[
                40:48, j * COLS : (j + 1) * COLS
            ]
        out_ref[d] = pack_ref[56 * d : 56 * d + 56, :].astype(BF16)


def sum_kernel(got_ref, one_ref, two_ref):
    total = got_ref[0].astype(F32)
    for d in range(1, got_ref.shape[0]):
        total = total + got_ref[d].astype(F32)
    chunk = 5
    for tap in range(6):
        two_ref[tap] = total[32 + 4 * tap : 36 + 4 * tap, 0:CH]
    for tap in range(6, 9):
        lo = 8 + 4 * tap
        two_ref[tap] = jnp.concatenate(
            [total[lo : lo + 4, CH:COLS], total[lo + 12 : lo + 16, CH : 3 * CH - COLS]], axis=1
        )
    for ky in range(3):
        lo = 2 * ky * chunk
        wide = jnp.concatenate(
            [total[lo : lo + chunk], total[lo + chunk : lo + 2 * chunk]], axis=1
        )
        for kx in range(3):
            one_ref[3 * ky + kx] = wide[:, kx * CH : (kx + 1) * CH]


def ring(axis, step):
    count = lax.axis_size(axis)
    return [(i, (i + step) % count) for i in range(count)]


def body(
    feat_policy,
    feat_ref,
    noise,
    w1_policy,
    w1_ref,
    b1_policy,
    b1_ref,
    gn_gain_policy,
    gn_bias_policy,
    gn_gain_ref,
    gn_bias_ref,
    w2_policy,
    w2_ref,
    time_table,
    timestep,
    winner,
):
    space = lax.axis_size("space")
    s_index = lax.axis_index("space").astype(jnp.int32)
    is_top = (s_index == 0).astype(jnp.int32)
    is_bottom = (s_index == space - 1).astype(jnp.int32)
    place = jnp.stack(
        [
            winner[0].astype(jnp.int32),
            is_top,
            is_bottom,
            s_index & 1,
            s_index >> 1,
            lax.axis_index("tensor").astype(jnp.int32),
            timestep[0].astype(jnp.int32),
        ]
    )

    def gather(own):
        return [own] + [lax.ppermute(own, "tensor", ring("tensor", k)) for k in (1, 2, 3)]

    own_p = feat_policy[0].transpose(0, 2, 1, 3)
    feat_ref, own_p = lax.optimization_barrier((feat_ref, own_p))
    own_r = feat_ref[0].transpose(0, 2, 1, 3)
    parts_p = gather(own_p)
    parts_r = gather(own_r)

    vectors = [b1_policy, b1_ref, gn_gain_policy, gn_bias_policy, gn_gain_ref, gn_bias_ref]
    columns, lift, drop, noise_rows, near_p, near_r = call(
        prep_kernel,
        [place, *[v[None, :] for v in vectors], w2_policy, w2_ref, time_table.T, noise[0],
         w1_policy.reshape(9 * CH, C), w1_ref.reshape(9 * CH, C)],
        [
            arr((2 * CH, COLS), F32),
            arr((2, 2, 72, CH), BF16),
            arr((2 * CH, 72), BF16),
            arr((ROWS, 8, COLS), F32),
            arr((9 * CH, C), BF16),
            arr((9 * CH, C), BF16),
        ],
        10**6,
        smem=1,
    )

    conv_flops = 2 * 9 * C * CH * 2 * PIX
    wide = arr((2 * CH, PIX), F32)
    thin = arr((2 * CH, COLS), F32)

    partner = [(i, i ^ 1) for i in range(space)]
    across = [(i, (i + 1 if i % 2 else i - 1) % space) for i in range(space)]
    pre_p, up_p, dn_p, to_ap, to_bp, feats = call(
        functools.partial(conv_kernel, False),
        [place, *parts_p, near_p, columns, noise_rows],
        [wide, thin, thin, arr((992, COLS), BF16), arr((992, COLS), BF16), arr((C, 2 * PIX), BF16)],
        conv_flops,
        smem=1,
        scratch=[pltpu.VMEM((C, 2 * PIX), BF16)],
    )
    got_bp = lax.ppermute(to_bp, "space", across)
    got_ap = lax.ppermute(to_ap, "space", partner)
    own_r, pre_p = lax.optimization_barrier((parts_r[0], pre_p))
    pre_r, up_r, dn_r, to_ar, to_br = call(
        functools.partial(conv_kernel, True),
        [place, own_r, *parts_r[1:], near_r, columns],
        [wide, thin, thin, arr((640, COLS), BF16), arr((640, COLS), BF16)],
        conv_flops,
        smem=1,
        scratch=[pltpu.VMEM((C, 2 * PIX), BF16)],
    )
    got_br = lax.ppermute(to_br, "space", across)
    got_ar = lax.ppermute(to_ar, "space", partner)

    ext_p, ext_r, noise_ext, sums = call(
        stat_kernel,
        [place, pre_p, up_p, dn_p, pre_r, up_r, dn_r, got_ap, got_bp, got_ar, got_br, noise_rows],
        [
            arr((2 * CH, 10 * COLS), F32),
            arr((2 * CH, 6 * COLS), F32),
            arr((8, 8, COLS), F32),
            arr((space, 16, COLS), F32),
        ],
        10**6,
        smem=1,
    )
    sums = lax.all_to_all(sums, "space", 0, 0, tiled=True)
    part, hidden, stat = call(
        hidden_kernel,
        [place, ext_p, ext_r, sums, columns, lift],
        [arr((12, 8, COLS), F32), arr((2 * CH, PIX), BF16), thin],
        10**7,
        smem=1,
    )
    others = [lax.ppermute(part, "tensor", ring("tensor", k)) for k in (1, 2, 3)]
    gnorm, head, partial = call(
        back_kernel,
        [place, part, *others, noise_ext, ext_p, stat, columns, hidden, drop],
        [arr((2 * CH, 6 * COLS), F32), arr((32, COLS), F32), arr((space, 24, COLS), F32)],
        10**7,
        smem=1,
    )
    partial = lax.all_to_all(partial, "space", 0, 0, tiled=True)
    keep, send, both, logits = call(
        weight_kernel,
        [place, gnorm, ext_p, stat, partial, feats, head],
        [arr((4, 40, 768), F32), arr((4, 48, 768), BF16), arr((32, COLS), F32), arr((1, 1), F32)],
        conv_flops,
        smem=1,
        scratch=[pltpu.VMEM((C, 768), F32)],
    )
    got = lax.ppermute(send, "space", partner)
    own, s1, s2, s3 = call(
        core_kernel,
        [place, keep, both, got],
        [arr((48, 768), F32)] + [arr((48, 768), BF16)] * 3,
        10**6,
        smem=1,
    )
    back = [
        lax.ppermute(sent, "space", ring("space", 2 * k)) for k, sent in ((1, s1), (2, s2), (3, s3))
    ]
    (packed,) = call(
        cross_kernel,
        [own, *back],
        [arr((8, 56, COLS), BF16)],
        10**6,
        scratch=[pltpu.VMEM((8 * 56, COLS), F32)],
    )
    packed = lax.all_to_all(packed, "dp", 0, 0, tiled=True)
    grad_one, grad_two = call(
        sum_kernel, [packed], [arr((9, 5, CH), F32), arr((9, 4, CH), F32)], 10**6
    )
    return (logits.reshape(1), grad_one.transpose(0, 2, 1), grad_two)


def solution(mesh):
    in_specs = (
        P("dp", None, "tensor", "space", None),
        P("dp", None, "tensor", "space", None),
        P("dp", None, None, "space", None),
        P(None, "tensor", None),
        P(None, "tensor", None),
        P("tensor"),
        P("tensor"),
        P("tensor"),
        P("tensor"),
        P("tensor"),
        P("tensor"),
        P(None, None, "tensor"),
        P(None, None, "tensor"),
        P(None, "tensor"),
        P("dp"),
        P("dp"),
    )
    out_specs = (P("dp"), P(None, "tensor", ("dp", "space")), P(None, None, "tensor"))
    return jax.shard_map(body, mesh=mesh, in_specs=in_specs, out_specs=out_specs, check_vma=False)
```

```python
import functools

import jax
import jax.numpy as jnp
from jax import lax
from jax.experimental import pallas as pl
from jax.experimental.pallas import tpu as pltpu
from jax.sharding import PartitionSpec as P

C = 320
GROUPS = 32
BETA = 500.0
EPS = 1e-05
CH = 80
ROWS = 4
COLS = 128
PIX = ROWS * COLS
GSIZE = C // GROUPS
LOCAL_GROUPS = CH // GSIZE
COUNT = float(GSIZE * 32 * 128)
CELLS = float(4 * 32 * 128)
F32 = jnp.float32
BF16 = jnp.bfloat16
HIGHEST = lax.Precision.HIGHEST

VM = pl.BlockSpec(memory_space=pltpu.VMEM)
SM = pl.BlockSpec(memory_space=pltpu.SMEM)


def call(kernel, ins, outs, flops, smem=0, scratch=()):
    in_bytes = sum(a.size * a.dtype.itemsize for a in ins)
    out_bytes = sum(s.size * s.dtype.itemsize for s in outs)
    return pl.pallas_call(
        kernel,
        out_shape=outs,
        in_specs=[SM] * smem + [VM] * (len(ins) - smem),
        out_specs=[VM] * len(outs),
        scratch_shapes=list(scratch),
        cost_estimate=pl.CostEstimate(
            flops=flops, bytes_accessed=in_bytes + out_bytes, transcendentals=0
        ),
        compiler_params=pltpu.CompilerParams(vmem_limit_bytes=12 * 1024 * 1024),
    )(*ins)


def arr(shape, dtype):
    return jax.ShapeDtypeStruct(shape, dtype)


def dot(a, b):
    return lax.dot_general(a, b, (((1,), (0,)), ((), ())), preferred_element_type=F32)


def dot_nt(a, b):
    return lax.dot_general(a, b, (((1,), (1,)), ((), ())), preferred_element_type=F32)


def exact_dot(a, b):
    return lax.dot_general(
        a, b, (((1,), (0,)), ((), ())), preferred_element_type=F32, precision=HIGHEST
    )


def from_left(tile):
    lane = lax.broadcasted_iota(jnp.int32, tile.shape, tile.ndim - 1)
    return jnp.where(lane == 0, 0.0, pltpu.roll(tile, 1, tile.ndim - 1))


def from_right(tile):
    lane = lax.broadcasted_iota(jnp.int32, tile.shape, tile.ndim - 1)
    return jnp.where(lane == COLS - 1, 0.0, pltpu.roll(tile, COLS - 1, tile.ndim - 1))


def row_of(tile, r):
    return tile[:, r * COLS : (r + 1) * COLS]


def sigmoid(value):
    return 0.5 + 0.5 * jnp.tanh(0.5 * value)


def members():
    group = lax.broadcasted_iota(jnp.int32, (2 * LOCAL_GROUPS, 2 * CH), 0)
    chan = lax.broadcasted_iota(jnp.int32, (2 * LOCAL_GROUPS, 2 * CH), 1)
    low = group * GSIZE
    return jnp.where((chan >= low) & (chan < low + GSIZE), 1.0, 0.0).astype(F32)


def spread(stat):
    chan = lax.broadcasted_iota(jnp.int32, (2 * CH, 2 * LOCAL_GROUPS), 0)
    group = lax.broadcasted_iota(jnp.int32, (2 * CH, 2 * LOCAL_GROUPS), 1)
    low = group * GSIZE
    pick = jnp.where((chan >= low) & (chan < low + GSIZE), 1.0, 0.0).astype(F32)
    return exact_dot(pick, stat)


def in_lanes(columns):
    rows = columns[0].shape[0]
    lane = lax.broadcasted_iota(jnp.int32, (rows, COLS), 1)
    out = jnp.zeros((rows, COLS), F32)
    for index, column in enumerate(columns):
        out = jnp.where(lane == index, column, out)
    return out


def prep_kernel(
    place_ref, b_p, b_r, gain_p, off_p, gain_r, off_r, w2_p, w2_r, table_ref, noise_ref, w1_p, w1_r,
    col_ref, lift_ref, drop_ref, rows_ref, w1_p_out, w1_r_out
):
    w1_p_out[...] = w1_p[...]
    w1_r_out[...] = w1_r[...]
    lane = lax.broadcasted_iota(jnp.int32, table_ref.shape, 1)
    shift = jnp.sum(
        jnp.where(lane == place_ref[6], table_ref[...], 0.0), axis=1, keepdims=True
    )
    eye = lax.broadcasted_iota(jnp.int32, (CH, CH), 0) == lax.broadcasted_iota(
        jnp.int32, (CH, CH), 1
    )

    def upright(ref):
        return jnp.sum(jnp.where(eye, ref[...], 0.0), axis=1, keepdims=True)

    block = in_lanes(
        [
            upright(gain_p),
            upright(off_p),
            upright(gain_r),
            upright(off_r),
            upright(b_p) + shift,
            upright(b_r) + shift,
        ]
    )
    col_ref[0:CH, :] = block
    col_ref[CH : 2 * CH, :] = block
    one = jnp.where(eye, 1.0, 0.0).astype(BF16)
    zero = jnp.zeros((4, CH), F32)
    for m, ref in enumerate((w2_p, w2_r)):
        for im in range(2):
            pieces = []
            for tap in range(9):
                rows = ref[tap].astype(F32)
                pieces += [rows, zero] if im == 0 else [zero, rows]
            padded = jnp.concatenate(pieces, axis=0).astype(BF16)
            lift_ref[m, im] = padded
            if m == 0:
                drop_ref[im * CH : (im + 1) * CH, :] = dot_nt(one, padded).astype(BF16)
    for im in range(2):
        for o in range(4):
            slot = im * 4 + o
            for r in range(ROWS):
                rows_ref[r, slot : slot + 1, :] = noise_ref[im, o, r : r + 1, :]


def conv_kernel(last, t_ref, f0, f1, f2, f3, w_ref, col_ref, *refs):
    if last:
        pre_ref, up_ref, dn_ref, send_a, send_b, fs_ref = refs
    else:
        noise_ref, pre_ref, up_ref, dn_ref, send_a, send_b, perm_ref, fs_ref = refs
    t = t_ref[5]
    bias = 5 if last else 4
    for k in range(4):
        base = pl.multiple_of(lax.rem(t - k + 4, 4) * CH, 16)
        for im in range(2):
            for r in range(ROWS):
                lo = im * PIX + r * COLS
                fs_ref[pl.ds(base, CH), lo : lo + COLS] = (f0, f1, f2, f3)[k][im, r]
    odd = t_ref[3] > 0
    count = 2 if last else 4
    if not last:
        for index in range(2):
            first, second = noise_ref[index], noise_ref[2 + index]
            for ref, value in (
                (send_a, jnp.where(odd, first, second)),
                (send_b, jnp.where(odd, second, first)),
            ):
                high = value.astype(BF16).astype(F32)
                both = jnp.concatenate([high, value - high], axis=0).astype(BF16)
                ref[960 + 16 * index : 976 + 16 * index, :] = both
        row = lax.broadcasted_iota(jnp.int32, (C, C), 0)
        chan = lax.broadcasted_iota(jnp.int32, (C, C), 1)
        core, rest = row // 160, row % 160
        want = 40 * (rest % 8) + 10 * (rest // 40) + 5 * core + (rest % 40) // 8
        pick = jnp.where(chan == want, 1.0, 0.0).astype(BF16)
        perm_ref[...] = dot(pick, fs_ref[...]).astype(BF16)
    for im in range(2):
        feats = fs_ref[:, im * PIX : (im + 1) * PIX]
        taps = [dot(w_ref[ky * 3 * CH : (ky + 1) * 3 * CH, :], feats) for ky in range(3)]
        chans = slice(im * CH, (im + 1) * CH)
        outs = []
        for r in range(-1, ROWS + 1):
            total = None
            for ky in range(3):
                src = r + ky - 1
                if 0 <= src < ROWS:
                    term = row_of(taps[ky], src)
                    total = term if total is None else total + term
            out = (
                total[CH : 2 * CH]
                + from_left(total[0:CH])
                + from_right(total[2 * CH : 3 * CH])
            )
            if r == -1:
                up_ref[chans, :] = out
            elif r == ROWS:
                dn_ref[chans, :] = out
            else:
                out = out + col_ref[chans, bias : bias + 1]
                pre_ref[chans, r * COLS : (r + 1) * COLS] = out
            outs.append(out)
        for index in range(count):
            upper, lower = outs[index], outs[ROWS + 2 - count + index]
            for ref, value in (
                (send_a, jnp.where(odd, upper, lower)),
                (send_b, jnp.where(odd, lower, upper)),
            ):
                high = value.astype(BF16)
                lo = index * 2 * CH + im * CH
                ref[lo : lo + CH, :] = high
                ref_low = (count + index) * 2 * CH + im * CH
                if count == 2:
                    ref[ref_low : ref_low + CH, :] = (value - high.astype(F32)).astype(BF16)
        if count == 4:
            for index in range(2):
                upper, lower = outs[index], outs[ROWS + index]
                for ref, value in (
                    (send_a, jnp.where(odd, upper, lower)),
                    (send_b, jnp.where(odd, lower, upper)),
                ):
                    rest = value - value.astype(BF16).astype(F32)
                    lo = (count + index) * 2 * CH + im * CH
                    ref[lo : lo + CH, :] = rest.astype(BF16)


def stat_kernel(
    place_ref, pre_p, up_p, dn_p, pre_r, up_r, dn_r, got_ap, got_bp, got_ar, got_br, noise_ref,
    ext_p, ext_r, noise_ext, out_ref
):
    odd = place_ref[3] > 0
    top = place_ref[1] > 0
    bottom = place_ref[2] > 0

    def rows_at(side, lo, hi):
        return jnp.where(odd, side[0][lo:hi, :], side[1][lo:hi, :]).astype(F32)

    def got(side, index):
        return rows_at(side, index * 2 * CH, (index + 1) * 2 * CH)

    def near(ref, index, low):
        return got(ref, index) + got(ref, low)

    columns = []
    first = 0
    for pre, up, dn, ext, got_a, got_b, halo in (
        (pre_p, up_p, dn_p, ext_p, got_ap, got_bp, 3),
        (pre_r, up_r, dn_r, ext_r, got_ar, got_br, 1),
    ):
        left, right = (got_a, got_b), (got_b, got_a)
        low = first + halo + 1
        rows = [pre[:, r * COLS : (r + 1) * COLS] for r in range(ROWS)]
        rows[0] = rows[0] + jnp.where(top, 0.0, near(left, first + halo, low + 1))
        rows[ROWS - 1] = rows[ROWS - 1] + jnp.where(bottom, 0.0, near(right, first, low))
        total = rows[0] + rows[1] + rows[2] + rows[3]
        square = (
            rows[0] * rows[0] + rows[1] * rows[1] + rows[2] * rows[2] + rows[3] * rows[3]
        )
        before = [got(left, first + index) for index in range(halo)]
        before[-1] = near(left, first + halo - 1, low) + up[...]
        after = [got(right, first + 1 + index) for index in range(halo)]
        after[0] = near(right, first + 1, low + 1) + dn[...]
        for index, row in enumerate(before + rows + after):
            ext[:, index * COLS : (index + 1) * COLS] = row
        columns.append(jnp.sum(total, axis=1, keepdims=True))
        columns.append(jnp.sum(square, axis=1, keepdims=True))
    for index in range(2):
        lo = 960 + 16 * index
        left, right = (got_ap, got_bp), (got_bp, got_ap)
        pair = rows_at(left, lo, lo + 16)
        noise_ext[index] = pair[0:8] + pair[8:16]
        pair = rows_at(right, lo, lo + 16)
        noise_ext[ROWS + 2 + index] = pair[0:8] + pair[8:16]
    for r in range(ROWS):
        noise_ext[2 + r] = noise_ref[r]
    out_ref[...] = exact_dot(members(), in_lanes(columns))


def add_kernel(one_ref, two_ref, out_ref):
    out_ref[...] = one_ref[...] + two_ref[...]


def moments(total):
    wide = spread(total / COUNT)
    result = []
    for m in range(2):
        mean = wide[:, 2 * m : 2 * m + 1]
        square = wide[:, 2 * m + 1 : 2 * m + 2]
        result.append((mean, lax.rsqrt(square - mean * mean + EPS)))
    return result


def hidden_kernel(
    edge_ref, ext_p, ext_r, sums_ref, more_ref, col_ref, lift_ref, part_ref, hid_ref, stat_ref
):
    stats = moments(sums_ref[...] + more_ref[...])
    stat_ref[...] = in_lanes([stats[0][0], stats[0][1]])
    for m, (ext, halo, start) in enumerate(((ext_p, 3, 0), (ext_r, 1, 8))):
        mean, inv = stats[m]
        gain = col_ref[:, 2 * m : 2 * m + 1]
        shift = col_ref[:, 2 * m + 1 : 2 * m + 2]
        slope = jnp.broadcast_to(inv * gain, (2 * CH, COLS))
        offset = jnp.broadcast_to(shift - mean * (inv * gain), (2 * CH, COLS))
        pieces = []
        for index in range(ROWS + 2 * halo):
            value = ext[:, index * COLS : (index + 1) * COLS]
            normed = value * slope + offset
            hidden = normed * sigmoid(normed)
            if index < halo:
                hidden = jnp.where(edge_ref[1] > 0, 0.0, hidden)
            if index >= ROWS + halo:
                hidden = jnp.where(edge_ref[2] > 0, 0.0, hidden)
            hidden = hidden.astype(BF16)
            if m == 0 and halo <= index < halo + ROWS:
                hid_ref[:, (index - halo) * COLS : (index - halo + 1) * COLS] = hidden
            pieces.append(hidden)
        joined = jnp.concatenate(pieces, axis=1)
        taps = dot(lift_ref[m, 0], joined[0:CH]) + dot(lift_ref[m, 1], joined[CH : 2 * CH])
        for index in range(ROWS + 2 * halo - 2):
            totals = [None, None, None]
            for kx in range(3):
                for ky in range(3):
                    tap = 3 * ky + kx
                    lo = (index + ky) * COLS
                    term = taps[8 * tap : 8 * tap + 8, lo : lo + COLS]
                    totals[kx] = term if totals[kx] is None else totals[kx] + term
            part_ref[start + index] = (
                totals[1] + from_left(totals[0]) + from_right(totals[2])
            )


def back_kernel(
    edge_ref, p0, p1, p2, p3, noise_ext, ext_p, stat_ref, col_ref, hid_ref, drop_ref,
    gnorm_ref, head_ref, out_ref
):
    def pred(index):
        return (p0[index] + p1[index]) + (p2[index] + p3[index])

    residual = [pred(index) - noise_ext[index] for index in range(ROWS + 4)]
    frozen = [pred(8 + r) - noise_ext[2 + r] for r in range(ROWS)]
    errors = []
    for rows in (residual[2 : 2 + ROWS], frozen):
        square = rows[0] * rows[0]
        for row in rows[1:]:
            square = square + row * row
        errors.append(jnp.sum(square, axis=1, keepdims=True))
    image = lax.broadcasted_iota(jnp.int32, (8, COLS), 0)
    residual = [jnp.where(image < 4, row, -row) for row in residual]
    for index in range(2):
        residual[index] = jnp.where(edge_ref[1] > 0, 0.0, residual[index])
        residual[ROWS + 2 + index] = jnp.where(edge_ref[2] > 0, 0.0, residual[ROWS + 2 + index])
    moved = [
        [from_right(row) for row in residual],
        residual,
        [from_left(row) for row in residual],
    ]
    blocks = []
    for ky in range(3):
        for kx in range(3):
            blocks.append(
                jnp.concatenate([moved[kx][r + 2 - ky] for r in range(ROWS + 2)], axis=1)
            )
    cot = jnp.concatenate(blocks, axis=0).astype(BF16)
    dhidden = dot(drop_ref[...], cot)
    mean = stat_ref[:, 0:1]
    inv = jnp.broadcast_to(stat_ref[:, 1:2], (2 * CH, COLS))
    base = jnp.broadcast_to(-mean * stat_ref[:, 1:2], (2 * CH, COLS))
    gain = jnp.broadcast_to(col_ref[:, 0:1], (2 * CH, COLS))
    shift = jnp.broadcast_to(col_ref[:, 1:2], (2 * CH, COLS))
    first = None
    second = None
    for index in range(ROWS + 2):
        lanes = slice(index * COLS, (index + 1) * COLS)
        centered = ext_p[:, (index + 2) * COLS : (index + 3) * COLS] * inv + base
        normed = centered * gain + shift
        gate = sigmoid(normed)
        gnorm = dhidden[:, lanes] * gate * (1.0 + normed * (1.0 - gate)) * gain
        gnorm_ref[:, lanes] = gnorm
        if 1 <= index <= ROWS:
            first = gnorm if first is None else first + gnorm
            extra = gnorm * centered
            second = extra if second is None else second + extra
    first = jnp.sum(first, axis=1, keepdims=True)
    second = jnp.sum(second, axis=1, keepdims=True)
    sums = exact_dot(members(), in_lanes([first, second]))
    mine = cot[:, COLS : (ROWS + 1) * COLS]
    grads = [dot_nt(mine, hid_ref[im * CH : (im + 1) * CH, :]) for im in range(2)]
    error = in_lanes(errors)
    head_ref[...] = jnp.zeros(head_ref.shape, F32)
    for tap in range(9):
        head = grads[0][8 * tap : 8 * tap + 4] + grads[1][8 * tap + 4 : 8 * tap + 8]
        if tap < 6:
            head_ref[4 * tap : 4 * tap + 4, 0:CH] = head
        else:
            lo = 4 * tap - 24
            head_ref[lo : lo + 4, CH:COLS] = head[:, 0 : COLS - CH]
            head_ref[lo + 12 : lo + 16, CH : 3 * CH - COLS] = head[:, COLS - CH : CH]
    out_ref[0:16, :] = sums
    out_ref[16:24, :] = error


def weight_kernel(
    place_ref, gnorm_ref, ext_p, stat_ref, red_ref, more_ref, fs_ref, head_ref,
    keep_ref, send_ref, both_ref, logit_ref, grad_ref
):
    total = red_ref[...] + more_ref[...]
    row = lax.broadcasted_iota(jnp.int32, (8, COLS), 0)
    signed = jnp.where(row < 4, total[16:24], -total[16:24])
    gaps = jnp.sum(signed, axis=0, keepdims=True)
    gap = (gaps[:, 0:1] - gaps[:, 1:2]) * (1.0 / CELLS)
    sign = 1.0 - 2.0 * place_ref[0].astype(F32)
    logit = (-0.5 * BETA) * sign * gap
    logit_ref[...] = logit
    scale = (BETA / CELLS) * sign * jax.nn.sigmoid(-logit)
    wide = spread(total[0:16] / COUNT)
    mean = stat_ref[:, 0:1]
    inv = stat_ref[:, 1:2]
    tilt = inv * inv * wide[:, 1:2]
    base = jnp.broadcast_to(tilt * mean - inv * wide[:, 0:1], (2 * CH, COLS))
    tilt = jnp.broadcast_to(tilt, (2 * CH, COLS))
    inv = jnp.broadcast_to(inv, (2 * CH, COLS))
    parts = []
    for index in range(ROWS + 2):
        value = ext_p[:, (index + 2) * COLS : (index + 3) * COLS]
        gnorm = gnorm_ref[:, index * COLS : (index + 1) * COLS]
        delta = inv * gnorm - tilt * value + base
        if index == 0:
            delta = jnp.where(place_ref[1] > 0, 0.0, delta)
        if index == ROWS + 1:
            delta = jnp.where(place_ref[2] > 0, 0.0, delta)
        parts.append(
            [from_right(delta).astype(BF16), delta.astype(BF16), from_left(delta).astype(BF16)]
        )
    blank = jnp.zeros((16, 2 * PIX), BF16)
    for ky in range(3):
        rows = []
        for kx in range(3):
            tiles = []
            for im in range(2):
                for r in range(ROWS):
                    tiles.append(parts[r + 2 - ky][kx][im * CH : (im + 1) * CH])
            rows.append(jnp.concatenate(tiles, axis=1))
        stack = jnp.concatenate(rows + [blank], axis=0)
        grad = dot_nt(fs_ref[...], stack) * scale
        grad_ref[:, 256 * ky : 256 * ky + 256] = grad
    core = place_ref[3]
    head = head_ref[...] * scale
    both_ref[...] = head
    for x in range(4):
        mine = pl.multiple_of(core * 160 + 40 * x, 8)
        his = pl.multiple_of((1 - core) * 160 + 40 * x, 8)
        keep_ref[x] = grad_ref[pl.ds(mine, 40), :]
        tail = [head[8 * j : 8 * j + 8] for j in range(3)] + [jnp.zeros((8, 3 * COLS), F32)]
        block = jnp.concatenate(
            [grad_ref[pl.ds(his, 40), :], jnp.concatenate(tail, axis=1)], axis=0
        )
        send_ref[x] = block.astype(BF16)


def core_kernel(x_ref, keep_ref, both_ref, got_ref, own_ref, s1, s2, s3):
    x = x_ref[4]
    tail = [both_ref[8 * j : 8 * j + 8, :] for j in range(3)] + [jnp.zeros((8, 3 * COLS), F32)]
    tail = jnp.concatenate(tail, axis=1)
    for k, ref in enumerate((own_ref, s1, s2, s3)):
        where = lax.rem(x + k, 4)
        got = got_ref[where].astype(F32)
        block = jnp.concatenate([keep_ref[where] + got[0:40], tail + got[40:48]], axis=0)
        ref[...] = block.astype(ref.dtype)


def cross_kernel(own_ref, r1, r2, r3, out_ref, pack_ref):
    total = (own_ref[...] + r1[...].astype(F32)) + (r2[...].astype(F32) + r3[...].astype(F32))
    for half in range(6):
        lanes = slice(half * COLS, (half + 1) * COLS)
        for ii in range(5):
            pack_ref[pl.ds(half * 5 + ii, 8, stride=56), :] = total[8 * ii : 8 * ii + 8, lanes]
    for spare in (30, 31):
        pack_ref[pl.ds(spare, 8, stride=56), :] = jnp.zeros((8, COLS), F32)
    for d in range(8):
        for j in range(3):
            pack_ref[56 * d + 32 + 8 * j : 56 * d + 40 + 8 * j, :] = total[
                40:48, j * COLS : (j + 1) * COLS
            ]
        out_ref[d] = pack_ref[56 * d : 56 * d + 56, :].astype(BF16)


def sum_kernel(got_ref, one_ref, two_ref):
    total = got_ref[0].astype(F32)
    for d in range(1, got_ref.shape[0]):
        total = total + got_ref[d].astype(F32)
    chunk = 5
    for tap in range(6):
        two_ref[tap] = total[32 + 4 * tap : 36 + 4 * tap, 0:CH]
    for tap in range(6, 9):
        lo = 8 + 4 * tap
        two_ref[tap] = jnp.concatenate(
            [total[lo : lo + 4, CH:COLS], total[lo + 12 : lo + 16, CH : 3 * CH - COLS]], axis=1
        )
    for ky in range(3):
        lo = 2 * ky * chunk
        wide = jnp.concatenate(
            [total[lo : lo + chunk], total[lo + chunk : lo + 2 * chunk]], axis=1
        )
        for kx in range(3):
            one_ref[3 * ky + kx] = wide[:, kx * CH : (kx + 1) * CH]


def ring(axis, step):
    count = lax.axis_size(axis)
    return [(i, (i + step) % count) for i in range(count)]


def body(
    feat_policy,
    feat_ref,
    noise,
    w1_policy,
    w1_ref,
    b1_policy,
    b1_ref,
    gn_gain_policy,
    gn_bias_policy,
    gn_gain_ref,
    gn_bias_ref,
    w2_policy,
    w2_ref,
    time_table,
    timestep,
    winner,
):
    space = lax.axis_size("space")
    s_index = lax.axis_index("space").astype(jnp.int32)
    is_top = (s_index == 0).astype(jnp.int32)
    is_bottom = (s_index == space - 1).astype(jnp.int32)
    place = jnp.stack(
        [
            winner[0].astype(jnp.int32),
            is_top,
            is_bottom,
            s_index & 1,
            s_index >> 1,
            lax.axis_index("tensor").astype(jnp.int32),
            timestep[0].astype(jnp.int32),
        ]
    )

    def gather(own):
        return [own] + [lax.ppermute(own, "tensor", ring("tensor", k)) for k in (1, 2, 3)]

    own_p = feat_policy[0].transpose(0, 2, 1, 3)
    feat_ref, own_p = lax.optimization_barrier((feat_ref, own_p))
    own_r = feat_ref[0].transpose(0, 2, 1, 3)
    parts_p = gather(own_p)
    parts_r = gather(own_r)

    vectors = [b1_policy, b1_ref, gn_gain_policy, gn_bias_policy, gn_gain_ref, gn_bias_ref]
    columns, lift, drop, noise_rows, near_p, near_r = call(
        prep_kernel,
        [place, *[v[None, :] for v in vectors], w2_policy, w2_ref, time_table.T, noise[0],
         w1_policy.reshape(9 * CH, C), w1_ref.reshape(9 * CH, C)],
        [
            arr((2 * CH, COLS), F32),
            arr((2, 2, 72, CH), BF16),
            arr((2 * CH, 72), BF16),
            arr((ROWS, 8, COLS), F32),
            arr((9 * CH, C), BF16),
            arr((9 * CH, C), BF16),
        ],
        10**6,
        smem=1,
    )

    conv_flops = 2 * 9 * C * CH * 2 * PIX
    wide = arr((2 * CH, PIX), F32)
    thin = arr((2 * CH, COLS), F32)

    partner = [(i, i ^ 1) for i in range(space)]
    across = [(i, (i + 1 if i % 2 else i - 1) % space) for i in range(space)]
    chips = space // 2
    beside = [(i, 2 * ((i // 2) ^ 1) + i % 2) for i in range(space)]
    facing = [(i, 2 * (chips - 1 - i // 2) + i % 2) for i in range(space)]

    def spread_sum(value):
        for pairs in (partner, beside):
            other = lax.ppermute(value, "space", pairs)
            (value,) = call(add_kernel, [value, other], [arr(value.shape, F32)], 10**4)
        return value, lax.ppermute(value, "space", facing)

    pre_p, up_p, dn_p, to_ap, to_bp, feats = call(
        functools.partial(conv_kernel, False),
        [place, *parts_p, near_p, columns, noise_rows],
        [wide, thin, thin, arr((992, COLS), BF16), arr((992, COLS), BF16), arr((C, 2 * PIX), BF16)],
        conv_flops,
        smem=1,
        scratch=[pltpu.VMEM((C, 2 * PIX), BF16)],
    )
    got_bp = lax.ppermute(to_bp, "space", across)
    got_ap = lax.ppermute(to_ap, "space", partner)
    own_r, pre_p = lax.optimization_barrier((parts_r[0], pre_p))
    pre_r, up_r, dn_r, to_ar, to_br = call(
        functools.partial(conv_kernel, True),
        [place, own_r, *parts_r[1:], near_r, columns],
        [wide, thin, thin, arr((640, COLS), BF16), arr((640, COLS), BF16)],
        conv_flops,
        smem=1,
        scratch=[pltpu.VMEM((C, 2 * PIX), BF16)],
    )
    got_br = lax.ppermute(to_br, "space", across)
    got_ar = lax.ppermute(to_ar, "space", partner)

    ext_p, ext_r, noise_ext, sums = call(
        stat_kernel,
        [place, pre_p, up_p, dn_p, pre_r, up_r, dn_r, got_ap, got_bp, got_ar, got_br, noise_rows],
        [
            arr((2 * CH, 10 * COLS), F32),
            arr((2 * CH, 6 * COLS), F32),
            arr((8, 8, COLS), F32),
            arr((16, COLS), F32),
        ],
        10**6,
        smem=1,
    )
    sums, more = spread_sum(sums)
    part, hidden, stat = call(
        hidden_kernel,
        [place, ext_p, ext_r, sums, more, columns, lift],
        [arr((12, 8, COLS), F32), arr((2 * CH, PIX), BF16), thin],
        10**7,
        smem=1,
    )
    others = [lax.ppermute(part, "tensor", ring("tensor", k)) for k in (1, 2, 3)]
    gnorm, head, partial = call(
        back_kernel,
        [place, part, *others, noise_ext, ext_p, stat, columns, hidden, drop],
        [arr((2 * CH, 6 * COLS), F32), arr((32, COLS), F32), arr((24, COLS), F32)],
        10**7,
        smem=1,
    )
    partial, extra = spread_sum(partial)
    keep, send, both, logits = call(
        weight_kernel,
        [place, gnorm, ext_p, stat, partial, extra, feats, head],
        [arr((4, 40, 768), F32), arr((4, 48, 768), BF16), arr((32, COLS), F32), arr((1, 1), F32)],
        conv_flops,
        smem=1,
        scratch=[pltpu.VMEM((C, 768), F32)],
    )
    got = lax.ppermute(send, "space", partner)
    own, s1, s2, s3 = call(
        core_kernel,
        [place, keep, both, got],
        [arr((48, 768), F32)] + [arr((48, 768), BF16)] * 3,
        10**6,
        smem=1,
    )
    back = [
        lax.ppermute(sent, "space", ring("space", 2 * k)) for k, sent in ((1, s1), (2, s2), (3, s3))
    ]
    (packed,) = call(
        cross_kernel,
        [own, *back],
        [arr((8, 56, COLS), BF16)],
        10**6,
        scratch=[pltpu.VMEM((8 * 56, COLS), F32)],
    )
    packed = lax.all_to_all(packed, "dp", 0, 0, tiled=True)
    grad_one, grad_two = call(
        sum_kernel, [packed], [arr((9, 5, CH), F32), arr((9, 4, CH), F32)], 10**6
    )
    return (logits.reshape(1), grad_one.transpose(0, 2, 1), grad_two)


def solution(mesh):
    in_specs = (
        P("dp", None, "tensor", "space", None),
        P("dp", None, "tensor", "space", None),
        P("dp", None, None, "space", None),
        P(None, "tensor", None),
        P(None, "tensor", None),
        P("tensor"),
        P("tensor"),
        P("tensor"),
        P("tensor"),
        P("tensor"),
        P("tensor"),
        P(None, None, "tensor"),
        P(None, None, "tensor"),
        P(None, "tensor"),
        P("dp"),
        P("dp"),
    )
    out_specs = (P("dp"), P(None, "tensor", ("dp", "space")), P(None, None, "tensor"))
    return jax.shard_map(body, mesh=mesh, in_specs=in_specs, out_specs=out_specs, check_vma=False)
```

```python
import functools

import jax
import jax.numpy as jnp
from jax import lax
from jax.experimental import pallas as pl
from jax.experimental.pallas import tpu as pltpu
from jax.sharding import PartitionSpec as P

C = 320
GROUPS = 32
BETA = 500.0
EPS = 1e-05
CH = 80
ROWS = 4
COLS = 128
PIX = ROWS * COLS
GSIZE = C // GROUPS
LOCAL_GROUPS = CH // GSIZE
COUNT = float(GSIZE * 32 * 128)
CELLS = float(4 * 32 * 128)
F32 = jnp.float32
BF16 = jnp.bfloat16
HIGHEST = lax.Precision.HIGHEST

VM = pl.BlockSpec(memory_space=pltpu.VMEM)
SM = pl.BlockSpec(memory_space=pltpu.SMEM)


def call(kernel, ins, outs, flops, smem=0, scratch=()):
    in_bytes = sum(a.size * a.dtype.itemsize for a in ins)
    out_bytes = sum(s.size * s.dtype.itemsize for s in outs)
    return pl.pallas_call(
        kernel,
        out_shape=outs,
        in_specs=[SM] * smem + [VM] * (len(ins) - smem),
        out_specs=[VM] * len(outs),
        scratch_shapes=list(scratch),
        cost_estimate=pl.CostEstimate(
            flops=flops, bytes_accessed=in_bytes + out_bytes, transcendentals=0
        ),
        compiler_params=pltpu.CompilerParams(vmem_limit_bytes=12 * 1024 * 1024),
    )(*ins)


def arr(shape, dtype):
    return jax.ShapeDtypeStruct(shape, dtype)


def dot(a, b):
    return lax.dot_general(a, b, (((1,), (0,)), ((), ())), preferred_element_type=F32)


def dot_nt(a, b):
    return lax.dot_general(a, b, (((1,), (1,)), ((), ())), preferred_element_type=F32)


def exact_dot(a, b):
    return lax.dot_general(
        a, b, (((1,), (0,)), ((), ())), preferred_element_type=F32, precision=HIGHEST
    )


def from_left(tile):
    lane = lax.broadcasted_iota(jnp.int32, tile.shape, tile.ndim - 1)
    return jnp.where(lane == 0, 0.0, pltpu.roll(tile, 1, tile.ndim - 1))


def from_right(tile):
    lane = lax.broadcasted_iota(jnp.int32, tile.shape, tile.ndim - 1)
    return jnp.where(lane == COLS - 1, 0.0, pltpu.roll(tile, COLS - 1, tile.ndim - 1))


def row_of(tile, r):
    return tile[:, r * COLS : (r + 1) * COLS]


def sigmoid(value):
    return 0.5 + 0.5 * jnp.tanh(0.5 * value)


def members():
    group = lax.broadcasted_iota(jnp.int32, (2 * LOCAL_GROUPS, 2 * CH), 0)
    chan = lax.broadcasted_iota(jnp.int32, (2 * LOCAL_GROUPS, 2 * CH), 1)
    low = group * GSIZE
    return jnp.where((chan >= low) & (chan < low + GSIZE), 1.0, 0.0).astype(F32)


def spread(stat):
    chan = lax.broadcasted_iota(jnp.int32, (2 * CH, 2 * LOCAL_GROUPS), 0)
    group = lax.broadcasted_iota(jnp.int32, (2 * CH, 2 * LOCAL_GROUPS), 1)
    low = group * GSIZE
    pick = jnp.where((chan >= low) & (chan < low + GSIZE), 1.0, 0.0).astype(F32)
    return exact_dot(pick, stat)


def in_lanes(columns):
    rows = columns[0].shape[0]
    lane = lax.broadcasted_iota(jnp.int32, (rows, COLS), 1)
    out = jnp.zeros((rows, COLS), F32)
    for index, column in enumerate(columns):
        out = jnp.where(lane == index, column, out)
    return out


def prep_kernel(
    place_ref, b_p, b_r, gain_p, off_p, gain_r, off_r, w2_p, w2_r, table_ref, noise_ref, w1_p, w1_r,
    col_ref, lift_ref, drop_ref, rows_ref, w1_p_out, w1_r_out
):
    w1_p_out[...] = w1_p[...]
    w1_r_out[...] = w1_r[...]
    lane = lax.broadcasted_iota(jnp.int32, table_ref.shape, 1)
    shift = jnp.sum(
        jnp.where(lane == place_ref[6], table_ref[...], 0.0), axis=1, keepdims=True
    )
    eye = lax.broadcasted_iota(jnp.int32, (CH, CH), 0) == lax.broadcasted_iota(
        jnp.int32, (CH, CH), 1
    )

    def upright(ref):
        return jnp.sum(jnp.where(eye, ref[...], 0.0), axis=1, keepdims=True)

    block = in_lanes(
        [
            upright(gain_p),
            upright(off_p),
            upright(gain_r),
            upright(off_r),
            upright(b_p) + shift,
            upright(b_r) + shift,
        ]
    )
    col_ref[0:CH, :] = block
    col_ref[CH : 2 * CH, :] = block
    one = jnp.where(eye, 1.0, 0.0).astype(BF16)
    zero = jnp.zeros((4, CH), F32)
    for m, ref in enumerate((w2_p, w2_r)):
        for im in range(2):
            pieces = []
            for tap in range(9):
                rows = ref[tap].astype(F32)
                pieces += [rows, zero] if im == 0 else [zero, rows]
            padded = jnp.concatenate(pieces, axis=0).astype(BF16)
            lift_ref[m, im] = padded
            if m == 0:
                drop_ref[im * CH : (im + 1) * CH, :] = dot_nt(one, padded).astype(BF16)
    for im in range(2):
        for o in range(4):
            slot = im * 4 + o
            for r in range(ROWS):
                rows_ref[r, slot : slot + 1, :] = noise_ref[im, o, r : r + 1, :]


def conv_kernel(last, t_ref, f0, f1, f2, f3, w_ref, col_ref, *refs):
    if last:
        pre_ref, up_ref, dn_ref, send_a, send_b, fs_ref = refs
    else:
        noise_ref, pre_ref, up_ref, dn_ref, send_a, send_b, perm_ref, fs_ref = refs
    t = t_ref[5]
    bias = 5 if last else 4
    for k in range(4):
        base = pl.multiple_of(lax.rem(t - k + 4, 4) * CH, 16)
        for im in range(2):
            for r in range(ROWS):
                lo = im * PIX + r * COLS
                fs_ref[pl.ds(base, CH), lo : lo + COLS] = (f0, f1, f2, f3)[k][im, r]
    odd = t_ref[3] > 0
    count = 2 if last else 4
    if not last:
        for index in range(2):
            first, second = noise_ref[index], noise_ref[2 + index]
            for ref, value in (
                (send_a, jnp.where(odd, first, second)),
                (send_b, jnp.where(odd, second, first)),
            ):
                high = value.astype(BF16).astype(F32)
                both = jnp.concatenate([high, value - high], axis=0).astype(BF16)
                ref[960 + 16 * index : 976 + 16 * index, :] = both
        row = lax.broadcasted_iota(jnp.int32, (C, C), 0)
        chan = lax.broadcasted_iota(jnp.int32, (C, C), 1)
        core, rest = row // 160, row % 160
        want = 40 * (rest % 8) + 10 * (rest // 40) + 5 * core + (rest % 40) // 8
        pick = jnp.where(chan == want, 1.0, 0.0).astype(BF16)
        perm_ref[...] = dot(pick, fs_ref[...]).astype(BF16)
    for im in range(2):
        feats = fs_ref[:, im * PIX : (im + 1) * PIX]
        taps = [dot(w_ref[ky * 3 * CH : (ky + 1) * 3 * CH, :], feats) for ky in range(3)]
        chans = slice(im * CH, (im + 1) * CH)
        outs = []
        for r in range(-1, ROWS + 1):
            total = None
            for ky in range(3):
                src = r + ky - 1
                if 0 <= src < ROWS:
                    term = row_of(taps[ky], src)
                    total = term if total is None else total + term
            out = (
                total[CH : 2 * CH]
                + from_left(total[0:CH])
                + from_right(total[2 * CH : 3 * CH])
            )
            if r == -1:
                up_ref[chans, :] = out
            elif r == ROWS:
                dn_ref[chans, :] = out
            else:
                out = out + col_ref[chans, bias : bias + 1]
                pre_ref[chans, r * COLS : (r + 1) * COLS] = out
            outs.append(out)
        for index in range(count):
            upper, lower = outs[index], outs[ROWS + 2 - count + index]
            for ref, value in (
                (send_a, jnp.where(odd, upper, lower)),
                (send_b, jnp.where(odd, lower, upper)),
            ):
                high = value.astype(BF16)
                lo = index * 2 * CH + im * CH
                ref[lo : lo + CH, :] = high
                ref_low = (count + index) * 2 * CH + im * CH
                if count == 2:
                    ref[ref_low : ref_low + CH, :] = (value - high.astype(F32)).astype(BF16)
        if count == 4:
            for index in range(2):
                upper, lower = outs[index], outs[ROWS + index]
                for ref, value in (
                    (send_a, jnp.where(odd, upper, lower)),
                    (send_b, jnp.where(odd, lower, upper)),
                ):
                    rest = value - value.astype(BF16).astype(F32)
                    lo = (count + index) * 2 * CH + im * CH
                    ref[lo : lo + CH, :] = rest.astype(BF16)


def stat_kernel(
    place_ref, pre_p, up_p, dn_p, pre_r, up_r, dn_r, got_ap, got_bp, got_ar, got_br, noise_ref,
    ext_p, ext_r, noise_ext, out_ref
):
    odd = place_ref[3] > 0
    top = place_ref[1] > 0
    bottom = place_ref[2] > 0

    def rows_at(side, lo, hi):
        return jnp.where(odd, side[0][lo:hi, :].astype(F32), side[1][lo:hi, :].astype(F32))

    def got(side, index):
        return rows_at(side, index * 2 * CH, (index + 1) * 2 * CH)

    def near(ref, index, low):
        return got(ref, index) + got(ref, low)

    columns = []
    first = 0
    for pre, up, dn, ext, got_a, got_b, halo in (
        (pre_p, up_p, dn_p, ext_p, got_ap, got_bp, 3),
        (pre_r, up_r, dn_r, ext_r, got_ar, got_br, 1),
    ):
        left, right = (got_a, got_b), (got_b, got_a)
        low = first + halo + 1
        rows = [pre[:, r * COLS : (r + 1) * COLS] for r in range(ROWS)]
        rows[0] = rows[0] + jnp.where(top, 0.0, near(left, first + halo, low + 1))
        rows[ROWS - 1] = rows[ROWS - 1] + jnp.where(bottom, 0.0, near(right, first, low))
        total = rows[0] + rows[1] + rows[2] + rows[3]
        square = (
            rows[0] * rows[0] + rows[1] * rows[1] + rows[2] * rows[2] + rows[3] * rows[3]
        )
        before = [got(left, first + index) for index in range(halo)]
        before[-1] = near(left, first + halo - 1, low) + up[...]
        after = [got(right, first + 1 + index) for index in range(halo)]
        after[0] = near(right, first + 1, low + 1) + dn[...]
        for index, row in enumerate(before + rows + after):
            ext[:, index * COLS : (index + 1) * COLS] = row
        columns.append(jnp.sum(total, axis=1, keepdims=True))
        columns.append(jnp.sum(square, axis=1, keepdims=True))
    for index in range(2):
        lo = 960 + 16 * index
        left, right = (got_ap, got_bp), (got_bp, got_ap)
        pair = rows_at(left, lo, lo + 16)
        noise_ext[index] = pair[0:8] + pair[8:16]
        pair = rows_at(right, lo, lo + 16)
        noise_ext[ROWS + 2 + index] = pair[0:8] + pair[8:16]
    for r in range(ROWS):
        noise_ext[2 + r] = noise_ref[r]
    sums = exact_dot(members(), in_lanes(columns))
    for peer in range(out_ref.shape[0]):
        out_ref[peer] = sums


def moments(total):
    wide = spread(total / COUNT)
    result = []
    for m in range(2):
        mean = wide[:, 2 * m : 2 * m + 1]
        square = wide[:, 2 * m + 1 : 2 * m + 2]
        result.append((mean, lax.rsqrt(square - mean * mean + EPS)))
    return result


def hidden_kernel(
    edge_ref, ext_p, ext_r, sums_ref, col_ref, lift_ref, part_ref, hid_ref, stat_ref
):
    stats = moments(jnp.sum(sums_ref[...], axis=0))
    stat_ref[...] = in_lanes([stats[0][0], stats[0][1]])
    for m, (ext, halo, start) in enumerate(((ext_p, 3, 0), (ext_r, 1, 8))):
        mean, inv = stats[m]
        gain = col_ref[:, 2 * m : 2 * m + 1]
        shift = col_ref[:, 2 * m + 1 : 2 * m + 2]
        pieces = []
        for index in range(ROWS + 2 * halo):
            value = ext[:, index * COLS : (index + 1) * COLS]
            normed = ((value - mean) * inv) * gain + shift
            hidden = normed * sigmoid(normed)
            if index < halo:
                hidden = jnp.where(edge_ref[1] > 0, 0.0, hidden)
            if index >= ROWS + halo:
                hidden = jnp.where(edge_ref[2] > 0, 0.0, hidden)
            hidden = hidden.astype(BF16)
            if m == 0 and halo <= index < halo + ROWS:
                hid_ref[:, (index - halo) * COLS : (index - halo + 1) * COLS] = hidden
            pieces.append(hidden)
        joined = jnp.concatenate(pieces, axis=1)
        taps = dot(lift_ref[m, 0], joined[0:CH]) + dot(lift_ref[m, 1], joined[CH : 2 * CH])
        for index in range(ROWS + 2 * halo - 2):
            totals = [None, None, None]
            for kx in range(3):
                for ky in range(3):
                    tap = 3 * ky + kx
                    lo = (index + ky) * COLS
                    term = taps[8 * tap : 8 * tap + 8, lo : lo + COLS]
                    totals[kx] = term if totals[kx] is None else totals[kx] + term
            part_ref[start + index] = (
                totals[1] + from_left(totals[0]) + from_right(totals[2])
            )


def back_kernel(
    edge_ref, p0, p1, p2, p3, noise_ext, ext_p, stat_ref, col_ref, hid_ref, drop_ref,
    gnorm_ref, head_ref, out_ref
):
    def pred(index):
        return (p0[index] + p1[index]) + (p2[index] + p3[index])

    residual = [pred(index) - noise_ext[index] for index in range(ROWS + 4)]
    frozen = [pred(8 + r) - noise_ext[2 + r] for r in range(ROWS)]
    errors = []
    for rows in (residual[2 : 2 + ROWS], frozen):
        square = rows[0] * rows[0]
        for row in rows[1:]:
            square = square + row * row
        errors.append(jnp.sum(square, axis=1, keepdims=True))
    image = lax.broadcasted_iota(jnp.int32, (8, COLS), 0)
    residual = [jnp.where(image < 4, row, -row) for row in residual]
    for index in range(2):
        residual[index] = jnp.where(edge_ref[1] > 0, 0.0, residual[index])
        residual[ROWS + 2 + index] = jnp.where(edge_ref[2] > 0, 0.0, residual[ROWS + 2 + index])
    moved = [
        [from_right(row) for row in residual],
        residual,
        [from_left(row) for row in residual],
    ]
    blocks = []
    for ky in range(3):
        for kx in range(3):
            blocks.append(
                jnp.concatenate([moved[kx][r + 2 - ky] for r in range(ROWS + 2)], axis=1)
            )
    cot = jnp.concatenate(blocks, axis=0).astype(BF16)
    dhidden = dot(drop_ref[...], cot)
    mean = stat_ref[:, 0:1]
    inv = stat_ref[:, 1:2]
    gain = col_ref[:, 0:1]
    shift = col_ref[:, 1:2]
    first = None
    second = None
    for index in range(ROWS + 2):
        lanes = slice(index * COLS, (index + 1) * COLS)
        centered = (ext_p[:, (index + 2) * COLS : (index + 3) * COLS] - mean) * inv
        normed = centered * gain + shift
        gate = sigmoid(normed)
        gnorm = dhidden[:, lanes] * gate * (1.0 + normed * (1.0 - gate)) * gain
        gnorm_ref[:, lanes] = gnorm
        if 1 <= index <= ROWS:
            first = gnorm if first is None else first + gnorm
            extra = gnorm * centered
            second = extra if second is None else second + extra
    first = jnp.sum(first, axis=1, keepdims=True)
    second = jnp.sum(second, axis=1, keepdims=True)
    sums = exact_dot(members(), in_lanes([first, second]))
    mine = cot[:, COLS : (ROWS + 1) * COLS]
    grads = [dot_nt(mine, hid_ref[im * CH : (im + 1) * CH, :]) for im in range(2)]
    error = in_lanes(errors)
    head_ref[...] = jnp.zeros(head_ref.shape, F32)
    for tap in range(9):
        head = grads[0][8 * tap : 8 * tap + 4] + grads[1][8 * tap + 4 : 8 * tap + 8]
        if tap < 6:
            head_ref[4 * tap : 4 * tap + 4, 0:CH] = head
        else:
            lo = 4 * tap - 24
            head_ref[lo : lo + 4, CH:COLS] = head[:, 0 : COLS - CH]
            head_ref[lo + 12 : lo + 16, CH : 3 * CH - COLS] = head[:, COLS - CH : CH]
    for peer in range(out_ref.shape[0]):
        out_ref[peer, 0:16, :] = sums
        out_ref[peer, 16:24, :] = error


def weight_kernel(
    place_ref, gnorm_ref, ext_p, stat_ref, red_ref, fs_ref, head_ref,
    keep_ref, send_ref, both_ref, logit_ref, grad_ref
):
    total = jnp.sum(red_ref[...], axis=0)
    row = lax.broadcasted_iota(jnp.int32, (8, COLS), 0)
    signed = jnp.where(row < 4, total[16:24], -total[16:24])
    gaps = jnp.sum(signed, axis=0, keepdims=True)
    gap = (gaps[:, 0:1] - gaps[:, 1:2]) * (1.0 / CELLS)
    sign = 1.0 - 2.0 * place_ref[0].astype(F32)
    logit = (-0.5 * BETA) * sign * gap
    logit_ref[...] = logit
    scale = (BETA / CELLS) * sign * jax.nn.sigmoid(-logit)
    wide = spread(total[0:16] / COUNT)
    mean = stat_ref[:, 0:1]
    inv = stat_ref[:, 1:2]
    parts = []
    for index in range(ROWS + 2):
        centered = (ext_p[:, (index + 2) * COLS : (index + 3) * COLS] - mean) * inv
        gnorm = gnorm_ref[:, index * COLS : (index + 1) * COLS]
        delta = inv * (gnorm - wide[:, 0:1] - centered * wide[:, 1:2])
        if index == 0:
            delta = jnp.where(place_ref[1] > 0, 0.0, delta)
        if index == ROWS + 1:
            delta = jnp.where(place_ref[2] > 0, 0.0, delta)
        parts.append(
            [from_right(delta).astype(BF16), delta.astype(BF16), from_left(delta).astype(BF16)]
        )
    blank = jnp.zeros((16, 2 * PIX), BF16)
    for ky in range(3):
        rows = []
        for kx in range(3):
            tiles = []
            for im in range(2):
                for r in range(ROWS):
                    tiles.append(parts[r + 2 - ky][kx][im * CH : (im + 1) * CH])
            rows.append(jnp.concatenate(tiles, axis=1))
        stack = jnp.concatenate(rows + [blank], axis=0)
        grad = dot_nt(fs_ref[...], stack) * scale
        grad_ref[:, 256 * ky : 256 * ky + 256] = grad
    core = place_ref[3]
    head = head_ref[...] * scale
    both_ref[...] = head
    for x in range(4):
        mine = pl.multiple_of(core * 160 + 40 * x, 8)
        his = pl.multiple_of((1 - core) * 160 + 40 * x, 8)
        keep_ref[x] = grad_ref[pl.ds(mine, 40), :]
        tail = [head[8 * j : 8 * j + 8] for j in range(3)] + [jnp.zeros((8, 3 * COLS), F32)]
        block = jnp.concatenate(
            [grad_ref[pl.ds(his, 40), :], jnp.concatenate(tail, axis=1)], axis=0
        )
        send_ref[x] = block.astype(BF16)


def core_kernel(x_ref, keep_ref, both_ref, got_ref, own_ref, s1, s2, s3):
    x = x_ref[4]
    tail = [both_ref[8 * j : 8 * j + 8, :] for j in range(3)] + [jnp.zeros((8, 3 * COLS), F32)]
    tail = jnp.concatenate(tail, axis=1)
    for k, ref in enumerate((own_ref, s1, s2, s3)):
        where = lax.rem(x + k, 4)
        got = got_ref[where].astype(F32)
        block = jnp.concatenate([keep_ref[where] + got[0:40], tail + got[40:48]], axis=0)
        ref[...] = block.astype(ref.dtype)


def cross_kernel(own_ref, r1, r2, r3, out_ref, pack_ref):
    total = (own_ref[...] + r1[...].astype(F32)) + (r2[...].astype(F32) + r3[...].astype(F32))
    for half in range(6):
        lanes = slice(half * COLS, (half + 1) * COLS)
        for ii in range(5):
            pack_ref[pl.ds(half * 5 + ii, 8, stride=56), :] = total[8 * ii : 8 * ii + 8, lanes]
    for spare in (30, 31):
        pack_ref[pl.ds(spare, 8, stride=56), :] = jnp.zeros((8, COLS), F32)
    for d in range(8):
        for j in range(3):
            pack_ref[56 * d + 32 + 8 * j : 56 * d + 40 + 8 * j, :] = total[
                40:48, j * COLS : (j + 1) * COLS
            ]
        out_ref[d] = pack_ref[56 * d : 56 * d + 56, :].astype(BF16)


def sum_kernel(got_ref, one_ref, two_ref):
    total = got_ref[0].astype(F32)
    for d in range(1, got_ref.shape[0]):
        total = total + got_ref[d].astype(F32)
    chunk = 5
    for tap in range(6):
        two_ref[tap] = total[32 + 4 * tap : 36 + 4 * tap, 0:CH]
    for tap in range(6, 9):
        lo = 8 + 4 * tap
        two_ref[tap] = jnp.concatenate(
            [total[lo : lo + 4, CH:COLS], total[lo + 12 : lo + 16, CH : 3 * CH - COLS]], axis=1
        )
    for ky in range(3):
        lo = 2 * ky * chunk
        wide = jnp.concatenate(
            [total[lo : lo + chunk], total[lo + chunk : lo + 2 * chunk]], axis=1
        )
        for kx in range(3):
            one_ref[3 * ky + kx] = wide[:, kx * CH : (kx + 1) * CH]


def ring(axis, step):
    count = lax.axis_size(axis)
    return [(i, (i + step) % count) for i in range(count)]


def body(
    feat_policy,
    feat_ref,
    noise,
    w1_policy,
    w1_ref,
    b1_policy,
    b1_ref,
    gn_gain_policy,
    gn_bias_policy,
    gn_gain_ref,
    gn_bias_ref,
    w2_policy,
    w2_ref,
    time_table,
    timestep,
    winner,
):
    space = lax.axis_size("space")
    s_index = lax.axis_index("space").astype(jnp.int32)
    is_top = (s_index == 0).astype(jnp.int32)
    is_bottom = (s_index == space - 1).astype(jnp.int32)
    place = jnp.stack(
        [
            winner[0].astype(jnp.int32),
            is_top,
            is_bottom,
            s_index & 1,
            s_index >> 1,
            lax.axis_index("tensor").astype(jnp.int32),
            timestep[0].astype(jnp.int32),
        ]
    )

    def gather(own, way):
        left = lax.ppermute(own, "tensor", ring("tensor", 1))
        right = lax.ppermute(own, "tensor", ring("tensor", -1))
        far = lax.ppermute(left if way > 0 else right, "tensor", ring("tensor", way))
        return [own, left, far, right]

    own_p = feat_policy[0].transpose(0, 2, 1, 3)
    feat_ref, own_p = lax.optimization_barrier((feat_ref, own_p))
    own_r = feat_ref[0].transpose(0, 2, 1, 3)
    parts_p = gather(own_p, -1)
    parts_r = gather(own_r, 1)

    vectors = [b1_policy, b1_ref, gn_gain_policy, gn_bias_policy, gn_gain_ref, gn_bias_ref]
    columns, lift, drop, noise_rows, near_p, near_r = call(
        prep_kernel,
        [place, *[v[None, :] for v in vectors], w2_policy, w2_ref, time_table.T, noise[0],
         w1_policy.reshape(9 * CH, C), w1_ref.reshape(9 * CH, C)],
        [
            arr((2 * CH, COLS), F32),
            arr((2, 2, 72, CH), BF16),
            arr((2 * CH, 72), BF16),
            arr((ROWS, 8, COLS), F32),
            arr((9 * CH, C), BF16),
            arr((9 * CH, C), BF16),
        ],
        10**6,
        smem=1,
    )

    conv_flops = 2 * 9 * C * CH * 2 * PIX
    wide = arr((2 * CH, PIX), F32)
    thin = arr((2 * CH, COLS), F32)

    partner = [(i, i ^ 1) for i in range(space)]
    across = [(i, (i + 1 if i % 2 else i - 1) % space) for i in range(space)]
    pre_p, up_p, dn_p, to_ap, to_bp, feats = call(
        functools.partial(conv_kernel, False),
        [place, *parts_p, near_p, columns, noise_rows],
        [wide, thin, thin, arr((992, COLS), BF16), arr((992, COLS), BF16), arr((C, 2 * PIX), BF16)],
        conv_flops,
        smem=1,
        scratch=[pltpu.VMEM((C, 2 * PIX), BF16)],
    )
    got_bp = lax.ppermute(to_bp, "space", across)
    got_ap = lax.ppermute(to_ap, "space", partner)
    own_r, pre_p = lax.optimization_barrier((parts_r[0], pre_p))
    pre_r, up_r, dn_r, to_ar, to_br = call(
        functools.partial(conv_kernel, True),
        [place, own_r, *parts_r[1:], near_r, columns],
        [wide, thin, thin, arr((640, COLS), BF16), arr((640, COLS), BF16)],
        conv_flops,
        smem=1,
        scratch=[pltpu.VMEM((C, 2 * PIX), BF16)],
    )
    got_br = lax.ppermute(to_br, "space", across)
    got_ar = lax.ppermute(to_ar, "space", partner)

    ext_p, ext_r, noise_ext, sums = call(
        stat_kernel,
        [place, pre_p, up_p, dn_p, pre_r, up_r, dn_r, got_ap, got_bp, got_ar, got_br, noise_rows],
        [
            arr((2 * CH, 10 * COLS), F32),
            arr((2 * CH, 6 * COLS), F32),
            arr((8, 8, COLS), F32),
            arr((space, 16, COLS), F32),
        ],
        10**6,
        smem=1,
    )
    sums = lax.all_to_all(sums, "space", 0, 0, tiled=True)
    part, hidden, stat = call(
        hidden_kernel,
        [place, ext_p, ext_r, sums, columns, lift],
        [arr((12, 8, COLS), F32), arr((2 * CH, PIX), BF16), thin],
        10**7,
        smem=1,
    )
    others = [lax.ppermute(part, "tensor", ring("tensor", k)) for k in (1, 2, 3)]
    gnorm, head, partial = call(
        back_kernel,
        [place, part, *others, noise_ext, ext_p, stat, columns, hidden, drop],
        [arr((2 * CH, 6 * COLS), F32), arr((32, COLS), F32), arr((space, 24, COLS), F32)],
        10**7,
        smem=1,
    )
    partial = lax.all_to_all(partial, "space", 0, 0, tiled=True)
    keep, send, both, logits = call(
        weight_kernel,
        [place, gnorm, ext_p, stat, partial, feats, head],
        [arr((4, 40, 768), F32), arr((4, 48, 768), BF16), arr((32, COLS), F32), arr((1, 1), F32)],
        conv_flops,
        smem=1,
        scratch=[pltpu.VMEM((C, 768), F32)],
    )
    got = lax.ppermute(send, "space", partner)
    own, s1, s2, s3 = call(
        core_kernel,
        [place, keep, both, got],
        [arr((48, 768), F32)] + [arr((48, 768), BF16)] * 3,
        10**6,
        smem=1,
    )
    back = [
        lax.ppermute(sent, "space", ring("space", 2 * k)) for k, sent in ((1, s1), (2, s2), (3, s3))
    ]
    (packed,) = call(
        cross_kernel,
        [own, *back],
        [arr((8, 56, COLS), BF16)],
        10**6,
        scratch=[pltpu.VMEM((8 * 56, COLS), F32)],
    )
    packed = lax.all_to_all(packed, "dp", 0, 0, tiled=True)
    grad_one, grad_two = call(
        sum_kernel, [packed], [arr((9, 5, CH), F32), arr((9, 4, CH), F32)], 10**6
    )
    return (logits.reshape(1), grad_one.transpose(0, 2, 1), grad_two)


def solution(mesh):
    in_specs = (
        P("dp", None, "tensor", "space", None),
        P("dp", None, "tensor", "space", None),
        P("dp", None, None, "space", None),
        P(None, "tensor", None),
        P(None, "tensor", None),
        P("tensor"),
        P("tensor"),
        P("tensor"),
        P("tensor"),
        P("tensor"),
        P("tensor"),
        P(None, None, "tensor"),
        P(None, None, "tensor"),
        P(None, "tensor"),
        P("dp"),
        P("dp"),
    )
    out_specs = (P("dp"), P(None, "tensor", ("dp", "space")), P(None, None, "tensor"))
    return jax.shard_map(body, mesh=mesh, in_specs=in_specs, out_specs=out_specs, check_vma=False)
```

```python
import functools

import jax
import jax.numpy as jnp
from jax import lax
from jax.experimental import pallas as pl
from jax.experimental.pallas import tpu as pltpu
from jax.sharding import PartitionSpec as P

C = 320
GROUPS = 32
BETA = 500.0
EPS = 1e-05
CH = 80
ROWS = 4
COLS = 128
PIX = ROWS * COLS
GSIZE = C // GROUPS
LOCAL_GROUPS = CH // GSIZE
COUNT = float(GSIZE * 32 * 128)
CELLS = float(4 * 32 * 128)
F32 = jnp.float32
BF16 = jnp.bfloat16
HIGHEST = lax.Precision.HIGHEST

VM = pl.BlockSpec(memory_space=pltpu.VMEM)
SM = pl.BlockSpec(memory_space=pltpu.SMEM)


def call(kernel, ins, outs, flops, smem=0, scratch=()):
    in_bytes = sum(a.size * a.dtype.itemsize for a in ins)
    out_bytes = sum(s.size * s.dtype.itemsize for s in outs)
    return pl.pallas_call(
        kernel,
        out_shape=outs,
        in_specs=[SM] * smem + [VM] * (len(ins) - smem),
        out_specs=[VM] * len(outs),
        scratch_shapes=list(scratch),
        cost_estimate=pl.CostEstimate(
            flops=flops, bytes_accessed=in_bytes + out_bytes, transcendentals=0
        ),
        compiler_params=pltpu.CompilerParams(vmem_limit_bytes=12 * 1024 * 1024),
    )(*ins)


def arr(shape, dtype):
    return jax.ShapeDtypeStruct(shape, dtype)


def dot(a, b):
    return lax.dot_general(a, b, (((1,), (0,)), ((), ())), preferred_element_type=F32)


def dot_nt(a, b):
    return lax.dot_general(a, b, (((1,), (1,)), ((), ())), preferred_element_type=F32)


def exact_dot(a, b):
    return lax.dot_general(
        a, b, (((1,), (0,)), ((), ())), preferred_element_type=F32, precision=HIGHEST
    )


def from_left(tile):
    lane = lax.broadcasted_iota(jnp.int32, tile.shape, tile.ndim - 1)
    return jnp.where(lane == 0, 0.0, pltpu.roll(tile, 1, tile.ndim - 1))


def from_right(tile):
    lane = lax.broadcasted_iota(jnp.int32, tile.shape, tile.ndim - 1)
    return jnp.where(lane == COLS - 1, 0.0, pltpu.roll(tile, COLS - 1, tile.ndim - 1))


def row_of(tile, r):
    return tile[:, r * COLS : (r + 1) * COLS]


def sigmoid(value):
    return 0.5 + 0.5 * jnp.tanh(0.5 * value)


def members():
    group = lax.broadcasted_iota(jnp.int32, (2 * LOCAL_GROUPS, 2 * CH), 0)
    chan = lax.broadcasted_iota(jnp.int32, (2 * LOCAL_GROUPS, 2 * CH), 1)
    low = group * GSIZE
    return jnp.where((chan >= low) & (chan < low + GSIZE), 1.0, 0.0).astype(F32)


def spread(stat):
    chan = lax.broadcasted_iota(jnp.int32, (2 * CH, 2 * LOCAL_GROUPS), 0)
    group = lax.broadcasted_iota(jnp.int32, (2 * CH, 2 * LOCAL_GROUPS), 1)
    low = group * GSIZE
    pick = jnp.where((chan >= low) & (chan < low + GSIZE), 1.0, 0.0).astype(F32)
    return exact_dot(pick, stat)


def in_lanes(columns):
    rows = columns[0].shape[0]
    lane = lax.broadcasted_iota(jnp.int32, (rows, COLS), 1)
    out = jnp.zeros((rows, COLS), F32)
    for index, column in enumerate(columns):
        out = jnp.where(lane == index, column, out)
    return out


def prep_kernel(
    place_ref, b_p, b_r, gain_p, off_p, gain_r, off_r, w2_p, w2_r, table_ref, noise_ref,
    col_ref, lift_ref, drop_ref, rows_ref
):
    lane = lax.broadcasted_iota(jnp.int32, table_ref.shape, 1)
    shift = jnp.sum(
        jnp.where(lane == place_ref[6], table_ref[...], 0.0), axis=1, keepdims=True
    )
    eye = lax.broadcasted_iota(jnp.int32, (CH, CH), 0) == lax.broadcasted_iota(
        jnp.int32, (CH, CH), 1
    )

    def upright(ref):
        return jnp.sum(jnp.where(eye, ref[...], 0.0), axis=1, keepdims=True)

    block = in_lanes(
        [
            upright(gain_p),
            upright(off_p),
            upright(gain_r),
            upright(off_r),
            upright(b_p) + shift,
            upright(b_r) + shift,
        ]
    )
    col_ref[0:CH, :] = block
    col_ref[CH : 2 * CH, :] = block
    one = jnp.where(eye, 1.0, 0.0).astype(BF16)
    zero = jnp.zeros((4, CH), F32)
    for m, ref in enumerate((w2_p, w2_r)):
        for im in range(2):
            pieces = []
            for tap in range(9):
                rows = ref[tap].astype(F32)
                pieces += [rows, zero] if im == 0 else [zero, rows]
            padded = jnp.concatenate(pieces, axis=0).astype(BF16)
            lift_ref[m, im] = padded
            if m == 0:
                drop_ref[im * CH : (im + 1) * CH, :] = dot_nt(one, padded).astype(BF16)
    for im in range(2):
        for o in range(4):
            slot = im * 4 + o
            for r in range(ROWS):
                rows_ref[r, slot : slot + 1, :] = noise_ref[im, o, r : r + 1, :]


def conv_kernel(last, t_ref, f0, f1, f2, f3, w_ref, *refs):
    if last:
        pre_ref, up_ref, dn_ref, send_a, send_b, fs_ref = refs
    else:
        noise_ref, pre_ref, up_ref, dn_ref, send_a, send_b, perm_ref, fs_ref = refs
    t = t_ref[0]
    for k in range(4):
        base = pl.multiple_of(lax.rem(t - k + 4, 4) * CH, 16)
        for im in range(2):
            for r in range(ROWS):
                lo = im * PIX + r * COLS
                fs_ref[pl.ds(base, CH), lo : lo + COLS] = (f0, f1, f2, f3)[k][im, r]
    odd = t_ref[1] > 0
    count = 2 if last else 4
    if not last:
        for index in range(2):
            first, second = [
                jnp.concatenate(
                    [noise_ref[im, o, r : r + 1, :] for im in range(2) for o in range(4)], axis=0
                )
                for r in (index, 2 + index)
            ]
            for ref, value in (
                (send_a, jnp.where(odd, first, second)),
                (send_b, jnp.where(odd, second, first)),
            ):
                high = value.astype(BF16).astype(F32)
                both = jnp.concatenate([high, value - high], axis=0).astype(BF16)
                ref[960 + 16 * index : 976 + 16 * index, :] = both
        row = lax.broadcasted_iota(jnp.int32, (C, C), 0)
        chan = lax.broadcasted_iota(jnp.int32, (C, C), 1)
        core, rest = row // 160, row % 160
        want = 40 * (rest % 8) + 10 * (rest // 40) + 5 * core + (rest % 40) // 8
        pick = jnp.where(chan == want, 1.0, 0.0).astype(BF16)
        perm_ref[...] = dot(pick, fs_ref[...]).astype(BF16)
    for im in range(2):
        feats = fs_ref[:, im * PIX : (im + 1) * PIX]
        taps = [dot(w_ref[ky * 3 * CH : (ky + 1) * 3 * CH, :], feats) for ky in range(3)]
        chans = slice(im * CH, (im + 1) * CH)
        outs = []
        for r in range(-1, ROWS + 1):
            total = None
            for ky in range(3):
                src = r + ky - 1
                if 0 <= src < ROWS:
                    term = row_of(taps[ky], src)
                    total = term if total is None else total + term
            out = (
                total[CH : 2 * CH]
                + from_left(total[0:CH])
                + from_right(total[2 * CH : 3 * CH])
            )
            if r == -1:
                up_ref[chans, :] = out
            elif r == ROWS:
                dn_ref[chans, :] = out
            else:
                pre_ref[chans, r * COLS : (r + 1) * COLS] = out
            outs.append(out)
        for index in range(count):
            upper, lower = outs[index], outs[ROWS + 2 - count + index]
            for ref, value in (
                (send_a, jnp.where(odd, upper, lower)),
                (send_b, jnp.where(odd, lower, upper)),
            ):
                high = value.astype(BF16)
                lo = index * 2 * CH + im * CH
                ref[lo : lo + CH, :] = high
                ref_low = (count + index) * 2 * CH + im * CH
                if count == 2:
                    ref[ref_low : ref_low + CH, :] = (value - high.astype(F32)).astype(BF16)
        if count == 4:
            for index in range(2):
                upper, lower = outs[index], outs[ROWS + index]
                for ref, value in (
                    (send_a, jnp.where(odd, upper, lower)),
                    (send_b, jnp.where(odd, lower, upper)),
                ):
                    rest = value - value.astype(BF16).astype(F32)
                    lo = (count + index) * 2 * CH + im * CH
                    ref[lo : lo + CH, :] = rest.astype(BF16)


def stat_kernel(
    place_ref, pre_p, up_p, dn_p, pre_r, up_r, dn_r, got_ap, got_bp, got_ar, got_br, noise_ref, col_ref,
    ext_p, ext_r, noise_ext, out_ref
):
    odd = place_ref[3] > 0
    top = place_ref[1] > 0
    bottom = place_ref[2] > 0

    def rows_at(side, lo, hi):
        return jnp.where(odd, side[0][lo:hi, :].astype(F32), side[1][lo:hi, :].astype(F32))

    def got(side, index):
        return rows_at(side, index * 2 * CH, (index + 1) * 2 * CH)

    def near(ref, index, low):
        return got(ref, index) + got(ref, low)

    columns = []
    first = 0
    for pre, up, dn, ext, got_a, got_b, halo, slot in (
        (pre_p, up_p, dn_p, ext_p, got_ap, got_bp, 3, 4),
        (pre_r, up_r, dn_r, ext_r, got_ar, got_br, 1, 5),
    ):
        left, right = (got_a, got_b), (got_b, got_a)
        low = first + halo + 1
        bias = jnp.broadcast_to(col_ref[:, slot : slot + 1], (2 * CH, COLS))
        rows = [pre[:, r * COLS : (r + 1) * COLS] for r in range(ROWS)]
        rows[0] = rows[0] + jnp.where(top, 0.0, near(left, first + halo, low + 1))
        rows[ROWS - 1] = rows[ROWS - 1] + jnp.where(bottom, 0.0, near(right, first, low))
        rows = [row + bias for row in rows]
        total = rows[0] + rows[1] + rows[2] + rows[3]
        square = (
            rows[0] * rows[0] + rows[1] * rows[1] + rows[2] * rows[2] + rows[3] * rows[3]
        )
        before = [got(left, first + index) for index in range(halo)]
        before[-1] = near(left, first + halo - 1, low) + up[...]
        after = [got(right, first + 1 + index) for index in range(halo)]
        after[0] = near(right, first + 1, low + 1) + dn[...]
        before = [row + bias for row in before]
        after = [row + bias for row in after]
        for index, row in enumerate(before + rows + after):
            ext[:, index * COLS : (index + 1) * COLS] = row
        columns.append(jnp.sum(total, axis=1, keepdims=True))
        columns.append(jnp.sum(square, axis=1, keepdims=True))
    for index in range(2):
        lo = 960 + 16 * index
        left, right = (got_ap, got_bp), (got_bp, got_ap)
        pair = rows_at(left, lo, lo + 16)
        noise_ext[index] = pair[0:8] + pair[8:16]
        pair = rows_at(right, lo, lo + 16)
        noise_ext[ROWS + 2 + index] = pair[0:8] + pair[8:16]
    for r in range(ROWS):
        noise_ext[2 + r] = noise_ref[r]
    sums = exact_dot(members(), in_lanes(columns))
    for peer in range(out_ref.shape[0]):
        out_ref[peer] = sums


def moments(total):
    wide = spread(total / COUNT)
    result = []
    for m in range(2):
        mean = wide[:, 2 * m : 2 * m + 1]
        square = wide[:, 2 * m + 1 : 2 * m + 2]
        result.append((mean, lax.rsqrt(square - mean * mean + EPS)))
    return result


def hidden_kernel(
    edge_ref, ext_p, ext_r, sums_ref, col_ref, lift_ref, part_ref, hid_ref, stat_ref
):
    stats = moments(jnp.sum(sums_ref[...], axis=0))
    stat_ref[...] = in_lanes([stats[0][0], stats[0][1]])
    for m, (ext, halo, start) in enumerate(((ext_p, 3, 0), (ext_r, 1, 8))):
        mean, inv = stats[m]
        gain = col_ref[:, 2 * m : 2 * m + 1]
        shift = col_ref[:, 2 * m + 1 : 2 * m + 2]
        pieces = []
        for index in range(ROWS + 2 * halo):
            value = ext[:, index * COLS : (index + 1) * COLS]
            normed = ((value - mean) * inv) * gain + shift
            hidden = normed * sigmoid(normed)
            if index < halo:
                hidden = jnp.where(edge_ref[1] > 0, 0.0, hidden)
            if index >= ROWS + halo:
                hidden = jnp.where(edge_ref[2] > 0, 0.0, hidden)
            hidden = hidden.astype(BF16)
            if m == 0 and halo <= index < halo + ROWS:
                hid_ref[:, (index - halo) * COLS : (index - halo + 1) * COLS] = hidden
            pieces.append(hidden)
        joined = jnp.concatenate(pieces, axis=1)
        taps = dot(lift_ref[m, 0], joined[0:CH]) + dot(lift_ref[m, 1], joined[CH : 2 * CH])
        for index in range(ROWS + 2 * halo - 2):
            totals = [None, None, None]
            for kx in range(3):
                for ky in range(3):
                    tap = 3 * ky + kx
                    lo = (index + ky) * COLS
                    term = taps[8 * tap : 8 * tap + 8, lo : lo + COLS]
                    totals[kx] = term if totals[kx] is None else totals[kx] + term
            part_ref[start + index] = (
                totals[1] + from_left(totals[0]) + from_right(totals[2])
            )


def back_kernel(
    edge_ref, p0, p1, p2, p3, noise_ext, ext_p, stat_ref, col_ref, hid_ref, drop_ref,
    gnorm_ref, head_ref, out_ref
):
    def pred(index):
        return (p0[index] + p1[index]) + (p2[index] + p3[index])

    residual = [pred(index) - noise_ext[index] for index in range(ROWS + 4)]
    frozen = [pred(8 + r) - noise_ext[2 + r] for r in range(ROWS)]
    errors = []
    for rows in (residual[2 : 2 + ROWS], frozen):
        square = rows[0] * rows[0]
        for row in rows[1:]:
            square = square + row * row
        errors.append(jnp.sum(square, axis=1, keepdims=True))
    image = lax.broadcasted_iota(jnp.int32, (8, COLS), 0)
    residual = [jnp.where(image < 4, row, -row) for row in residual]
    for index in range(2):
        residual[index] = jnp.where(edge_ref[1] > 0, 0.0, residual[index])
        residual[ROWS + 2 + index] = jnp.where(edge_ref[2] > 0, 0.0, residual[ROWS + 2 + index])
    moved = [
        [from_right(row) for row in residual],
        residual,
        [from_left(row) for row in residual],
    ]
    blocks = []
    for ky in range(3):
        for kx in range(3):
            blocks.append(
                jnp.concatenate([moved[kx][r + 2 - ky] for r in range(ROWS + 2)], axis=1)
            )
    cot = jnp.concatenate(blocks, axis=0).astype(BF16)
    dhidden = dot(drop_ref[...], cot)
    mean = stat_ref[:, 0:1]
    inv = stat_ref[:, 1:2]
    gain = col_ref[:, 0:1]
    shift = col_ref[:, 1:2]
    first = None
    second = None
    for index in range(ROWS + 2):
        lanes = slice(index * COLS, (index + 1) * COLS)
        centered = (ext_p[:, (index + 2) * COLS : (index + 3) * COLS] - mean) * inv
        normed = centered * gain + shift
        gate = sigmoid(normed)
        gnorm = dhidden[:, lanes] * gate * (1.0 + normed * (1.0 - gate)) * gain
        gnorm_ref[:, lanes] = gnorm
        if 1 <= index <= ROWS:
            first = gnorm if first is None else first + gnorm
            extra = gnorm * centered
            second = extra if second is None else second + extra
    first = jnp.sum(first, axis=1, keepdims=True)
    second = jnp.sum(second, axis=1, keepdims=True)
    sums = exact_dot(members(), in_lanes([first, second]))
    mine = cot[:, COLS : (ROWS + 1) * COLS]
    grads = [dot_nt(mine, hid_ref[im * CH : (im + 1) * CH, :]) for im in range(2)]
    error = in_lanes(errors)
    head_ref[...] = jnp.zeros(head_ref.shape, F32)
    for tap in range(9):
        head = grads[0][8 * tap : 8 * tap + 4] + grads[1][8 * tap + 4 : 8 * tap + 8]
        if tap < 6:
            head_ref[4 * tap : 4 * tap + 4, 0:CH] = head
        else:
            lo = 4 * tap - 24
            head_ref[lo : lo + 4, CH:COLS] = head[:, 0 : COLS - CH]
            head_ref[lo + 12 : lo + 16, CH : 3 * CH - COLS] = head[:, COLS - CH : CH]
    for peer in range(out_ref.shape[0]):
        out_ref[peer, 0:16, :] = sums
        out_ref[peer, 16:24, :] = error


def weight_kernel(
    place_ref, gnorm_ref, ext_p, stat_ref, red_ref, fs_ref, head_ref,
    keep_ref, send_ref, both_ref, logit_ref, grad_ref
):
    total = jnp.sum(red_ref[...], axis=0)
    row = lax.broadcasted_iota(jnp.int32, (8, COLS), 0)
    signed = jnp.where(row < 4, total[16:24], -total[16:24])
    gaps = jnp.sum(signed, axis=0, keepdims=True)
    gap = (gaps[:, 0:1] - gaps[:, 1:2]) * (1.0 / CELLS)
    sign = 1.0 - 2.0 * place_ref[0].astype(F32)
    logit = (-0.5 * BETA) * sign * gap
    logit_ref[...] = logit
    scale = (BETA / CELLS) * sign * jax.nn.sigmoid(-logit)
    wide = spread(total[0:16] / COUNT)
    mean = stat_ref[:, 0:1]
    inv = stat_ref[:, 1:2]
    parts = []
    for index in range(ROWS + 2):
        centered = (ext_p[:, (index + 2) * COLS : (index + 3) * COLS] - mean) * inv
        gnorm = gnorm_ref[:, index * COLS : (index + 1) * COLS]
        delta = inv * (gnorm - wide[:, 0:1] - centered * wide[:, 1:2])
        if index == 0:
            delta = jnp.where(place_ref[1] > 0, 0.0, delta)
        if index == ROWS + 1:
            delta = jnp.where(place_ref[2] > 0, 0.0, delta)
        parts.append(
            [from_right(delta).astype(BF16), delta.astype(BF16), from_left(delta).astype(BF16)]
        )
    blank = jnp.zeros((16, 2 * PIX), BF16)
    for ky in range(3):
        rows = []
        for kx in range(3):
            tiles = []
            for im in range(2):
                for r in range(ROWS):
                    tiles.append(parts[r + 2 - ky][kx][im * CH : (im + 1) * CH])
            rows.append(jnp.concatenate(tiles, axis=1))
        stack = jnp.concatenate(rows + [blank], axis=0)
        grad = dot_nt(fs_ref[...], stack) * scale
        grad_ref[:, 256 * ky : 256 * ky + 256] = grad
    core = place_ref[3]
    head = head_ref[...] * scale
    both_ref[...] = head
    for x in range(4):
        mine = pl.multiple_of(core * 160 + 40 * x, 8)
        his = pl.multiple_of((1 - core) * 160 + 40 * x, 8)
        keep_ref[x] = grad_ref[pl.ds(mine, 40), :]
        tail = [head[8 * j : 8 * j + 8] for j in range(3)] + [jnp.zeros((8, 3 * COLS), F32)]
        block = jnp.concatenate(
            [grad_ref[pl.ds(his, 40), :], jnp.concatenate(tail, axis=1)], axis=0
        )
        send_ref[x] = block.astype(BF16)


def core_kernel(x_ref, keep_ref, both_ref, got_ref, own_ref, s1, s2, s3):
    x = x_ref[4]
    tail = [both_ref[8 * j : 8 * j + 8, :] for j in range(3)] + [jnp.zeros((8, 3 * COLS), F32)]
    tail = jnp.concatenate(tail, axis=1)
    for k, ref in enumerate((own_ref, s1, s2, s3)):
        where = lax.rem(x + k, 4)
        got = got_ref[where].astype(F32)
        block = jnp.concatenate([keep_ref[where] + got[0:40], tail + got[40:48]], axis=0)
        ref[...] = block.astype(ref.dtype)


def cross_kernel(own_ref, r1, r2, r3, out_ref, pack_ref):
    total = (own_ref[...] + r1[...].astype(F32)) + (r2[...].astype(F32) + r3[...].astype(F32))
    for half in range(6):
        lanes = slice(half * COLS, (half + 1) * COLS)
        for ii in range(5):
            pack_ref[pl.ds(half * 5 + ii, 8, stride=56), :] = total[8 * ii : 8 * ii + 8, lanes]
    for spare in (30, 31):
        pack_ref[pl.ds(spare, 8, stride=56), :] = jnp.zeros((8, COLS), F32)
    for d in range(8):
        for j in range(3):
            pack_ref[56 * d + 32 + 8 * j : 56 * d + 40 + 8 * j, :] = total[
                40:48, j * COLS : (j + 1) * COLS
            ]
        out_ref[d] = pack_ref[56 * d : 56 * d + 56, :].astype(BF16)


def sum_kernel(got_ref, one_ref, two_ref):
    total = got_ref[0].astype(F32)
    for d in range(1, got_ref.shape[0]):
        total = total + got_ref[d].astype(F32)
    chunk = 5
    for tap in range(6):
        two_ref[tap] = total[32 + 4 * tap : 36 + 4 * tap, 0:CH]
    for tap in range(6, 9):
        lo = 8 + 4 * tap
        two_ref[tap] = jnp.concatenate(
            [total[lo : lo + 4, CH:COLS], total[lo + 12 : lo + 16, CH : 3 * CH - COLS]], axis=1
        )
    for ky in range(3):
        lo = 2 * ky * chunk
        wide = jnp.concatenate(
            [total[lo : lo + chunk], total[lo + chunk : lo + 2 * chunk]], axis=1
        )
        for kx in range(3):
            one_ref[3 * ky + kx] = wide[:, kx * CH : (kx + 1) * CH]


def ring(axis, step):
    count = lax.axis_size(axis)
    return [(i, (i + step) % count) for i in range(count)]


def body(
    feat_policy,
    feat_ref,
    noise,
    w1_policy,
    w1_ref,
    b1_policy,
    b1_ref,
    gn_gain_policy,
    gn_bias_policy,
    gn_gain_ref,
    gn_bias_ref,
    w2_policy,
    w2_ref,
    time_table,
    timestep,
    winner,
):
    space = lax.axis_size("space")
    s_index = lax.axis_index("space").astype(jnp.int32)
    spot = jnp.stack([lax.axis_index("tensor").astype(jnp.int32), s_index & 1])

    def gather(own):
        return [own] + [lax.ppermute(own, "tensor", ring("tensor", k)) for k in (1, 2, 3)]

    own_p = feat_policy[0].transpose(0, 2, 1, 3)
    feat_ref, own_p = lax.optimization_barrier((feat_ref, own_p))
    own_r = feat_ref[0].transpose(0, 2, 1, 3)
    parts_p = gather(own_p)
    parts_r = gather(own_r)

    conv_flops = 2 * 9 * C * CH * 2 * PIX
    wide = arr((2 * CH, PIX), F32)
    thin = arr((2 * CH, COLS), F32)

    partner = [(i, i ^ 1) for i in range(space)]
    across = [(i, (i + 1 if i % 2 else i - 1) % space) for i in range(space)]
    pre_p, up_p, dn_p, to_ap, to_bp, feats = call(
        functools.partial(conv_kernel, False),
        [spot, *parts_p, w1_policy.reshape(9 * CH, C), noise[0]],
        [wide, thin, thin, arr((992, COLS), BF16), arr((992, COLS), BF16), arr((C, 2 * PIX), BF16)],
        conv_flops,
        smem=1,
        scratch=[pltpu.VMEM((C, 2 * PIX), BF16)],
    )
    got_bp = lax.ppermute(to_bp, "space", across)
    got_ap = lax.ppermute(to_ap, "space", partner)
    own_r, pre_p = lax.optimization_barrier((parts_r[0], pre_p))
    pre_r, up_r, dn_r, to_ar, to_br = call(
        functools.partial(conv_kernel, True),
        [spot, own_r, *parts_r[1:], w1_ref.reshape(9 * CH, C)],
        [wide, thin, thin, arr((640, COLS), BF16), arr((640, COLS), BF16)],
        conv_flops,
        smem=1,
        scratch=[pltpu.VMEM((C, 2 * PIX), BF16)],
    )
    got_br = lax.ppermute(to_br, "space", across)
    got_ar = lax.ppermute(to_ar, "space", partner)

    pre_r, timestep = lax.optimization_barrier((pre_r, timestep))
    is_top = (s_index == 0).astype(jnp.int32)
    is_bottom = (s_index == space - 1).astype(jnp.int32)
    place = jnp.stack(
        [
            winner[0].astype(jnp.int32),
            is_top,
            is_bottom,
            s_index & 1,
            s_index >> 1,
            lax.axis_index("tensor").astype(jnp.int32),
            timestep[0].astype(jnp.int32),
        ]
    )
    vectors = [b1_policy, b1_ref, gn_gain_policy, gn_bias_policy, gn_gain_ref, gn_bias_ref]
    columns, lift, drop, noise_rows = call(
        prep_kernel,
        [place, *[v[None, :] for v in vectors], w2_policy, w2_ref, time_table.T, noise[0]],
        [
            arr((2 * CH, COLS), F32),
            arr((2, 2, 72, CH), BF16),
            arr((2 * CH, 72), BF16),
            arr((ROWS, 8, COLS), F32),
        ],
        10**6,
        smem=1,
    )

    ext_p, ext_r, noise_ext, sums = call(
        stat_kernel,
        [place, pre_p, up_p, dn_p, pre_r, up_r, dn_r, got_ap, got_bp, got_ar, got_br, noise_rows, columns],
        [
            arr((2 * CH, 10 * COLS), F32),
            arr((2 * CH, 6 * COLS), F32),
            arr((8, 8, COLS), F32),
            arr((space, 16, COLS), F32),
        ],
        10**6,
        smem=1,
    )
    sums = lax.all_to_all(sums, "space", 0, 0, tiled=True)
    part, hidden, stat = call(
        hidden_kernel,
        [place, ext_p, ext_r, sums, columns, lift],
        [arr((12, 8, COLS), F32), arr((2 * CH, PIX), BF16), thin],
        10**7,
        smem=1,
    )
    others = [lax.ppermute(part, "tensor", ring("tensor", k)) for k in (1, 2, 3)]
    gnorm, head, partial = call(
        back_kernel,
        [place, part, *others, noise_ext, ext_p, stat, columns, hidden, drop],
        [arr((2 * CH, 6 * COLS), F32), arr((32, COLS), F32), arr((space, 24, COLS), F32)],
        10**7,
        smem=1,
    )
    partial = lax.all_to_all(partial, "space", 0, 0, tiled=True)
    keep, send, both, logits = call(
        weight_kernel,
        [place, gnorm, ext_p, stat, partial, feats, head],
        [arr((4, 40, 768), F32), arr((4, 48, 768), BF16), arr((32, COLS), F32), arr((1, 1), F32)],
        conv_flops,
        smem=1,
        scratch=[pltpu.VMEM((C, 768), F32)],
    )
    got = lax.ppermute(send, "space", partner)
    own, s1, s2, s3 = call(
        core_kernel,
        [place, keep, both, got],
        [arr((48, 768), F32)] + [arr((48, 768), BF16)] * 3,
        10**6,
        smem=1,
    )
    back = [
        lax.ppermute(sent, "space", ring("space", 2 * k)) for k, sent in ((1, s1), (2, s2), (3, s3))
    ]
    (packed,) = call(
        cross_kernel,
        [own, *back],
        [arr((8, 56, COLS), BF16)],
        10**6,
        scratch=[pltpu.VMEM((8 * 56, COLS), F32)],
    )
    packed = lax.all_to_all(packed, "dp", 0, 0, tiled=True)
    grad_one, grad_two = call(
        sum_kernel, [packed], [arr((9, 5, CH), F32), arr((9, 4, CH), F32)], 10**6
    )
    return (logits.reshape(1), grad_one.transpose(0, 2, 1), grad_two)


def solution(mesh):
    in_specs = (
        P("dp", None, "tensor", "space", None),
        P("dp", None, "tensor", "space", None),
        P("dp", None, None, "space", None),
        P(None, "tensor", None),
        P(None, "tensor", None),
        P("tensor"),
        P("tensor"),
        P("tensor"),
        P("tensor"),
        P("tensor"),
        P("tensor"),
        P(None, None, "tensor"),
        P(None, None, "tensor"),
        P(None, "tensor"),
        P("dp"),
        P("dp"),
    )
    out_specs = (P("dp"), P(None, "tensor", ("dp", "space")), P(None, None, "tensor"))
    return jax.shard_map(body, mesh=mesh, in_specs=in_specs, out_specs=out_specs, check_vma=False)
```

```python
import functools

import jax
import jax.numpy as jnp
from jax import lax
from jax.experimental import pallas as pl
from jax.experimental.pallas import tpu as pltpu
from jax.sharding import PartitionSpec as P

C = 320
GROUPS = 32
BETA = 500.0
EPS = 1e-05
CH = 80
ROWS = 4
COLS = 128
PIX = ROWS * COLS
GSIZE = C // GROUPS
LOCAL_GROUPS = CH // GSIZE
COUNT = float(GSIZE * 32 * 128)
CELLS = float(4 * 32 * 128)
F32 = jnp.float32
BF16 = jnp.bfloat16
HIGHEST = lax.Precision.HIGHEST

VM = pl.BlockSpec(memory_space=pltpu.VMEM)
SM = pl.BlockSpec(memory_space=pltpu.SMEM)


def call(kernel, ins, outs, flops, smem=0, scratch=()):
    in_bytes = sum(a.size * a.dtype.itemsize for a in ins)
    out_bytes = sum(s.size * s.dtype.itemsize for s in outs)
    return pl.pallas_call(
        kernel,
        out_shape=outs,
        in_specs=[SM] * smem + [VM] * (len(ins) - smem),
        out_specs=[VM] * len(outs),
        scratch_shapes=list(scratch),
        cost_estimate=pl.CostEstimate(
            flops=flops, bytes_accessed=in_bytes + out_bytes, transcendentals=0
        ),
        compiler_params=pltpu.CompilerParams(vmem_limit_bytes=12 * 1024 * 1024),
    )(*ins)


def arr(shape, dtype):
    return jax.ShapeDtypeStruct(shape, dtype)


def dot(a, b):
    return lax.dot_general(a, b, (((1,), (0,)), ((), ())), preferred_element_type=F32)


def dot_nt(a, b):
    return lax.dot_general(a, b, (((1,), (1,)), ((), ())), preferred_element_type=F32)


def exact_dot(a, b):
    return lax.dot_general(
        a, b, (((1,), (0,)), ((), ())), preferred_element_type=F32, precision=HIGHEST
    )


def from_left(tile):
    lane = lax.broadcasted_iota(jnp.int32, tile.shape, tile.ndim - 1)
    return jnp.where(lane == 0, 0.0, pltpu.roll(tile, 1, tile.ndim - 1))


def from_right(tile):
    lane = lax.broadcasted_iota(jnp.int32, tile.shape, tile.ndim - 1)
    return jnp.where(lane == COLS - 1, 0.0, pltpu.roll(tile, COLS - 1, tile.ndim - 1))


def row_of(tile, r):
    return tile[:, r * COLS : (r + 1) * COLS]


def sigmoid(value):
    return 0.5 + 0.5 * jnp.tanh(0.5 * value)


def members():
    group = lax.broadcasted_iota(jnp.int32, (2 * LOCAL_GROUPS, 2 * CH), 0)
    chan = lax.broadcasted_iota(jnp.int32, (2 * LOCAL_GROUPS, 2 * CH), 1)
    low = group * GSIZE
    return jnp.where((chan >= low) & (chan < low + GSIZE), 1.0, 0.0).astype(F32)


def spread(stat):
    chan = lax.broadcasted_iota(jnp.int32, (2 * CH, 2 * LOCAL_GROUPS), 0)
    group = lax.broadcasted_iota(jnp.int32, (2 * CH, 2 * LOCAL_GROUPS), 1)
    low = group * GSIZE
    pick = jnp.where((chan >= low) & (chan < low + GSIZE), 1.0, 0.0).astype(F32)
    return exact_dot(pick, stat)


def in_lanes(columns):
    rows = columns[0].shape[0]
    lane = lax.broadcasted_iota(jnp.int32, (rows, COLS), 1)
    out = jnp.zeros((rows, COLS), F32)
    for index, column in enumerate(columns):
        out = jnp.where(lane == index, column, out)
    return out


def prep_kernel(
    place_ref, b_p, b_r, gain_p, off_p, gain_r, off_r, w2_p, w2_r, table_ref, noise_ref,
    col_ref, lift_ref, drop_ref, rows_ref
):
    lane = lax.broadcasted_iota(jnp.int32, table_ref.shape, 1)
    shift = jnp.sum(
        jnp.where(lane == place_ref[6], table_ref[...], 0.0), axis=1, keepdims=True
    )
    eye = lax.broadcasted_iota(jnp.int32, (CH, CH), 0) == lax.broadcasted_iota(
        jnp.int32, (CH, CH), 1
    )

    def upright(ref):
        return jnp.sum(jnp.where(eye, ref[...], 0.0), axis=1, keepdims=True)

    block = in_lanes(
        [
            upright(gain_p),
            upright(off_p),
            upright(gain_r),
            upright(off_r),
            upright(b_p) + shift,
            upright(b_r) + shift,
        ]
    )
    col_ref[0:CH, :] = block
    col_ref[CH : 2 * CH, :] = block
    one = jnp.where(eye, 1.0, 0.0).astype(BF16)
    zero = jnp.zeros((4, CH), F32)
    for m, ref in enumerate((w2_p, w2_r)):
        for im in range(2):
            pieces = []
            for tap in range(9):
                rows = ref[tap].astype(F32)
                pieces += [rows, zero] if im == 0 else [zero, rows]
            padded = jnp.concatenate(pieces, axis=0).astype(BF16)
            lift_ref[m, im] = padded
            if m == 0:
                drop_ref[im * CH : (im + 1) * CH, :] = dot_nt(one, padded).astype(BF16)
    for im in range(2):
        for o in range(4):
            slot = im * 4 + o
            for r in range(ROWS):
                rows_ref[r, slot : slot + 1, :] = noise_ref[im, o, r : r + 1, :]


def conv_kernel(last, t_ref, f0, f1, f2, f3, w_ref, *refs):
    if last:
        pre_ref, up_ref, dn_ref, send_a, send_b, fs_ref = refs
    else:
        noise_ref, pre_ref, up_ref, dn_ref, send_a, send_b, perm_ref, fs_ref = refs
    t = t_ref[5]
    for k in range(4):
        base = pl.multiple_of(lax.rem(t - k + 4, 4) * CH, 16)
        for im in range(2):
            for r in range(ROWS):
                lo = im * PIX + r * COLS
                fs_ref[pl.ds(base, CH), lo : lo + COLS] = (f0, f1, f2, f3)[k][im, r]
    odd = t_ref[3] > 0
    count = 2 if last else 4
    if not last:
        for index in range(2):
            first, second = [
                jnp.concatenate(
                    [noise_ref[im, o, r : r + 1, :] for im in range(2) for o in range(4)], axis=0
                )
                for r in (index, 2 + index)
            ]
            for ref, value in (
                (send_a, jnp.where(odd, first, second)),
                (send_b, jnp.where(odd, second, first)),
            ):
                high = value.astype(BF16).astype(F32)
                both = jnp.concatenate([high, value - high], axis=0).astype(BF16)
                ref[960 + 16 * index : 976 + 16 * index, :] = both
        row = lax.broadcasted_iota(jnp.int32, (C, C), 0)
        chan = lax.broadcasted_iota(jnp.int32, (C, C), 1)
        core, rest = row // 160, row % 160
        want = 40 * (rest % 8) + 10 * (rest // 40) + 5 * core + (rest % 40) // 8
        pick = jnp.where(chan == want, 1.0, 0.0).astype(BF16)
        perm_ref[...] = dot(pick, fs_ref[...]).astype(BF16)
    for im in range(2):
        feats = fs_ref[:, im * PIX : (im + 1) * PIX]
        taps = [dot(w_ref[ky * 3 * CH : (ky + 1) * 3 * CH, :], feats) for ky in range(3)]
        chans = slice(im * CH, (im + 1) * CH)
        outs = []
        for r in range(-1, ROWS + 1):
            total = None
            for ky in range(3):
                src = r + ky - 1
                if 0 <= src < ROWS:
                    term = row_of(taps[ky], src)
                    total = term if total is None else total + term
            out = (
                total[CH : 2 * CH]
                + from_left(total[0:CH])
                + from_right(total[2 * CH : 3 * CH])
            )
            if r == -1:
                up_ref[chans, :] = out
            elif r == ROWS:
                dn_ref[chans, :] = out
            else:
                pre_ref[chans, r * COLS : (r + 1) * COLS] = out
            outs.append(out)
        for index in range(count):
            upper, lower = outs[index], outs[ROWS + 2 - count + index]
            for ref, value in (
                (send_a, jnp.where(odd, upper, lower)),
                (send_b, jnp.where(odd, lower, upper)),
            ):
                high = value.astype(BF16)
                lo = index * 2 * CH + im * CH
                ref[lo : lo + CH, :] = high
                ref_low = (count + index) * 2 * CH + im * CH
                if count == 2:
                    ref[ref_low : ref_low + CH, :] = (value - high.astype(F32)).astype(BF16)
        if count == 4:
            for index in range(2):
                upper, lower = outs[index], outs[ROWS + index]
                for ref, value in (
                    (send_a, jnp.where(odd, upper, lower)),
                    (send_b, jnp.where(odd, lower, upper)),
                ):
                    rest = value - value.astype(BF16).astype(F32)
                    lo = (count + index) * 2 * CH + im * CH
                    ref[lo : lo + CH, :] = rest.astype(BF16)


def stat_kernel(
    place_ref, pre_p, up_p, dn_p, pre_r, up_r, dn_r, got_ap, got_bp, got_ar, got_br, noise_ref, col_ref,
    ext_p, ext_r, noise_ext, out_ref
):
    odd = place_ref[3] > 0
    top = place_ref[1] > 0
    bottom = place_ref[2] > 0

    def rows_at(side, lo, hi):
        return jnp.where(odd, side[0][lo:hi, :].astype(F32), side[1][lo:hi, :].astype(F32))

    def got(side, index):
        return rows_at(side, index * 2 * CH, (index + 1) * 2 * CH)

    def near(ref, index, low):
        return got(ref, index) + got(ref, low)

    columns = []
    first = 0
    for pre, up, dn, ext, got_a, got_b, halo, slot in (
        (pre_p, up_p, dn_p, ext_p, got_ap, got_bp, 3, 4),
        (pre_r, up_r, dn_r, ext_r, got_ar, got_br, 1, 5),
    ):
        left, right = (got_a, got_b), (got_b, got_a)
        low = first + halo + 1
        bias = jnp.broadcast_to(col_ref[:, slot : slot + 1], (2 * CH, COLS))
        rows = [pre[:, r * COLS : (r + 1) * COLS] for r in range(ROWS)]
        rows[0] = rows[0] + jnp.where(top, 0.0, near(left, first + halo, low + 1))
        rows[ROWS - 1] = rows[ROWS - 1] + jnp.where(bottom, 0.0, near(right, first, low))
        rows = [row + bias for row in rows]
        total = rows[0] + rows[1] + rows[2] + rows[3]
        square = (
            rows[0] * rows[0] + rows[1] * rows[1] + rows[2] * rows[2] + rows[3] * rows[3]
        )
        before = [got(left, first + index) for index in range(halo)]
        before[-1] = near(left, first + halo - 1, low) + up[...]
        after = [got(right, first + 1 + index) for index in range(halo)]
        after[0] = near(right, first + 1, low + 1) + dn[...]
        before = [row + bias for row in before]
        after = [row + bias for row in after]
        for index, row in enumerate(before + rows + after):
            ext[:, index * COLS : (index + 1) * COLS] = row
        columns.append(jnp.sum(total, axis=1, keepdims=True))
        columns.append(jnp.sum(square, axis=1, keepdims=True))
    for index in range(2):
        lo = 960 + 16 * index
        left, right = (got_ap, got_bp), (got_bp, got_ap)
        pair = rows_at(left, lo, lo + 16)
        noise_ext[index] = pair[0:8] + pair[8:16]
        pair = rows_at(right, lo, lo + 16)
        noise_ext[ROWS + 2 + index] = pair[0:8] + pair[8:16]
    for r in range(ROWS):
        noise_ext[2 + r] = noise_ref[r]
    sums = exact_dot(members(), in_lanes(columns))
    for peer in range(out_ref.shape[0]):
        out_ref[peer] = sums


def moments(total):
    wide = spread(total / COUNT)
    result = []
    for m in range(2):
        mean = wide[:, 2 * m : 2 * m + 1]
        square = wide[:, 2 * m + 1 : 2 * m + 2]
        result.append((mean, lax.rsqrt(square - mean * mean + EPS)))
    return result


def hidden_kernel(
    edge_ref, ext_p, ext_r, sums_ref, col_ref, lift_ref, part_ref, hid_ref, stat_ref
):
    stats = moments(jnp.sum(sums_ref[...], axis=0))
    stat_ref[...] = in_lanes([stats[0][0], stats[0][1]])
    for m, (ext, halo, start) in enumerate(((ext_p, 3, 0), (ext_r, 1, 8))):
        mean, inv = stats[m]
        gain = col_ref[:, 2 * m : 2 * m + 1]
        shift = col_ref[:, 2 * m + 1 : 2 * m + 2]
        pieces = []
        for index in range(ROWS + 2 * halo):
            value = ext[:, index * COLS : (index + 1) * COLS]
            normed = ((value - mean) * inv) * gain + shift
            hidden = normed * sigmoid(normed)
            if index < halo:
                hidden = jnp.where(edge_ref[1] > 0, 0.0, hidden)
            if index >= ROWS + halo:
                hidden = jnp.where(edge_ref[2] > 0, 0.0, hidden)
            hidden = hidden.astype(BF16)
            if m == 0 and halo <= index < halo + ROWS:
                hid_ref[:, (index - halo) * COLS : (index - halo + 1) * COLS] = hidden
            pieces.append(hidden)
        joined = jnp.concatenate(pieces, axis=1)
        taps = dot(lift_ref[m, 0], joined[0:CH]) + dot(lift_ref[m, 1], joined[CH : 2 * CH])
        for index in range(ROWS + 2 * halo - 2):
            totals = [None, None, None]
            for kx in range(3):
                for ky in range(3):
                    tap = 3 * ky + kx
                    lo = (index + ky) * COLS
                    term = taps[8 * tap : 8 * tap + 8, lo : lo + COLS]
                    totals[kx] = term if totals[kx] is None else totals[kx] + term
            part_ref[start + index] = (
                totals[1] + from_left(totals[0]) + from_right(totals[2])
            )


def back_kernel(
    edge_ref, p0, p1, p2, p3, noise_ext, ext_p, stat_ref, col_ref, hid_ref, drop_ref,
    gnorm_ref, head_ref, out_ref
):
    def pred(index):
        return (p0[index] + p1[index]) + (p2[index] + p3[index])

    residual = [pred(index) - noise_ext[index] for index in range(ROWS + 4)]
    frozen = [pred(8 + r) - noise_ext[2 + r] for r in range(ROWS)]
    errors = []
    for rows in (residual[2 : 2 + ROWS], frozen):
        square = rows[0] * rows[0]
        for row in rows[1:]:
            square = square + row * row
        errors.append(jnp.sum(square, axis=1, keepdims=True))
    image = lax.broadcasted_iota(jnp.int32, (8, COLS), 0)
    residual = [jnp.where(image < 4, row, -row) for row in residual]
    for index in range(2):
        residual[index] = jnp.where(edge_ref[1] > 0, 0.0, residual[index])
        residual[ROWS + 2 + index] = jnp.where(edge_ref[2] > 0, 0.0, residual[ROWS + 2 + index])
    moved = [
        [from_right(row) for row in residual],
        residual,
        [from_left(row) for row in residual],
    ]
    blocks = []
    for ky in range(3):
        for kx in range(3):
            blocks.append(
                jnp.concatenate([moved[kx][r + 2 - ky] for r in range(ROWS + 2)], axis=1)
            )
    cot = jnp.concatenate(blocks, axis=0).astype(BF16)
    dhidden = dot(drop_ref[...], cot)
    mean = stat_ref[:, 0:1]
    inv = stat_ref[:, 1:2]
    gain = col_ref[:, 0:1]
    shift = col_ref[:, 1:2]
    first = None
    second = None
    for index in range(ROWS + 2):
        lanes = slice(index * COLS, (index + 1) * COLS)
        centered = (ext_p[:, (index + 2) * COLS : (index + 3) * COLS] - mean) * inv
        normed = centered * gain + shift
        gate = sigmoid(normed)
        gnorm = dhidden[:, lanes] * gate * (1.0 + normed * (1.0 - gate)) * gain
        gnorm_ref[:, lanes] = gnorm
        if 1 <= index <= ROWS:
            first = gnorm if first is None else first + gnorm
            extra = gnorm * centered
            second = extra if second is None else second + extra
    first = jnp.sum(first, axis=1, keepdims=True)
    second = jnp.sum(second, axis=1, keepdims=True)
    sums = exact_dot(members(), in_lanes([first, second]))
    mine = cot[:, COLS : (ROWS + 1) * COLS]
    grads = [dot_nt(mine, hid_ref[im * CH : (im + 1) * CH, :]) for im in range(2)]
    error = in_lanes(errors)
    head_ref[...] = jnp.zeros(head_ref.shape, F32)
    for tap in range(9):
        head = grads[0][8 * tap : 8 * tap + 4] + grads[1][8 * tap + 4 : 8 * tap + 8]
        if tap < 6:
            head_ref[4 * tap : 4 * tap + 4, 0:CH] = head
        else:
            lo = 4 * tap - 24
            head_ref[lo : lo + 4, CH:COLS] = head[:, 0 : COLS - CH]
            head_ref[lo + 12 : lo + 16, CH : 3 * CH - COLS] = head[:, COLS - CH : CH]
    for peer in range(out_ref.shape[0]):
        out_ref[peer, 0:16, :] = sums
        out_ref[peer, 16:24, :] = error


def weight_kernel(
    place_ref, gnorm_ref, ext_p, stat_ref, red_ref, fs_ref, head_ref,
    keep_ref, send_ref, both_ref, logit_ref, grad_ref
):
    total = jnp.sum(red_ref[...], axis=0)
    row = lax.broadcasted_iota(jnp.int32, (8, COLS), 0)
    signed = jnp.where(row < 4, total[16:24], -total[16:24])
    gaps = jnp.sum(signed, axis=0, keepdims=True)
    gap = (gaps[:, 0:1] - gaps[:, 1:2]) * (1.0 / CELLS)
    sign = 1.0 - 2.0 * place_ref[0].astype(F32)
    logit = (-0.5 * BETA) * sign * gap
    logit_ref[...] = logit
    scale = (BETA / CELLS) * sign * jax.nn.sigmoid(-logit)
    wide = spread(total[0:16] / COUNT)
    mean = stat_ref[:, 0:1]
    inv = stat_ref[:, 1:2]
    parts = []
    for index in range(ROWS + 2):
        centered = (ext_p[:, (index + 2) * COLS : (index + 3) * COLS] - mean) * inv
        gnorm = gnorm_ref[:, index * COLS : (index + 1) * COLS]
        delta = inv * (gnorm - wide[:, 0:1] - centered * wide[:, 1:2])
        if index == 0:
            delta = jnp.where(place_ref[1] > 0, 0.0, delta)
        if index == ROWS + 1:
            delta = jnp.where(place_ref[2] > 0, 0.0, delta)
        parts.append(
            [from_right(delta).astype(BF16), delta.astype(BF16), from_left(delta).astype(BF16)]
        )
    blank = jnp.zeros((16, 2 * PIX), BF16)
    for ky in range(3):
        rows = []
        for kx in range(3):
            tiles = []
            for im in range(2):
                for r in range(ROWS):
                    tiles.append(parts[r + 2 - ky][kx][im * CH : (im + 1) * CH])
            rows.append(jnp.concatenate(tiles, axis=1))
        stack = jnp.concatenate(rows + [blank], axis=0)
        grad = dot_nt(fs_ref[...], stack) * scale
        grad_ref[:, 256 * ky : 256 * ky + 256] = grad
    core = place_ref[3]
    head = head_ref[...] * scale
    both_ref[...] = head
    for x in range(4):
        mine = pl.multiple_of(core * 160 + 40 * x, 8)
        his = pl.multiple_of((1 - core) * 160 + 40 * x, 8)
        keep_ref[x] = grad_ref[pl.ds(mine, 40), :]
        tail = [head[8 * j : 8 * j + 8] for j in range(3)] + [jnp.zeros((8, 3 * COLS), F32)]
        block = jnp.concatenate(
            [grad_ref[pl.ds(his, 40), :], jnp.concatenate(tail, axis=1)], axis=0
        )
        send_ref[x] = block.astype(BF16)


def core_kernel(x_ref, keep_ref, both_ref, got_ref, own_ref, s1, s2, s3):
    x = x_ref[4]
    tail = [both_ref[8 * j : 8 * j + 8, :] for j in range(3)] + [jnp.zeros((8, 3 * COLS), F32)]
    tail = jnp.concatenate(tail, axis=1)
    for k, ref in enumerate((own_ref, s1, s2, s3)):
        where = lax.rem(x + k, 4)
        got = got_ref[where].astype(F32)
        block = jnp.concatenate([keep_ref[where] + got[0:40], tail + got[40:48]], axis=0)
        ref[...] = block.astype(ref.dtype)


def cross_kernel(own_ref, r1, r2, r3, out_ref, pack_ref):
    total = (own_ref[...] + r1[...].astype(F32)) + (r2[...].astype(F32) + r3[...].astype(F32))
    for half in range(6):
        lanes = slice(half * COLS, (half + 1) * COLS)
        for ii in range(5):
            pack_ref[pl.ds(half * 5 + ii, 8, stride=56), :] = total[8 * ii : 8 * ii + 8, lanes]
    for spare in (30, 31):
        pack_ref[pl.ds(spare, 8, stride=56), :] = jnp.zeros((8, COLS), F32)
    for d in range(8):
        for j in range(3):
            pack_ref[56 * d + 32 + 8 * j : 56 * d + 40 + 8 * j, :] = total[
                40:48, j * COLS : (j + 1) * COLS
            ]
        out_ref[d] = pack_ref[56 * d : 56 * d + 56, :].astype(BF16)


def sum_kernel(got_ref, one_ref, two_ref):
    total = got_ref[0].astype(F32)
    for d in range(1, got_ref.shape[0]):
        total = total + got_ref[d].astype(F32)
    chunk = 5
    for tap in range(6):
        two_ref[tap] = total[32 + 4 * tap : 36 + 4 * tap, 0:CH]
    for tap in range(6, 9):
        lo = 8 + 4 * tap
        two_ref[tap] = jnp.concatenate(
            [total[lo : lo + 4, CH:COLS], total[lo + 12 : lo + 16, CH : 3 * CH - COLS]], axis=1
        )
    for ky in range(3):
        lo = 2 * ky * chunk
        wide = jnp.concatenate(
            [total[lo : lo + chunk], total[lo + chunk : lo + 2 * chunk]], axis=1
        )
        for kx in range(3):
            one_ref[3 * ky + kx] = wide[:, kx * CH : (kx + 1) * CH]


def ring(axis, step):
    count = lax.axis_size(axis)
    return [(i, (i + step) % count) for i in range(count)]


def body(
    feat_policy,
    feat_ref,
    noise,
    w1_policy,
    w1_ref,
    b1_policy,
    b1_ref,
    gn_gain_policy,
    gn_bias_policy,
    gn_gain_ref,
    gn_bias_ref,
    w2_policy,
    w2_ref,
    time_table,
    timestep,
    winner,
):
    space = lax.axis_size("space")
    s_index = lax.axis_index("space").astype(jnp.int32)
    is_top = (s_index == 0).astype(jnp.int32)
    is_bottom = (s_index == space - 1).astype(jnp.int32)
    place = jnp.stack(
        [
            winner[0].astype(jnp.int32),
            is_top,
            is_bottom,
            s_index & 1,
            s_index >> 1,
            lax.axis_index("tensor").astype(jnp.int32),
            timestep[0].astype(jnp.int32),
        ]
    )

    def gather(own):
        return [own] + [lax.ppermute(own, "tensor", ring("tensor", k)) for k in (3, 2, 1)][::-1]

    own_p = feat_policy[0].transpose(0, 2, 1, 3)
    feat_ref, own_p = lax.optimization_barrier((feat_ref, own_p))
    own_r = feat_ref[0].transpose(0, 2, 1, 3)
    parts_p = gather(own_p)
    parts_r = gather(own_r)

    conv_flops = 2 * 9 * C * CH * 2 * PIX
    wide = arr((2 * CH, PIX), F32)
    thin = arr((2 * CH, COLS), F32)

    partner = [(i, i ^ 1) for i in range(space)]
    across = [(i, (i + 1 if i % 2 else i - 1) % space) for i in range(space)]
    pre_p, up_p, dn_p, to_ap, to_bp, feats = call(
        functools.partial(conv_kernel, False),
        [place, *parts_p, w1_policy.reshape(9 * CH, C), noise[0]],
        [wide, thin, thin, arr((992, COLS), BF16), arr((992, COLS), BF16), arr((C, 2 * PIX), BF16)],
        conv_flops,
        smem=1,
        scratch=[pltpu.VMEM((C, 2 * PIX), BF16)],
    )
    got_bp = lax.ppermute(to_bp, "space", across)
    got_ap = lax.ppermute(to_ap, "space", partner)
    own_r, pre_p = lax.optimization_barrier((parts_r[0], pre_p))
    pre_r, up_r, dn_r, to_ar, to_br = call(
        functools.partial(conv_kernel, True),
        [place, own_r, *parts_r[1:], w1_ref.reshape(9 * CH, C)],
        [wide, thin, thin, arr((640, COLS), BF16), arr((640, COLS), BF16)],
        conv_flops,
        smem=1,
        scratch=[pltpu.VMEM((C, 2 * PIX), BF16)],
    )
    got_br = lax.ppermute(to_br, "space", across)
    got_ar = lax.ppermute(to_ar, "space", partner)

    pre_r, b1_policy = lax.optimization_barrier((pre_r, b1_policy))
    vectors = [b1_policy, b1_ref, gn_gain_policy, gn_bias_policy, gn_gain_ref, gn_bias_ref]
    columns, lift, drop, noise_rows = call(
        prep_kernel,
        [place, *[v[None, :] for v in vectors], w2_policy, w2_ref, time_table.T, noise[0]],
        [
            arr((2 * CH, COLS), F32),
            arr((2, 2, 72, CH), BF16),
            arr((2 * CH, 72), BF16),
            arr((ROWS, 8, COLS), F32),
        ],
        10**6,
        smem=1,
    )

    ext_p, ext_r, noise_ext, sums = call(
        stat_kernel,
        [place, pre_p, up_p, dn_p, pre_r, up_r, dn_r, got_ap, got_bp, got_ar, got_br, noise_rows, columns],
        [
            arr((2 * CH, 10 * COLS), F32),
            arr((2 * CH, 6 * COLS), F32),
            arr((8, 8, COLS), F32),
            arr((space, 16, COLS), F32),
        ],
        10**6,
        smem=1,
    )
    sums = lax.all_to_all(sums, "space", 0, 0, tiled=True)
    part, hidden, stat = call(
        hidden_kernel,
        [place, ext_p, ext_r, sums, columns, lift],
        [arr((12, 8, COLS), F32), arr((2 * CH, PIX), BF16), thin],
        10**7,
        smem=1,
    )
    others = [lax.ppermute(part, "tensor", ring("tensor", k)) for k in (1, 2, 3)]
    gnorm, head, partial = call(
        back_kernel,
        [place, part, *others, noise_ext, ext_p, stat, columns, hidden, drop],
        [arr((2 * CH, 6 * COLS), F32), arr((32, COLS), F32), arr((space, 24, COLS), F32)],
        10**7,
        smem=1,
    )
    partial = lax.all_to_all(partial, "space", 0, 0, tiled=True)
    keep, send, both, logits = call(
        weight_kernel,
        [place, gnorm, ext_p, stat, partial, feats, head],
        [arr((4, 40, 768), F32), arr((4, 48, 768), BF16), arr((32, COLS), F32), arr((1, 1), F32)],
        conv_flops,
        smem=1,
        scratch=[pltpu.VMEM((C, 768), F32)],
    )
    got = lax.ppermute(send, "space", partner)
    own, s1, s2, s3 = call(
        core_kernel,
        [place, keep, both, got],
        [arr((48, 768), F32)] + [arr((48, 768), BF16)] * 3,
        10**6,
        smem=1,
    )
    back = [
        lax.ppermute(sent, "space", ring("space", 2 * k)) for k, sent in ((1, s1), (2, s2), (3, s3))
    ]
    (packed,) = call(
        cross_kernel,
        [own, *back],
        [arr((8, 56, COLS), BF16)],
        10**6,
        scratch=[pltpu.VMEM((8 * 56, COLS), F32)],
    )
    packed = lax.all_to_all(packed, "dp", 0, 0, tiled=True)
    grad_one, grad_two = call(
        sum_kernel, [packed], [arr((9, 5, CH), F32), arr((9, 4, CH), F32)], 10**6
    )
    return (logits.reshape(1), grad_one.transpose(0, 2, 1), grad_two)


def solution(mesh):
    in_specs = (
        P("dp", None, "tensor", "space", None),
        P("dp", None, "tensor", "space", None),
        P("dp", None, None, "space", None),
        P(None, "tensor", None),
        P(None, "tensor", None),
        P("tensor"),
        P("tensor"),
        P("tensor"),
        P("tensor"),
        P("tensor"),
        P("tensor"),
        P(None, None, "tensor"),
        P(None, None, "tensor"),
        P(None, "tensor"),
        P("dp"),
        P("dp"),
    )
    out_specs = (P("dp"), P(None, "tensor", ("dp", "space")), P(None, None, "tensor"))
    return jax.shard_map(body, mesh=mesh, in_specs=in_specs, out_specs=out_specs, check_vma=False)
```

```python
import functools

import jax
import jax.numpy as jnp
from jax import lax
from jax.experimental import pallas as pl
from jax.experimental.pallas import tpu as pltpu
from jax.sharding import PartitionSpec as P


C = 320
GROUPS = 32
BETA = 500.0
EPS = 1e-05
CH = 80
ROWS = 4
COLS = 128
PIX = ROWS * COLS
GSIZE = C // GROUPS
LOCAL_GROUPS = CH // GSIZE
COUNT = float(GSIZE * 32 * 128)
CELLS = float(4 * 32 * 128)
F32 = jnp.float32
BF16 = jnp.bfloat16
HIGHEST = lax.Precision.HIGHEST

VM = pl.BlockSpec(memory_space=pltpu.VMEM)
SM = pl.BlockSpec(memory_space=pltpu.SMEM)


def call(kernel, ins, outs, flops, smem=0, scratch=()):
    in_bytes = sum(a.size * a.dtype.itemsize for a in ins)
    out_bytes = sum(s.size * s.dtype.itemsize for s in outs)
    return pl.pallas_call(
        kernel,
        out_shape=outs,
        in_specs=[SM] * smem + [VM] * (len(ins) - smem),
        out_specs=[VM] * len(outs),
        scratch_shapes=list(scratch),
        cost_estimate=pl.CostEstimate(
            flops=flops, bytes_accessed=in_bytes + out_bytes, transcendentals=0
        ),
        compiler_params=pltpu.CompilerParams(vmem_limit_bytes=12 * 1024 * 1024),
    )(*ins)


def arr(shape, dtype):
    return jax.ShapeDtypeStruct(shape, dtype)


def dot(a, b):
    return lax.dot_general(a, b, (((1,), (0,)), ((), ())), preferred_element_type=F32)


def dot_nt(a, b):
    return lax.dot_general(a, b, (((1,), (1,)), ((), ())), preferred_element_type=F32)


def exact_dot(a, b):
    return lax.dot_general(
        a, b, (((1,), (0,)), ((), ())), preferred_element_type=F32, precision=HIGHEST
    )


def from_left(tile):
    lane = lax.broadcasted_iota(jnp.int32, tile.shape, tile.ndim - 1)
    return jnp.where(lane == 0, 0.0, pltpu.roll(tile, 1, tile.ndim - 1))


def from_right(tile):
    lane = lax.broadcasted_iota(jnp.int32, tile.shape, tile.ndim - 1)
    return jnp.where(lane == COLS - 1, 0.0, pltpu.roll(tile, COLS - 1, tile.ndim - 1))


def row_of(tile, r):
    return tile[:, r * COLS : (r + 1) * COLS]


def sigmoid(value):
    return 0.5 + 0.5 * jnp.tanh(0.5 * value)


def members():
    group = lax.broadcasted_iota(jnp.int32, (2 * LOCAL_GROUPS, 2 * CH), 0)
    chan = lax.broadcasted_iota(jnp.int32, (2 * LOCAL_GROUPS, 2 * CH), 1)
    low = group * GSIZE
    return jnp.where((chan >= low) & (chan < low + GSIZE), 1.0, 0.0).astype(F32)


def spread(stat):
    chan = lax.broadcasted_iota(jnp.int32, (2 * CH, 2 * LOCAL_GROUPS), 0)
    group = lax.broadcasted_iota(jnp.int32, (2 * CH, 2 * LOCAL_GROUPS), 1)
    low = group * GSIZE
    pick = jnp.where((chan >= low) & (chan < low + GSIZE), 1.0, 0.0).astype(F32)
    return exact_dot(pick, stat)


def in_lanes(columns):
    rows = columns[0].shape[0]
    lane = lax.broadcasted_iota(jnp.int32, (rows, COLS), 1)
    out = jnp.zeros((rows, COLS), F32)
    for index, column in enumerate(columns):
        out = jnp.where(lane == index, column, out)
    return out


def prep_kernel(
    place_ref, b_p, b_r, gain_p, off_p, gain_r, off_r, w2_p, w2_r, table_ref, noise_ref,
    col_ref, lift_ref, drop_ref, rows_ref
):
    lane = lax.broadcasted_iota(jnp.int32, table_ref.shape, 1)
    shift = jnp.sum(
        jnp.where(lane == place_ref[6], table_ref[...], 0.0), axis=1, keepdims=True
    )
    eye = lax.broadcasted_iota(jnp.int32, (CH, CH), 0) == lax.broadcasted_iota(
        jnp.int32, (CH, CH), 1
    )

    def upright(ref):
        return jnp.sum(jnp.where(eye, ref[...], 0.0), axis=1, keepdims=True)

    block = in_lanes(
        [
            upright(gain_p),
            upright(off_p),
            upright(gain_r),
            upright(off_r),
            upright(b_p) + shift,
            upright(b_r) + shift,
        ]
    )
    col_ref[0:CH, :] = block
    col_ref[CH : 2 * CH, :] = block
    one = jnp.where(eye, 1.0, 0.0).astype(BF16)
    zero = jnp.zeros((4, CH), F32)
    for m, ref in enumerate((w2_p, w2_r)):
        for im in range(2):
            pieces = []
            for tap in range(9):
                rows = ref[tap].astype(F32)
                pieces += [rows, zero] if im == 0 else [zero, rows]
            padded = jnp.concatenate(pieces, axis=0).astype(BF16)
            lift_ref[m, im] = padded
            if m == 0:
                drop_ref[im * CH : (im + 1) * CH, :] = dot_nt(one, padded).astype(BF16)
    for im in range(2):
        for o in range(4):
            slot = im * 4 + o
            for r in range(ROWS):
                rows_ref[r, slot : slot + 1, :] = noise_ref[im, o, r : r + 1, :]


def conv_kernel(last, t_ref, f0, f1, f2, f3, w_ref, *refs):
    if last:
        pre_ref, up_ref, dn_ref, send_a, send_b, fs_ref = refs
    else:
        noise_ref, pre_ref, up_ref, dn_ref, send_a, send_b, perm_ref, fs_ref = refs
    t = t_ref[5]
    for k in range(4):
        base = pl.multiple_of(lax.rem(t - k + 4, 4) * CH, 16)
        for im in range(2):
            for r in range(ROWS):
                lo = im * PIX + r * COLS
                fs_ref[pl.ds(base, CH), lo : lo + COLS] = (f0, f1, f2, f3)[k][im, r]
    odd = t_ref[3] > 0
    count = 2 if last else 4
    if not last:
        for index in range(2):
            first, second = [
                jnp.concatenate(
                    [noise_ref[im, o, r : r + 1, :] for im in range(2) for o in range(4)], axis=0
                )
                for r in (index, 2 + index)
            ]
            for ref, value in (
                (send_a, jnp.where(odd, first, second)),
                (send_b, jnp.where(odd, second, first)),
            ):
                high = value.astype(BF16).astype(F32)
                both = jnp.concatenate([high, value - high], axis=0).astype(BF16)
                ref[960 + 16 * index : 976 + 16 * index, :] = both
        row = lax.broadcasted_iota(jnp.int32, (C, C), 0)
        chan = lax.broadcasted_iota(jnp.int32, (C, C), 1)
        core, rest = row // 160, row % 160
        want = 40 * (rest % 8) + 10 * (rest // 40) + 5 * core + (rest % 40) // 8
        pick = jnp.where(chan == want, 1.0, 0.0).astype(BF16)
        perm_ref[...] = dot(pick, fs_ref[...]).astype(BF16)
    for im in range(2):
        feats = fs_ref[:, im * PIX : (im + 1) * PIX]
        taps = [dot(w_ref[ky * 3 * CH : (ky + 1) * 3 * CH, :], feats) for ky in range(3)]
        chans = slice(im * CH, (im + 1) * CH)
        outs = []
        for r in range(-1, ROWS + 1):
            total = None
            for ky in range(3):
                src = r + ky - 1
                if 0 <= src < ROWS:
                    term = row_of(taps[ky], src)
                    total = term if total is None else total + term
            out = (
                total[CH : 2 * CH]
                + from_left(total[0:CH])
                + from_right(total[2 * CH : 3 * CH])
            )
            if r == -1:
                up_ref[chans, :] = out
            elif r == ROWS:
                dn_ref[chans, :] = out
            else:
                pre_ref[chans, r * COLS : (r + 1) * COLS] = out
            outs.append(out)
        for index in range(count):
            upper, lower = outs[index], outs[ROWS + 2 - count + index]
            for ref, value in (
                (send_a, jnp.where(odd, upper, lower)),
                (send_b, jnp.where(odd, lower, upper)),
            ):
                high = value.astype(BF16)
                lo = index * 2 * CH + im * CH
                ref[lo : lo + CH, :] = high
                ref_low = (count + index) * 2 * CH + im * CH
                if count == 2:
                    ref[ref_low : ref_low + CH, :] = (value - high.astype(F32)).astype(BF16)
        if count == 4:
            for index in range(2):
                upper, lower = outs[index], outs[ROWS + index]
                for ref, value in (
                    (send_a, jnp.where(odd, upper, lower)),
                    (send_b, jnp.where(odd, lower, upper)),
                ):
                    rest = value - value.astype(BF16).astype(F32)
                    lo = (count + index) * 2 * CH + im * CH
                    ref[lo : lo + CH, :] = rest.astype(BF16)


def stat_kernel(
    place_ref, pre_p, up_p, dn_p, pre_r, up_r, dn_r, got_ap, got_bp, got_ar, got_br, noise_ref, col_ref,
    ext_p, ext_r, noise_ext, out_ref
):
    odd = place_ref[3] > 0
    top = place_ref[1] > 0
    bottom = place_ref[2] > 0

    def rows_at(side, lo, hi):
        return jnp.where(odd, side[0][lo:hi, :].astype(F32), side[1][lo:hi, :].astype(F32))

    def got(side, index):
        return rows_at(side, index * 2 * CH, (index + 1) * 2 * CH)

    def near(ref, index, low):
        return got(ref, index) + got(ref, low)

    columns = []
    first = 0
    for pre, up, dn, ext, got_a, got_b, halo, slot in (
        (pre_p, up_p, dn_p, ext_p, got_ap, got_bp, 3, 4),
        (pre_r, up_r, dn_r, ext_r, got_ar, got_br, 1, 5),
    ):
        left, right = (got_a, got_b), (got_b, got_a)
        low = first + halo + 1
        bias = jnp.broadcast_to(col_ref[:, slot : slot + 1], (2 * CH, COLS))
        rows = [pre[:, r * COLS : (r + 1) * COLS] for r in range(ROWS)]
        rows[0] = rows[0] + jnp.where(top, 0.0, near(left, first + halo, low + 1))
        rows[ROWS - 1] = rows[ROWS - 1] + jnp.where(bottom, 0.0, near(right, first, low))
        rows = [row + bias for row in rows]
        total = rows[0] + rows[1] + rows[2] + rows[3]
        square = (
            rows[0] * rows[0] + rows[1] * rows[1] + rows[2] * rows[2] + rows[3] * rows[3]
        )
        before = [got(left, first + index) for index in range(halo)]
        before[-1] = near(left, first + halo - 1, low) + up[...]
        after = [got(right, first + 1 + index) for index in range(halo)]
        after[0] = near(right, first + 1, low + 1) + dn[...]
        before = [row + bias for row in before]
        after = [row + bias for row in after]
        for index, row in enumerate(before + rows + after):
            ext[:, index * COLS : (index + 1) * COLS] = row
        columns.append(jnp.sum(total, axis=1, keepdims=True))
        columns.append(jnp.sum(square, axis=1, keepdims=True))
    for index in range(2):
        lo = 960 + 16 * index
        left, right = (got_ap, got_bp), (got_bp, got_ap)
        pair = rows_at(left, lo, lo + 16)
        noise_ext[index] = pair[0:8] + pair[8:16]
        pair = rows_at(right, lo, lo + 16)
        noise_ext[ROWS + 2 + index] = pair[0:8] + pair[8:16]
    for r in range(ROWS):
        noise_ext[2 + r] = noise_ref[r]
    sums = exact_dot(members(), in_lanes(columns))
    for peer in range(out_ref.shape[0]):
        out_ref[peer] = sums


def moments(total):
    wide = spread(total / COUNT)
    result = []
    for m in range(2):
        mean = wide[:, 2 * m : 2 * m + 1]
        square = wide[:, 2 * m + 1 : 2 * m + 2]
        result.append((mean, lax.rsqrt(square - mean * mean + EPS)))
    return result


def hidden_kernel(
    edge_ref, ext_p, ext_r, sums_ref, col_ref, lift_ref, part_ref, hid_ref, stat_ref
):
    stats = moments(jnp.sum(sums_ref[...], axis=0))
    stat_ref[...] = in_lanes([stats[0][0], stats[0][1]])
    for m, (ext, halo, start) in enumerate(((ext_p, 3, 0), (ext_r, 1, 8))):
        mean, inv = stats[m]
        gain = col_ref[:, 2 * m : 2 * m + 1]
        shift = col_ref[:, 2 * m + 1 : 2 * m + 2]
        pieces = []
        for index in range(ROWS + 2 * halo):
            value = ext[:, index * COLS : (index + 1) * COLS]
            normed = ((value - mean) * inv) * gain + shift
            hidden = normed * sigmoid(normed)
            if index < halo:
                hidden = jnp.where(edge_ref[1] > 0, 0.0, hidden)
            if index >= ROWS + halo:
                hidden = jnp.where(edge_ref[2] > 0, 0.0, hidden)
            hidden = hidden.astype(BF16)
            if m == 0 and halo <= index < halo + ROWS:
                hid_ref[:, (index - halo) * COLS : (index - halo + 1) * COLS] = hidden
            pieces.append(hidden)
        joined = jnp.concatenate(pieces, axis=1)
        taps = dot(lift_ref[m, 0], joined[0:CH]) + dot(lift_ref[m, 1], joined[CH : 2 * CH])
        for index in range(ROWS + 2 * halo - 2):
            totals = [None, None, None]
            for kx in range(3):
                for ky in range(3):
                    tap = 3 * ky + kx
                    lo = (index + ky) * COLS
                    term = taps[8 * tap : 8 * tap + 8, lo : lo + COLS]
                    totals[kx] = term if totals[kx] is None else totals[kx] + term
            part_ref[start + index] = (
                totals[1] + from_left(totals[0]) + from_right(totals[2])
            )


def back_kernel(
    edge_ref, p0, p1, p2, p3, noise_ext, ext_p, stat_ref, col_ref, hid_ref, drop_ref,
    gnorm_ref, head_ref, out_ref
):
    def pred(index):
        return (p0[index] + p1[index]) + (p2[index] + p3[index])

    residual = [pred(index) - noise_ext[index] for index in range(ROWS + 4)]
    frozen = [pred(8 + r) - noise_ext[2 + r] for r in range(ROWS)]
    errors = []
    for rows in (residual[2 : 2 + ROWS], frozen):
        square = rows[0] * rows[0]
        for row in rows[1:]:
            square = square + row * row
        errors.append(jnp.sum(square, axis=1, keepdims=True))
    image = lax.broadcasted_iota(jnp.int32, (8, COLS), 0)
    residual = [jnp.where(image < 4, row, -row) for row in residual]
    for index in range(2):
        residual[index] = jnp.where(edge_ref[1] > 0, 0.0, residual[index])
        residual[ROWS + 2 + index] = jnp.where(edge_ref[2] > 0, 0.0, residual[ROWS + 2 + index])
    moved = [
        [from_right(row) for row in residual],
        residual,
        [from_left(row) for row in residual],
    ]
    blocks = []
    for ky in range(3):
        for kx in range(3):
            blocks.append(
                jnp.concatenate([moved[kx][r + 2 - ky] for r in range(ROWS + 2)], axis=1)
            )
    cot = jnp.concatenate(blocks, axis=0).astype(BF16)
    dhidden = dot(drop_ref[...], cot)
    mean = stat_ref[:, 0:1]
    inv = stat_ref[:, 1:2]
    gain = col_ref[:, 0:1]
    shift = col_ref[:, 1:2]
    first = None
    second = None
    for index in range(ROWS + 2):
        lanes = slice(index * COLS, (index + 1) * COLS)
        centered = (ext_p[:, (index + 2) * COLS : (index + 3) * COLS] - mean) * inv
        normed = centered * gain + shift
        gate = sigmoid(normed)
        gnorm = dhidden[:, lanes] * gate * (1.0 + normed * (1.0 - gate)) * gain
        gnorm_ref[:, lanes] = gnorm
        if 1 <= index <= ROWS:
            first = gnorm if first is None else first + gnorm
            extra = gnorm * centered
            second = extra if second is None else second + extra
    first = jnp.sum(first, axis=1, keepdims=True)
    second = jnp.sum(second, axis=1, keepdims=True)
    sums = exact_dot(members(), in_lanes([first, second]))
    mine = cot[:, COLS : (ROWS + 1) * COLS]
    grads = [dot_nt(mine, hid_ref[im * CH : (im + 1) * CH, :]) for im in range(2)]
    error = in_lanes(errors)
    head_ref[...] = jnp.zeros(head_ref.shape, F32)
    for tap in range(9):
        head = grads[0][8 * tap : 8 * tap + 4] + grads[1][8 * tap + 4 : 8 * tap + 8]
        if tap < 6:
            head_ref[4 * tap : 4 * tap + 4, 0:CH] = head
        else:
            lo = 4 * tap - 24
            head_ref[lo : lo + 4, CH:COLS] = head[:, 0 : COLS - CH]
            head_ref[lo + 12 : lo + 16, CH : 3 * CH - COLS] = head[:, COLS - CH : CH]
    for peer in range(out_ref.shape[0]):
        out_ref[peer, 0:16, :] = sums
        out_ref[peer, 16:24, :] = error


def weight_kernel(
    place_ref, gnorm_ref, ext_p, stat_ref, red_ref, fs_ref, head_ref,
    keep_ref, send_ref, both_ref, logit_ref, grad_ref
):
    total = jnp.sum(red_ref[...], axis=0)
    row = lax.broadcasted_iota(jnp.int32, (8, COLS), 0)
    signed = jnp.where(row < 4, total[16:24], -total[16:24])
    gaps = jnp.sum(signed, axis=0, keepdims=True)
    gap = (gaps[:, 0:1] - gaps[:, 1:2]) * (1.0 / CELLS)
    sign = 1.0 - 2.0 * place_ref[0].astype(F32)
    logit = (-0.5 * BETA) * sign * gap
    logit_ref[...] = logit
    scale = (BETA / CELLS) * sign * jax.nn.sigmoid(-logit)
    wide = spread(total[0:16] / COUNT)
    mean = stat_ref[:, 0:1]
    inv = stat_ref[:, 1:2]
    parts = []
    for index in range(ROWS + 2):
        centered = (ext_p[:, (index + 2) * COLS : (index + 3) * COLS] - mean) * inv
        gnorm = gnorm_ref[:, index * COLS : (index + 1) * COLS]
        delta = inv * (gnorm - wide[:, 0:1] - centered * wide[:, 1:2])
        if index == 0:
            delta = jnp.where(place_ref[1] > 0, 0.0, delta)
        if index == ROWS + 1:
            delta = jnp.where(place_ref[2] > 0, 0.0, delta)
        parts.append(
            [from_right(delta).astype(BF16), delta.astype(BF16), from_left(delta).astype(BF16)]
        )
    blank = jnp.zeros((16, 2 * PIX), BF16)
    for ky in range(3):
        rows = []
        for kx in range(3):
            tiles = []
            for im in range(2):
                for r in range(ROWS):
                    tiles.append(parts[r + 2 - ky][kx][im * CH : (im + 1) * CH])
            rows.append(jnp.concatenate(tiles, axis=1))
        stack = jnp.concatenate(rows + [blank], axis=0)
        grad = dot_nt(fs_ref[...], stack) * scale
        grad_ref[:, 256 * ky : 256 * ky + 256] = grad
    core = place_ref[3]
    head = head_ref[...] * scale
    both_ref[...] = head
    for x in range(4):
        mine = pl.multiple_of(core * 160 + 40 * x, 8)
        his = pl.multiple_of((1 - core) * 160 + 40 * x, 8)
        keep_ref[x] = grad_ref[pl.ds(mine, 40), :]
        tail = [head[8 * j : 8 * j + 8] for j in range(3)] + [jnp.zeros((8, 3 * COLS), F32)]
        block = jnp.concatenate(
            [grad_ref[pl.ds(his, 40), :], jnp.concatenate(tail, axis=1)], axis=0
        )
        send_ref[x] = block.astype(BF16)


def core_kernel(x_ref, keep_ref, both_ref, got_ref, own_ref, s1, s2, s3):
    x = x_ref[4]
    tail = [both_ref[8 * j : 8 * j + 8, :] for j in range(3)] + [jnp.zeros((8, 3 * COLS), F32)]
    tail = jnp.concatenate(tail, axis=1)
    for k, ref in enumerate((own_ref, s1, s2, s3)):
        where = lax.rem(x + k, 4)
        got = got_ref[where].astype(F32)
        block = jnp.concatenate([keep_ref[where] + got[0:40], tail + got[40:48]], axis=0)
        ref[...] = block.astype(ref.dtype)


def cross_kernel(own_ref, r1, r2, r3, out_ref, pack_ref):
    total = (own_ref[...] + r1[...].astype(F32)) + (r2[...].astype(F32) + r3[...].astype(F32))
    for half in range(6):
        lanes = slice(half * COLS, (half + 1) * COLS)
        for ii in range(5):
            pack_ref[pl.ds(half * 5 + ii, 8, stride=56), :] = total[8 * ii : 8 * ii + 8, lanes]
    for spare in (30, 31):
        pack_ref[pl.ds(spare, 8, stride=56), :] = jnp.zeros((8, COLS), F32)
    for d in range(8):
        for j in range(3):
            pack_ref[56 * d + 32 + 8 * j : 56 * d + 40 + 8 * j, :] = total[
                40:48, j * COLS : (j + 1) * COLS
            ]
        out_ref[d] = pack_ref[56 * d : 56 * d + 56, :].astype(BF16)


def sum_kernel(got_ref, one_ref, two_ref):
    total = got_ref[0].astype(F32)
    for d in range(1, got_ref.shape[0]):
        total = total + got_ref[d].astype(F32)
    chunk = 5
    for tap in range(6):
        two_ref[tap] = total[32 + 4 * tap : 36 + 4 * tap, 0:CH]
    for tap in range(6, 9):
        lo = 8 + 4 * tap
        two_ref[tap] = jnp.concatenate(
            [total[lo : lo + 4, CH:COLS], total[lo + 12 : lo + 16, CH : 3 * CH - COLS]], axis=1
        )
    for ky in range(3):
        lo = 2 * ky * chunk
        wide = jnp.concatenate(
            [total[lo : lo + chunk], total[lo + chunk : lo + 2 * chunk]], axis=1
        )
        for kx in range(3):
            one_ref[3 * ky + kx] = wide[:, kx * CH : (kx + 1) * CH]


def ring(axis, step):
    count = lax.axis_size(axis)
    return [(i, (i + step) % count) for i in range(count)]


def body(
    feat_policy,
    feat_ref,
    noise,
    w1_policy,
    w1_ref,
    b1_policy,
    b1_ref,
    gn_gain_policy,
    gn_bias_policy,
    gn_gain_ref,
    gn_bias_ref,
    w2_policy,
    w2_ref,
    time_table,
    timestep,
    winner,
):
    space = lax.axis_size("space")
    s_index = lax.axis_index("space").astype(jnp.int32)
    is_top = (s_index == 0).astype(jnp.int32)
    is_bottom = (s_index == space - 1).astype(jnp.int32)
    place = jnp.stack(
        [
            winner[0].astype(jnp.int32),
            is_top,
            is_bottom,
            s_index & 1,
            s_index >> 1,
            lax.axis_index("tensor").astype(jnp.int32),
            timestep[0].astype(jnp.int32),
        ]
    )

    def gather(own):
        parts = [own]
        for k in (1, 2, 3):
            parts.append(lax.ppermute(own, "tensor", ring("tensor", k)))
        return parts

    own_p = feat_policy[0].transpose(0, 2, 1, 3)
    feat_ref, own_p = lax.optimization_barrier((feat_ref, own_p))
    own_r = feat_ref[0].transpose(0, 2, 1, 3)
    parts_p = gather(own_p)
    parts_r = gather(own_r)

    conv_flops = 2 * 9 * C * CH * 2 * PIX
    wide = arr((2 * CH, PIX), F32)
    thin = arr((2 * CH, COLS), F32)

    partner = [(i, i ^ 1) for i in range(space)]
    across = [(i, (i + 1 if i % 2 else i - 1) % space) for i in range(space)]
    pre_p, up_p, dn_p, to_ap, to_bp, feats = call(
        functools.partial(conv_kernel, False),
        [place, *parts_p, w1_policy.reshape(9 * CH, C), noise[0]],
        [wide, thin, thin, arr((992, COLS), BF16), arr((992, COLS), BF16), arr((C, 2 * PIX), BF16)],
        conv_flops,
        smem=1,
        scratch=[pltpu.VMEM((C, 2 * PIX), BF16)],
    )
    got_bp = lax.ppermute(to_bp, "space", across)
    got_ap = lax.ppermute(to_ap, "space", partner)
    own_r, pre_p = lax.optimization_barrier((parts_r[0], pre_p))
    pre_r, up_r, dn_r, to_ar, to_br = call(
        functools.partial(conv_kernel, True),
        [place, own_r, *parts_r[1:], w1_ref.reshape(9 * CH, C)],
        [wide, thin, thin, arr((640, COLS), BF16), arr((640, COLS), BF16)],
        conv_flops,
        smem=1,
        scratch=[pltpu.VMEM((C, 2 * PIX), BF16)],
    )
    got_br = lax.ppermute(to_br, "space", across)
    got_ar = lax.ppermute(to_ar, "space", partner)

    pre_r, b1_policy = lax.optimization_barrier((pre_r, b1_policy))
    vectors = [b1_policy, b1_ref, gn_gain_policy, gn_bias_policy, gn_gain_ref, gn_bias_ref]
    columns, lift, drop, noise_rows = call(
        prep_kernel,
        [place, *[v[None, :] for v in vectors], w2_policy, w2_ref, time_table.T, noise[0]],
        [
            arr((2 * CH, COLS), F32),
            arr((2, 2, 72, CH), BF16),
            arr((2 * CH, 72), BF16),
            arr((ROWS, 8, COLS), F32),
        ],
        10**6,
        smem=1,
    )

    ext_p, ext_r, noise_ext, sums = call(
        stat_kernel,
        [place, pre_p, up_p, dn_p, pre_r, up_r, dn_r, got_ap, got_bp, got_ar, got_br, noise_rows, columns],
        [
            arr((2 * CH, 10 * COLS), F32),
            arr((2 * CH, 6 * COLS), F32),
            arr((8, 8, COLS), F32),
            arr((space, 16, COLS), F32),
        ],
        10**6,
        smem=1,
    )
    sums = lax.all_to_all(sums, "space", 0, 0, tiled=True)
    part, hidden, stat = call(
        hidden_kernel,
        [place, ext_p, ext_r, sums, columns, lift],
        [arr((12, 8, COLS), F32), arr((2 * CH, PIX), BF16), thin],
        10**7,
        smem=1,
    )
    others = [lax.ppermute(part, "tensor", ring("tensor", k)) for k in (1, 2, 3)]
    gnorm, head, partial = call(
        back_kernel,
        [place, part, *others, noise_ext, ext_p, stat, columns, hidden, drop],
        [arr((2 * CH, 6 * COLS), F32), arr((32, COLS), F32), arr((space, 24, COLS), F32)],
        10**7,
        smem=1,
    )
    partial = lax.all_to_all(partial, "space", 0, 0, tiled=True)
    keep, send, both, logits = call(
        weight_kernel,
        [place, gnorm, ext_p, stat, partial, feats, head],
        [arr((4, 40, 768), F32), arr((4, 48, 768), BF16), arr((32, COLS), F32), arr((1, 1), F32)],
        conv_flops,
        smem=1,
        scratch=[pltpu.VMEM((C, 768), F32)],
    )
    got = lax.ppermute(send, "space", partner)
    own, s1, s2, s3 = call(
        core_kernel,
        [place, keep, both, got],
        [arr((48, 768), F32)] + [arr((48, 768), BF16)] * 3,
        10**6,
        smem=1,
    )
    back = [
        lax.ppermute(sent, "space", ring("space", 2 * k)) for k, sent in ((1, s1), (2, s2), (3, s3))
    ]
    (packed,) = call(
        cross_kernel,
        [own, *back],
        [arr((8, 56, COLS), BF16)],
        10**6,
        scratch=[pltpu.VMEM((8 * 56, COLS), F32)],
    )
    packed = lax.all_to_all(packed, "dp", 0, 0, tiled=True)
    grad_one, grad_two = call(
        sum_kernel, [packed], [arr((9, 5, CH), F32), arr((9, 4, CH), F32)], 10**6
    )
    return (logits.reshape(1), grad_one.transpose(0, 2, 1), grad_two)


def solution(mesh):
    in_specs = (
        P("dp", None, "tensor", "space", None),
        P("dp", None, "tensor", "space", None),
        P("dp", None, None, "space", None),
        P(None, "tensor", None),
        P(None, "tensor", None),
        P("tensor"),
        P("tensor"),
        P("tensor"),
        P("tensor"),
        P("tensor"),
        P("tensor"),
        P(None, None, "tensor"),
        P(None, None, "tensor"),
        P(None, "tensor"),
        P("dp"),
        P("dp"),
    )
    out_specs = (P("dp"), P(None, "tensor", ("dp", "space")), P(None, None, "tensor"))
    return jax.shard_map(body, mesh=mesh, in_specs=in_specs, out_specs=out_specs, check_vma=False)
```
